256 devices in a mesh: ax: 8 (over x, y_lo), az: 32 (over z, y_hi, core).
Axes of the slice: x: 4, y: 4 (y_hi: 2, y_lo: 2; y = y_hi * 2 + y_lo), z: 8, core: 2. Of those that a mesh axis runs over, the one named last changes fastest.
Arguments:
- flow_state: float32 [5, 32, 1024, 256], P(None, 'ax', 'az'), may hold values from -6 to 6
- radial_coef: float32 [32, 1024, 256], P('ax', 'az'), may hold values from 50 to 2000
- blanking: int32 [32, 1024, 256], P('ax', 'az'), may hold values from 0 to 1, as said below
- canard_index: int32 [32, 1024], P('ax', 'az'), may hold values from 0 to 127
- canard_table: float32 [8, 128, 5, 256], P('ax', 'az'), may hold values from -6 to 6
- coupling: float32 [5, 5], replicated, may hold values from -0.15 to 0.15
- upwind_split: float32 [5], replicated, may hold values from 0.05 to 0.95
Outputs:
- update: float32 [5, 32, 1024, 256], P(None, 'ax', 'az')
The draws below stay inside these ranges and needn't reach their ends.
Inputs may be any that keep to these rules, and one draw needn't show every extreme that they name: `blanking`: 0 marks a blanked cell.
All inputs are finite; a program needn't handle non-finite values.
Results may differ from the reference program's by a relative error of at most 0.0001.
Values sent between devices are 32-bit elements; how exact they have to be, the bound alone decides.
No kernel may reach another device: no remote copies, remote signals or barrier semaphores. Data moves between devices by JAX's collectives and lax.ppermute only.
A program may use at most 128 MiB of HBM per device.

```python
import math
import jax
import jax.numpy as jnp
from jax import lax

NV = 5
NR = 256
CZ = 4
NT = 1024
NZ = 32
SROWS = 128
N_AX = 8


def draw_blanking(key, part):
    box_count = 8
    streams = jax.random.split(jax.random.fold_in(key, 7331), 6)
    z_start = jax.random.randint(streams[0], (box_count,), 0, NZ)
    z_length = jax.random.randint(streams[1], (box_count,), 1, NZ + 1)
    t_start = jax.random.randint(streams[2], (box_count,), 0, NT)
    t_length = jax.random.randint(streams[3], (box_count,), 1, max(NT // 8, 1) + 1)
    r_length = jax.random.randint(streams[4], (box_count,), max(NR // 8, 1), NR // 2 + 1)
    r_middle = jax.random.randint(streams[5], (box_count,), NR // 4, NR // 2 + 1)
    at_axis = jnp.arange(box_count, dtype=jnp.int32) % 2 == 0
    r_start = jnp.where(at_axis, 0, r_middle)
    plane_pos = jnp.arange(NZ, dtype=jnp.int32)
    column_pos = jnp.arange(NT, dtype=jnp.int32)
    radial_pos = jnp.arange(NR, dtype=jnp.int32)
    blanked = jnp.zeros((NZ, NT, NR), dtype=bool)
    for which in range(box_count):
        along_z = (plane_pos >= z_start[which]) & (plane_pos < z_start[which] + z_length[which])
        along_t = (column_pos - t_start[which]) % NT < t_length[which]
        along_r = (radial_pos >= r_start[which]) & (radial_pos < r_start[which] + r_length[which])
        blanked = blanked | along_z[:, None, None] & along_t[None, :, None] & along_r[None, None, :]
    return jnp.where(blanked, 0, 1).astype(jnp.int32)


def set_ends(result, stream_key, least, high):
    extent = result.shape
    place = [jax.random.randint(jax.random.fold_in(stream_key, axis), (), 0, extent[axis]) for axis in range(len(extent))]
    result = result.at[tuple(place)].set(least)
    longest = extent.index(max(extent))
    place[longest] = (place[longest] + 1) % extent[longest]
    return result.at[tuple(place)].set(high)


def shard_levels(rng, dims, shards, smallest, high):
    loudness = 1.0
    for position, parts in shards:
        heights = jax.random.uniform(jax.random.fold_in(jax.random.fold_in(rng, 6), position), (parts,), jnp.float32, smallest / len(shards), high / len(shards))
        loudness = loudness * jnp.repeat(jnp.exp(heights), dims[position] // parts).reshape((-1,) + (1,) * (len(dims) - 1 - position))
    return loudness


def gaussian(stream_key, shape, deviation, bound, cuts=(), held_as=jnp.bfloat16):
    gain = shard_levels(stream_key, shape, cuts, -0.22, 0.18) if cuts else 1.0
    values = jax.random.normal(stream_key, shape, jnp.float32) * deviation * gain
    return jnp.minimum(jnp.maximum(values, -bound), bound).astype(held_as)


def setup_inputs(seed: int = 0) -> dict:
    arg_keys = jax.random.split(jax.random.key(seed), 8)
    flow_state = gaussian(arg_keys[0], (NV, NZ, NT, NR), 1.0, 6.0, ((1, 8), (2, 32)), jnp.float32)
    radial_coef = jnp.clip(jnp.exp(math.log(2000.0) - 3.6888795 * jax.random.uniform(arg_keys[1], (NZ, NT, NR), jnp.float32) ** shard_levels(arg_keys[1], (NZ, NT, NR), ((0, 8), (1, 32)), -0.2, 0.2)), 50.0, 2000.0)
    blanking = draw_blanking(jax.random.fold_in(arg_keys[7], 71), 0)
    canard_index = set_ends(jax.random.randint(arg_keys[3], (NZ, NT), 0, SROWS), jax.random.fold_in(arg_keys[3], 1), 0, SROWS - 1).astype(jnp.int32)
    canard_table = gaussian(arg_keys[4], (N_AX, SROWS, NV, NR), 1.0, 6.0, ((0, 8), (1, 32)), jnp.float32)
    coupling = jnp.clip(jax.random.uniform(arg_keys[5], (NV, NV), jnp.float32, -0.15, 0.15), -0.15, 0.15)
    upwind_split = jnp.clip(jax.random.uniform(arg_keys[6], (NV,), jnp.float32, 0.05, 0.95), 0.05, 0.95)
    return dict(flow_state=flow_state, radial_coef=radial_coef, blanking=blanking, canard_index=canard_index, canard_table=canard_table, coupling=coupling, upwind_split=upwind_split)


def mat_mul(left, right):
    return jnp.sum(left[:, :, None] * right[None], axis=1)


def mat_vec(left, vector):
    return jnp.sum(left * vector[None], axis=1)


def invert(matrix):
    size = matrix.shape[0]
    eye = jnp.eye(size, dtype=matrix.dtype)
    working = matrix
    inverse = jnp.broadcast_to(eye.reshape(size, size, *([1] * (matrix.ndim - 2))), matrix.shape)
    for pivot_idx in range(size):
        pivot_val = working[pivot_idx, pivot_idx]
        row_work = working[pivot_idx] / pivot_val[None]
        row_inv = inverse[pivot_idx] / pivot_val[None]
        column = working[:, pivot_idx]
        working = working - column[:, None] * row_work[None]
        inverse = inverse - column[:, None] * row_inv[None]
        working = working.at[pivot_idx].set(row_work)
        inverse = inverse.at[pivot_idx].set(row_inv)
    return inverse


def face_coefs(lam_lines, mask_lines):
    inner_faces = 0.5 * (lam_lines[:-1] * mask_lines[1:] + lam_lines[1:] * mask_lines[:-1])
    border = jnp.zeros_like(lam_lines[:1])
    return jnp.concatenate([border, inner_faces], 0), jnp.concatenate([inner_faces, border], 0)


def build_blocks(lam_lines, mask_lines, coupling, upwind_split):
    outward, inward = face_coefs(lam_lines, mask_lines)
    comps = coupling.shape[0]
    eye = jnp.eye(comps, dtype=jnp.float32)
    toward_out = jnp.diag(upwind_split) + coupling
    toward_in = jnp.diag(1.0 - upwind_split) - coupling.T
    base = 1.0 + 0.5 * (outward + inward)
    lower = -outward[None, None] * toward_out[:, :, None, None]
    upper = -inward[None, None] * toward_in[:, :, None, None]
    diagonal = base[None, None] * eye[:, :, None, None]
    return lower, diagonal, upper


def take_even(array):
    return array[..., 0::2, :]


def take_odd(array):
    return array[..., 1::2, :]


def shifted_up(array):
    return jnp.concatenate([array[..., 1:, :], jnp.zeros_like(array[..., :1, :])], axis=-2)


def reduce_half(lower, diagonal, upper, rhs):
    saved = []
    while rhs.shape[-2] > 1:
        low_even, low_odd = take_even(lower), take_odd(lower)
        diag_even, diag_odd = take_even(diagonal), take_odd(diagonal)
        up_even, up_odd = take_even(upper), take_odd(upper)
        rhs_even, rhs_odd = take_even(rhs), take_odd(rhs)
        inv_even = invert(diag_even)
        gain_low = mat_mul(inv_even, low_even)
        gain_up = mat_mul(inv_even, up_even)
        gain_rhs = mat_vec(inv_even, rhs_even)
        lower = -mat_mul(low_odd, gain_low)
        diagonal = diag_odd - mat_mul(low_odd, gain_up) - mat_mul(up_odd, shifted_up(gain_low))
        upper = -mat_mul(up_odd, shifted_up(gain_up))
        rhs = rhs_odd - mat_vec(low_odd, gain_rhs) - mat_vec(up_odd, shifted_up(gain_rhs))
        saved.append((gain_low, gain_up, gain_rhs))
    return diagonal, rhs, saved


def back_sub(solution, saved):
    for gain_low, gain_up, gain_rhs in reversed(saved):
        previous = jnp.concatenate([jnp.zeros_like(solution[..., :1, :]), solution[..., :-1, :]], axis=-2)
        evens = gain_rhs - mat_vec(gain_low, previous) - mat_vec(gain_up, solution)
        comps, rows, width = solution.shape
        solution = jnp.stack([evens, solution], axis=2).reshape(comps, 2 * rows, width)
    return solution


def join_axis(diag_own, rhs_own, diag_other, rhs_other, lam_axis):
    comps = diag_own.shape[0]
    eye = jnp.eye(comps, dtype=jnp.float32)[:, :, None, None]
    across = 0.5 * lam_axis[None, :]
    own_total = diag_own + across * eye
    other_total = diag_other + across * eye
    inv_other = invert(other_total)
    schur = own_total - across * (inv_other * across)
    carried = mat_vec(inv_other, rhs_other)
    folded = rhs_own + across * carried
    return mat_vec(invert(schur), folded)


def stencil(field):
    padded = jnp.pad(field, ((0, 0), (1, 1), (0, 0), (0, 0)))
    behind = padded[:, :-2]
    ahead = padded[:, 2:]
    before_t = jnp.roll(field, 1, axis=2)
    after_t = jnp.roll(field, -1, axis=2)
    return behind + ahead + before_t + after_t - 4.0 * field + 0.5 * (behind - ahead)


def reference(flow_state, radial_coef, blanking, canard_index, canard_table, coupling, upwind_split):
    mask_field = blanking.astype(jnp.float32)
    lam_masked = radial_coef * mask_field
    groups = jnp.arange(NZ, dtype=jnp.int32) // CZ
    table_rows = canard_table[groups[:, None], canard_index]
    forcing = jnp.transpose(table_rows, (2, 0, 1, 3))

    def one_plane(plane_data):
        rhs_plane, lam_plane, mask_plane = plane_data
        rhs_lines = jnp.flip(rhs_plane, -1).transpose(0, 2, 1)
        lam_lines = jnp.flip(lam_plane, -1).T
        mask_lines = jnp.flip(mask_plane, -1).T
        lower, diagonal, upper = build_blocks(lam_lines, mask_lines, coupling, upwind_split)
        diag_red, rhs_red, saved = reduce_half(lower, diagonal, upper, rhs_lines)
        half_turn = lam_lines.shape[-1] // 2
        other_diag = jnp.roll(diag_red, half_turn, axis=-1)
        other_rhs = jnp.roll(rhs_red, half_turn, axis=-1)
        other_lam = jnp.roll(lam_lines[-1], half_turn, axis=-1)
        other_mask = jnp.roll(mask_lines[-1], half_turn, axis=-1)
        lam_axis = 0.5 * (lam_lines[-1] * other_mask + other_lam * mask_lines[-1])
        innermost = join_axis(diag_red, rhs_red, other_diag, other_rhs, lam_axis)
        solution = back_sub(innermost, saved)
        return jnp.flip(solution.transpose(0, 2, 1), -1)

    def solve_all(rhs):
        planes_out = lax.map(one_plane, (jnp.transpose(rhs, (1, 0, 2, 3)), lam_masked, mask_field))
        return jnp.transpose(planes_out, (1, 0, 2, 3))

    first_delta = solve_all(mask_field[None] * (stencil(flow_state) + forcing))
    second_delta = solve_all(mask_field[None] * (stencil(flow_state + first_delta) + forcing))
    return 0.5 * (first_delta + second_delta)
```

```python
import jax
import jax.numpy as jnp
from jax import lax
from jax.experimental import pallas as pl
from jax.experimental.pallas import tpu as pltpu
from jax.sharding import PartitionSpec as P

N = 5
NN = 25
SEG = 8
LANES = 128
HALF = 16
VMEM_LIMIT = 20 * 1024 * 1024
F32 = jnp.float32
STEPS = [(s * (2 * i + 1), s) for s in (1, 2, 4, 8) for i in range(8 // s)]


def up(x, s):
    return pltpu.roll(x, SEG - s, 0)


def down(x, s):
    return pltpu.roll(x, s, 0)


def splat_consts(coupling_ref, upwind_ref):
    shape = (SEG, LANES)
    p = [[jnp.full(shape, coupling_ref[i, j], F32) for j in range(N)] for i in range(N)]
    w = [jnp.full(shape, upwind_ref[0, i], F32) for i in range(N)]
    a = [[p[i][j] + w[i] if i == j else p[i][j] for j in range(N)] for i in range(N)]
    b = [[(1.0 - w[i]) - p[j][i] if i == j else -p[j][i] for j in range(N)] for i in range(N)]
    return a, b


def dot_row(row, cols, j):
    acc = row[0] * cols[0][j]
    for k in range(1, N):
        acc = acc + row[k] * cols[k][j]
    return acc


def mat_mul(x, y):
    return [[dot_row(x[i], y, j) for j in range(N)] for i in range(N)]


def mat_vec(x, v):
    out = []
    for i in range(N):
        acc = x[i][0] * v[0]
        for k in range(1, N):
            acc = acc + x[i][k] * v[k]
        out.append(acc)
    return out


def invert(matrix):
    m = [list(row) for row in matrix]
    for p in range(N):
        piv = 1.0 / m[p][p]
        m[p] = [piv if j == p else m[p][j] * piv for j in range(N)]
        for i in range(N):
            if i != p:
                f = m[i][p]
                m[i] = [-(f * piv) if j == p else m[i][j] - f * m[p][j] for j in range(N)]
    return m


def load_mat(ref, slot, base):
    return [[ref[slot, base + i * N + j] for j in range(N)] for i in range(N)]


def load_row(ref, slot, base, i):
    return [ref[slot, base + i * N + j] for j in range(N)]


def store_mat(ref, slot, base, mat):
    for i in range(N):
        for j in range(N):
            ref[slot, base + i * N + j] = mat[i][j]


def strided(ref, k):
    return ref[pl.ds(k, SEG, stride=2 * HALF), :]


def slot_of(p):
    return p + 2


D0, OUT0, IN0 = 0, NN, 2 * NN
LO0, LI0 = 0, NN


def factor_kernel(coef_ref, blank_ref, coup_ref, upw_ref, mb, mf, scal, sd, lam_t, mask_t, face, pw):
    mask = blank_ref[...].astype(F32).reshape(LANES, 2 * HALF * SEG)
    lam = coef_ref[...].reshape(LANES, 2 * HALF * SEG) * mask
    lam_t[...] = lam.T
    mask_t[...] = mask.T
    a, b = splat_consts(coup_ref, upw_ref)
    for which, mat in enumerate((mat_mul(a, a), mat_mul(b, b), mat_mul(a, b), mat_mul(b, a))):
        store_mat(pw, which, 0, mat)

    sub = lax.broadcasted_iota(jnp.int32, (SEG, LANES), 0)
    first_lam, first_mask = strided(lam_t, 0), strided(mask_t, 0)
    lam_k, mask_k = first_lam, first_mask
    for k in range(2 * HALF):
        if k < 2 * HALF - 1:
            lam_n, mask_n = strided(lam_t, k + 1), strided(mask_t, k + 1)
            f = 0.5 * (lam_k * mask_n + lam_n * mask_k)
        else:
            lam_n, mask_n = up(first_lam, 1), up(first_mask, 1)
            f = jnp.where(sub == SEG - 1, 0.0, 0.5 * (lam_k * mask_n + lam_n * mask_k))
        face[k + 1] = f
        lam_k, mask_k = lam_n, mask_n
    face[0] = down(face[2 * HALF], 1)

    def build_odd(m, c):
        fl, fr = face[2 * m + 1], face[2 * m + 2]
        scal[m, 0] = 1.0 / (1.0 + 0.5 * (fl + fr))
        scal[m, 1] = fl
        scal[m, 2] = fr
        return c

    lax.fori_loop(0, HALF, build_odd, 0)

    def build_even(p, c):
        prev = jnp.where(p == 0, HALF - 1, p - 1)
        inv, fl, fr = scal[p, 0], scal[p, 1], scal[p, 2]
        inv_p, fl_p, fr_p = scal[prev, 0], scal[prev, 1], scal[prev, 2]
        beta = fr_p * fr_p * inv_p
        delta = fr_p * fl_p * inv_p
        beta = jnp.where(p == 0, down(beta, 1), beta)
        alpha = fl * fl * inv
        gamma = fl * fr * inv
        d = 1.0 + 0.5 * (face[2 * p] + face[2 * p + 1])
        for i in range(N):
            for j in range(N):
                e = i * N + j
                val = -(alpha * pw[2, e] + beta * pw[3, e])
                mb[slot_of(p), D0 + e] = d + val if i == j else val
                mb[slot_of(p), OUT0 + e] = gamma * pw[0, e]
                mb[slot_of(p), IN0 + e] = delta * pw[1, e]
        return c

    lax.fori_loop(0, HALF, build_even, 0)
    last = scal[HALF - 1, 1] * scal[HALF - 1, 2] * scal[HALF - 1, 0]
    for e in range(NN):
        mb[slot_of(HALF), D0 + e] = jnp.zeros((SEG, LANES), F32)
        mb[slot_of(HALF), OUT0 + e] = jnp.zeros((SEG, LANES), F32)
        mb[slot_of(HALF), IN0 + e] = last * pw[1, e]

    def eliminate(it, c):
        s = jnp.where(it < 8, 1, jnp.where(it < 12, 2, jnp.where(it < 14, 4, 8)))
        first = jnp.where(it < 8, 0, jnp.where(it < 12, 8, jnp.where(it < 14, 12, 14)))
        m = s * (2 * (it - first) + 1)
        sm, sp, sq = slot_of(m), slot_of(m - s), slot_of(m + s)
        di = invert(load_mat(mb, sm, D0))
        store_mat(mb, sm, D0, di)
        for i in range(N):
            row = load_row(mb, sp, OUT0, i)
            for j in range(N):
                mf[sm, LO0 + i * N + j] = dot_row(row, di, j)
            row = load_row(mb, sq, IN0, i)
            for j in range(N):
                mf[sm, LI0 + i * N + j] = dot_row(row, di, j)
        in_m = load_mat(mb, sm, IN0)
        for i in range(N):
            row = load_row(mf, sm, LO0, i)
            for j in range(N):
                e = i * N + j
                mb[sp, D0 + e] = mb[sp, D0 + e] - dot_row(row, in_m, j)
            row = load_row(mf, sm, LI0, i)
            for j in range(N):
                mb[sq, IN0 + i * N + j] = dot_row(row, in_m, j)
        out_m = load_mat(mb, sm, OUT0)
        for i in range(N):
            row = load_row(mf, sm, LI0, i)
            for j in range(N):
                e = i * N + j
                mb[sq, D0 + e] = mb[sq, D0 + e] - dot_row(row, out_m, j)
            row = load_row(mf, sm, LO0, i)
            for j in range(N):
                mb[sp, OUT0 + i * N + j] = dot_row(row, out_m, j)
        return c

    lax.fori_loop(0, len(STEPS), eliminate, 0)

    s0, s16 = slot_of(0), slot_of(HALF)
    for e in range(NN):
        mb[0, D0 + e] = mb[s0, D0 + e] + down(mb[s16, D0 + e], 1)
        mb[0, OUT0 + e] = mb[s0, OUT0 + e]
        mb[0, IN0 + e] = down(mb[s16, IN0 + e], 1)
    for level, s in enumerate((1, 2, 4)):
        d = load_mat(mb, level, D0)
        di = invert(d)
        store_mat(mb, level, D0, di)
        di_up = [[up(di[i][j], s) for j in range(N)] for i in range(N)]
        for i in range(N):
            row = load_row(mb, level, OUT0, i)
            for j in range(N):
                mf[level, LO0 + i * N + j] = dot_row(row, di_up, j)
        di_down = [[down(di[i][j], s) for j in range(N)] for i in range(N)]
        for i in range(N):
            row = load_row(mb, level, IN0, i)
            for j in range(N):
                mf[level, LI0 + i * N + j] = dot_row(row, di_down, j)
        in_up = [[up(mb[level, IN0 + i * N + j], s) for j in range(N)] for i in range(N)]
        acc = []
        for i in range(N):
            row = load_row(mf, level, LO0, i)
            acc.append([d[i][j] - dot_row(row, in_up, j) for j in range(N)])
        out_down = [[down(mb[level, OUT0 + i * N + j], s) for j in range(N)] for i in range(N)]
        for i in range(N):
            row = load_row(mf, level, LI0, i)
            for j in range(N):
                val = acc[i][j] - dot_row(row, out_down, j)
                if level < 2:
                    mb[level + 1, D0 + i * N + j] = val
                else:
                    sd[pl.ds(i * N + j, 1), :] = val[0:1]
        if level < 2:
            out_up = [[up(mb[level, OUT0 + i * N + j], s) for j in range(N)] for i in range(N)]
            for i in range(N):
                row = load_row(mf, level, LO0, i)
                for j in range(N):
                    mb[level + 1, OUT0 + i * N + j] = dot_row(row, out_up, j)
            in_down = [[down(mb[level, IN0 + i * N + j], s) for j in range(N)] for i in range(N)]
            for i in range(N):
                row = load_row(mf, level, LI0, i)
                for j in range(N):
                    mb[level + 1, IN0 + i * N + j] = dot_row(row, in_down, j)
    sd[pl.ds(NN, 1), :] = first_lam[0:1]
    sd[pl.ds(NN + 1, 1), :] = first_mask[0:1]
    sd[pl.ds(NN + 2, 5), :] = jnp.zeros((5, LANES), F32)


def join_kernel(own_ref, other_ref, j_ref):
    lam, mask = own_ref[pl.ds(NN, 1), :], own_ref[pl.ds(NN + 1, 1), :]
    other_lam, other_mask = other_ref[pl.ds(NN, 1), :], other_ref[pl.ds(NN + 1, 1), :]
    c = 0.25 * (lam * other_mask + other_lam * mask)

    def total(ref):
        mat = [[ref[pl.ds(i * N + j, 1), :] for j in range(N)] for i in range(N)]
        return [[mat[i][j] + c if i == j else mat[i][j] for j in range(N)] for i in range(N)]

    own, inv_other = total(own_ref), invert(total(other_ref))
    schur = [[own[i][j] - c * (c * inv_other[i][j]) for j in range(N)] for i in range(N)]
    j1 = invert(schur)
    j2 = mat_mul(j1, inv_other)
    for i in range(N):
        for j in range(N):
            j_ref[pl.ds(i * N + j, 1), :] = j1[i][j]
            j_ref[pl.ds(NN + i * N + j, 1), :] = c * j2[i][j]


def stencil_block(u, v, z, planes, zprev, znext, tprev, tnext):
    cur = u[v, z]
    rows = lax.broadcasted_iota(jnp.int32, cur.shape, 0)
    behind = u[v, z - 1] if z > 0 else zprev[v]
    ahead = u[v, z + 1] if z < planes - 1 else znext[v]
    sectors = cur.shape[0]
    before_t = jnp.where(rows == 0, tprev[v, pl.ds(z, 1), :], pltpu.roll(cur, 1, 0))
    after_t = jnp.where(rows == sectors - 1, tnext[v, pl.ds(z, 1), :], pltpu.roll(cur, sectors - 1, 0))
    return behind + ahead + before_t + after_t - 4.0 * cur + 0.5 * (behind - ahead)


def forward_body(rhs_t, mf, scal, coup_ref, upw_ref, e_ref, o_ref, y_ref):
    a, b = splat_consts(coup_ref, upw_ref)
    zero = jnp.zeros((SEG, LANES), F32)
    carry = [zero] * N
    first = None
    for m in range(HALF):
        inv, fl, fr = scal[m, 0], scal[m, 1], scal[m, 2]
        odd = [strided(rhs_t.at[v], 2 * m + 1) for v in range(N)]
        scaled = [x * inv for x in odd]
        ta = mat_vec(a, scaled)
        tb = mat_vec(b, scaled)
        for v in range(N):
            o_ref[m, v] = odd[v]
            e_ref[slot_of(m), v] = strided(rhs_t.at[v], 2 * m) + carry[v] + fl * ta[v]
        carry = [fr * tb[v] for v in range(N)]
    for v in range(N):
        e_ref[slot_of(0), v] = e_ref[slot_of(0), v] + down(carry[v], 1)
        e_ref[slot_of(HALF), v] = zero
    for m, s in STEPS:
        vec = [e_ref[slot_of(m), v] for v in range(N)]
        lo = mat_vec(load_mat(mf, slot_of(m), LO0), vec)
        li = mat_vec(load_mat(mf, slot_of(m), LI0), vec)
        for v in range(N):
            e_ref[slot_of(m - s), v] = e_ref[slot_of(m - s), v] + lo[v]
            e_ref[slot_of(m + s), v] = e_ref[slot_of(m + s), v] + li[v]
    cur = [e_ref[slot_of(0), v] + down(e_ref[slot_of(HALF), v], 1) for v in range(N)]
    for level, s in enumerate((1, 2, 4)):
        for v in range(N):
            e_ref[level, v] = cur[v]
        lo = mat_vec(load_mat(mf, level, LO0), [up(x, s) for x in cur])
        li = mat_vec(load_mat(mf, level, LI0), [down(x, s) for x in cur])
        cur = [cur[v] + lo[v] + li[v] for v in range(N)]
    for v in range(N):
        y_ref[pl.ds(v, 1), :] = cur[v][0:1]
    y_ref[pl.ds(N, 3), :] = jnp.zeros((3, LANES), F32)


def forward_first_kernel(
    u, zprev, znext, tprev, tnext, blank, idx, table, mf, scal, coup, upw, e_ref, o_ref, y_ref, rhs_t
):
    planes, sectors, radial = blank.shape
    mask = blank[...].astype(F32).reshape(planes * sectors, radial)
    rows = lax.broadcasted_iota(jnp.int32, (table.shape[0], LANES), 0)
    onehot = (rows == idx[...]).astype(F32).T
    for v in range(N):
        force = jnp.dot(
            onehot,
            table[:, pl.ds(v * radial, radial)],
            precision=lax.Precision.HIGHEST,
            preferred_element_type=F32,
        )
        blocks = [stencil_block(u, v, z, planes, zprev, znext, tprev, tnext) for z in range(planes)]
        rhs = mask * (jnp.concatenate(blocks, axis=0) + force)
        rhs_t[v] = rhs.T
    forward_body(rhs_t, mf, scal, coup, upw, e_ref, o_ref, y_ref)


def forward_second_kernel(
    u, zprev, znext, tprev, tnext, blank, mf, scal, coup, upw, e_ref, o_ref, y_ref, rhs_t
):
    planes, sectors, radial = blank.shape
    mask = blank[...].astype(F32).reshape(planes * sectors, radial)
    for v in range(N):
        blocks = [stencil_block(u, v, z, planes, zprev, znext, tprev, tnext) for z in range(planes)]
        rhs_t[v] = (mask * jnp.concatenate(blocks, axis=0)).T
    forward_body(rhs_t, mf, scal, coup, upw, e_ref, o_ref, y_ref)


def backward_body(y_own, y_other, j_ref, mb, scal, coup_ref, upw_ref, e_ref, o_ref, x_ref, x_t):
    a, b = splat_consts(coup_ref, upw_ref)
    sub = lax.broadcasted_iota(jnp.int32, (SEG, LANES), 0)
    own = [y_own[pl.ds(v, 1), :] for v in range(N)]
    other = [y_other[pl.ds(v, 1), :] for v in range(N)]
    cur = []
    for i in range(N):
        acc = j_ref[pl.ds(i * N, 1), :] * own[0]
        for k in range(N):
            if k > 0:
                acc = acc + j_ref[pl.ds(i * N + k, 1), :] * own[k]
            acc = acc + j_ref[pl.ds(NN + i * N + k, 1), :] * other[k]
        cur.append(jnp.broadcast_to(acc, (SEG, LANES)))

    def recover(slot, high, low):
        o = mat_vec(load_mat(mb, slot, OUT0), high)
        i = mat_vec(load_mat(mb, slot, IN0), low)
        total = [e_ref[slot, v] + o[v] + i[v] for v in range(N)]
        return mat_vec(load_mat(mb, slot, D0), total)

    for level, s in ((2, 4), (1, 2), (0, 1)):
        new = recover(level, [up(x, s) for x in cur], [down(x, s) for x in cur])
        cur = [jnp.where(sub % (2 * s) == s, new[v], cur[v]) for v in range(N)]
    for v in range(N):
        x_ref[0, v] = cur[v]
        x_ref[HALF, v] = up(cur[v], 1)
    for m, s in reversed(STEPS):
        new = recover(
            slot_of(m), [x_ref[m + s, v] for v in range(N)], [x_ref[m - s, v] for v in range(N)]
        )
        for v in range(N):
            x_ref[m, v] = new[v]
    low = [x_ref[0, v] for v in range(N)]
    for m in range(HALF):
        inv, fl, fr = scal[m, 0], scal[m, 1], scal[m, 2]
        high = [x_ref[m + 1, v] for v in range(N)]
        ta = mat_vec(a, high)
        tb = mat_vec(b, low)
        for v in range(N):
            odd = inv * (o_ref[m, v] + fr * ta[v] + fl * tb[v])
            x_t.at[v][pl.ds(2 * m, SEG, stride=2 * HALF), :] = low[v]
            x_t.at[v][pl.ds(2 * m + 1, SEG, stride=2 * HALF), :] = odd
        low = high


def backward_first_kernel(
    y_own, y_other, j_ref, mb, scal, coup, upw, e_ref, o_ref,
    out, zfirst, zlast, tfirst, tlast, x_ref, x_t,
):
    backward_body(y_own, y_other, j_ref, mb, scal, coup, upw, e_ref, o_ref, x_ref, x_t)
    _, planes, sectors, radial = out.shape
    for v in range(N):
        field = x_t[v].T.reshape(planes, sectors, radial)
        out[v] = field
        zfirst[v] = field[0]
        zlast[v] = field[planes - 1]
        for z in range(planes):
            tfirst[v, pl.ds(z, 1), :] = field[z, 0:1]
            tlast[v, pl.ds(z, 1), :] = field[z, sectors - 1 : sectors]


def backward_second_kernel(
    y_own, y_other, j_ref, mb, scal, coup, upw, e_ref, o_ref, first, out, x_ref, x_t
):
    backward_body(y_own, y_other, j_ref, mb, scal, coup, upw, e_ref, o_ref, x_ref, x_t)
    _, planes, sectors, radial = out.shape
    for v in range(N):
        out[v] = first[v] + 0.5 * x_t[v].T.reshape(planes, sectors, radial)


def call(kernel, inputs, outs, scratch, flops, smem=()):
    vmem = pl.BlockSpec(memory_space=pltpu.VMEM)
    in_specs = [pl.BlockSpec(memory_space=pltpu.SMEM) if i in smem else vmem for i in range(len(inputs))]
    out_shape = [jax.ShapeDtypeStruct(s, F32) for s in outs]
    moved = sum(x.size for x in inputs) * 4 + sum(s.size for s in out_shape) * 4
    return pl.pallas_call(
        kernel,
        out_shape=out_shape,
        in_specs=in_specs,
        out_specs=[vmem] * len(outs),
        scratch_shapes=[pltpu.VMEM(s, F32) for s in scratch],
        compiler_params=pltpu.CompilerParams(vmem_limit_bytes=VMEM_LIMIT),
        cost_estimate=pl.CostEstimate(flops=flops, bytes_accessed=moved, transcendentals=0),
    )(*inputs)


def shifted(x, axis, step, wrap):
    size = lax.axis_size(axis)
    pairs = [(i, (i + step) % size) for i in range(size) if wrap or 0 <= i + step < size]
    return lax.ppermute(x, axis, pairs)


def halos(zfirst, zlast, tfirst, tlast):
    return (
        shifted(zlast, "ax", 1, False),
        shifted(zfirst, "ax", -1, False),
        shifted(tlast, "az", 1, True),
        shifted(tfirst, "az", -1, True),
    )


def per_device(
    flow_state, radial_coef, blanking, canard_index, canard_table, coupling, upwind_split
):
    comps, planes, sectors, radial = flow_state.shape
    tile = (SEG, LANES)
    upw = upwind_split.reshape(1, N)
    local_rows = canard_table.shape[1]
    half_turn = lax.axis_size("az") // 2

    first_halos = halos(
        flow_state[:, 0], flow_state[:, planes - 1], flow_state[:, :, 0], flow_state[:, :, sectors - 1]
    )
    table = lax.all_gather(
        canard_table.reshape(local_rows, comps * radial), "az", axis=0, tiled=True
    )
    idx = canard_index.reshape(1, planes * sectors)

    field = (comps, planes, sectors, radial)
    mb, mf, scal, sd = call(
        factor_kernel,
        (radial_coef, blanking, coupling, upw),
        [(HALF + 3, 3 * NN) + tile, (HALF + 2, 2 * NN) + tile, (HALF, 3) + tile, (32, LANES)],
        [(radial, LANES), (radial, LANES), (2 * HALF + 1,) + tile, (4, NN) + tile],
        32_000_000,
        (2, 3),
    )
    other_sd = shifted(sd, "az", half_turn, True)
    fwd_outs = [(HALF + 3, N) + tile, (HALF, N) + tile, tile]
    rhs_scratch = [(N, radial, LANES)]
    back_scratch = [(HALF + 1, N) + tile, (N, radial, LANES)]

    e1, o1, y1 = call(
        forward_first_kernel,
        (flow_state, *first_halos, blanking, idx, table, mf, scal, coupling, upw),
        fwd_outs,
        rhs_scratch,
        4_000_000,
        (10, 11),
    )
    other_y1 = shifted(y1, "az", half_turn, True)
    (joint,) = call(join_kernel, (sd, other_sd), [(2 * NN, LANES)], [], 200_000)
    first, *edges = call(
        backward_first_kernel,
        (y1, other_y1, joint, mb, scal, coupling, upw, e1, o1),
        [field, (comps, sectors, radial), (comps, sectors, radial), (comps, planes, radial), (comps, planes, radial)],
        back_scratch,
        4_000_000,
        (5, 6),
    )
    second_halos = halos(*edges)
    e2, o2, y2 = call(
        forward_second_kernel,
        (first, *second_halos, blanking, mf, scal, coupling, upw),
        fwd_outs,
        rhs_scratch,
        4_000_000,
        (8, 9),
    )
    other_y2 = shifted(y2, "az", half_turn, True)
    (update,) = call(
        backward_second_kernel,
        (y2, other_y2, joint, mb, scal, coupling, upw, e2, o2, first),
        [field],
        back_scratch,
        4_000_000,
        (5, 6),
    )
    return update


def solution(mesh):
    return jax.shard_map(
        per_device,
        mesh=mesh,
        in_specs=(
            P(None, "ax", "az", None),
            P("ax", "az", None),
            P("ax", "az", None),
            P("ax", "az"),
            P("ax", "az", None, None),
            P(),
            P(),
        ),
        out_specs=P(None, "ax", "az", None),
        check_vma=False,
    )
```

```python
import jax
import jax.numpy as jnp
from jax import lax
from jax.experimental import pallas as pl
from jax.experimental.pallas import tpu as pltpu
from jax.sharding import PartitionSpec as P

N = 5
NN = 25
SEG = 8
LANES = 128
HALF = 16
VMEM_LIMIT = 16 * 1024 * 1024
F32 = jnp.float32
STEPS = [(s * (2 * i + 1), s) for s in (1, 2, 4, 8) for i in range(8 // s)]


def up(x, s):
    return pltpu.roll(x, SEG - s, 0)


def down(x, s):
    return pltpu.roll(x, s, 0)


def splat_consts(coupling_ref, upwind_ref):
    shape = (SEG, LANES)
    p = [[jnp.full(shape, coupling_ref[i, j], F32) for j in range(N)] for i in range(N)]
    w = [jnp.full(shape, upwind_ref[i], F32) for i in range(N)]
    a = [[p[i][j] + w[i] if i == j else p[i][j] for j in range(N)] for i in range(N)]
    b = [[(1.0 - w[i]) - p[j][i] if i == j else -p[j][i] for j in range(N)] for i in range(N)]
    return a, b


def dot_row(row, cols, j):
    acc = row[0] * cols[0][j]
    for k in range(1, N):
        acc = acc + row[k] * cols[k][j]
    return acc


def mat_mul(x, y):
    return [[dot_row(x[i], y, j) for j in range(N)] for i in range(N)]


def mat_vec(x, v):
    out = []
    for i in range(N):
        acc = x[i][0] * v[0]
        for k in range(1, N):
            acc = acc + x[i][k] * v[k]
        out.append(acc)
    return out


def invert(matrix):
    m = [list(row) for row in matrix]
    for p in range(N):
        piv = 1.0 / m[p][p]
        m[p] = [piv if j == p else m[p][j] * piv for j in range(N)]
        for i in range(N):
            if i != p:
                f = m[i][p]
                m[i] = [-(f * piv) if j == p else m[i][j] - f * m[p][j] for j in range(N)]
    return m


def load_mat(ref, slot, base):
    return [[ref[slot, base + i * N + j] for j in range(N)] for i in range(N)]


def load_row(ref, slot, base, i):
    return [ref[slot, base + i * N + j] for j in range(N)]


def store_mat(ref, slot, base, mat):
    for i in range(N):
        for j in range(N):
            ref[slot, base + i * N + j] = mat[i][j]


def strided(ref, k):
    return ref[pl.ds(k, SEG, stride=2 * HALF), :]


def slot_of(p):
    return p + 2


LAM_ROW, MASK_ROW, VEC_ROW, JOINT_ROWS = NN, NN + 1, NN + 2, 32
D0, OUT0, IN0 = 0, NN, 2 * NN
LO0, LI0 = 0, NN


def prelude_kernel(
    flow, table, coef, blank, index, coup, upw,
    u, rows, coef_ref, mask_ref, place, cst, zfirst, zlast, tfirst, tlast,
    piece, blank_ref, index_ref, coup_ref, upw_ref, sem,
):
    pairs = (
        (table.at[0], piece),
        (coup, coup_ref),
        (upw, upw_ref),
        (index, index_ref),
        (blank, blank_ref),
        (coef, coef_ref),
        (flow, u),
    )
    copies = [pltpu.make_async_copy(src, dst, sem.at[i]) for i, (src, dst) in enumerate(pairs)]
    for copy in copies:
        copy.start()
    _, planes, sectors, radial = u.shape
    copies[0].wait()
    for row in range(piece.shape[1]):
        for v in range(N):
            rows[pl.ds(row, 1), pl.ds(v * radial, radial)] = piece[v, pl.ds(row, 1), :]
    copies[1].wait()
    copies[2].wait()
    a, b = splat_consts(coup_ref, upw_ref)
    store_mat(cst, 0, 0, a)
    store_mat(cst, 1, 0, b)
    copies[3].wait()
    place[...] = table_place(index_ref[...])
    copies[4].wait()
    mask_ref[...] = blank_ref[...].astype(F32).reshape(planes * sectors, radial)
    copies[5].wait()
    copies[6].wait()
    for v in range(N):
        zfirst[v] = u[v, 0]
        zlast[v] = u[v, planes - 1]
        for z in range(planes):
            tfirst[v, pl.ds(z, 1), :] = u[v, z, pl.ds(0, 1), :]
            tlast[v, pl.ds(z, 1), :] = u[v, z, pl.ds(sectors - 1, 1), :]


def append_kernel(low, high, out):
    half = low.shape[0]
    out[pl.ds(0, half), :] = low[...]
    out[pl.ds(half, half), :] = high[...]


def factor_kernel(coef_ref, mask_ref, cst, mb, mf, scal, sd, lam_t, mask_t, face, pw):
    mask = mask_ref[...]
    lam = coef_ref[...].reshape(LANES, 2 * HALF * SEG) * mask
    lam_t[...] = lam.T
    mask_t[...] = mask.T
    a, b = load_mat(cst, 0, 0), load_mat(cst, 1, 0)
    for which, mat in enumerate((mat_mul(a, a), mat_mul(b, b), mat_mul(a, b), mat_mul(b, a))):
        store_mat(pw, which, 0, mat)

    sub = lax.broadcasted_iota(jnp.int32, (SEG, LANES), 0)
    first_lam, first_mask = strided(lam_t, 0), strided(mask_t, 0)
    lam_k, mask_k = first_lam, first_mask
    for k in range(2 * HALF):
        if k < 2 * HALF - 1:
            lam_n, mask_n = strided(lam_t, k + 1), strided(mask_t, k + 1)
            f = 0.5 * (lam_k * mask_n + lam_n * mask_k)
        else:
            lam_n, mask_n = up(first_lam, 1), up(first_mask, 1)
            f = jnp.where(sub == SEG - 1, 0.0, 0.5 * (lam_k * mask_n + lam_n * mask_k))
        face[k + 1] = f
        lam_k, mask_k = lam_n, mask_n
    face[0] = down(face[2 * HALF], 1)

    def build_odd(m, c):
        fl, fr = face[2 * m + 1], face[2 * m + 2]
        scal[m, 0] = 1.0 / (1.0 + 0.5 * (fl + fr))
        scal[m, 1] = fl
        scal[m, 2] = fr
        return c

    lax.fori_loop(0, HALF, build_odd, 0)

    def build_even(p, c):
        prev = jnp.where(p == 0, HALF - 1, p - 1)
        inv, fl, fr = scal[p, 0], scal[p, 1], scal[p, 2]
        inv_p, fl_p, fr_p = scal[prev, 0], scal[prev, 1], scal[prev, 2]
        beta = fr_p * fr_p * inv_p
        delta = fr_p * fl_p * inv_p
        beta = jnp.where(p == 0, down(beta, 1), beta)
        alpha = fl * fl * inv
        gamma = fl * fr * inv
        d = 1.0 + 0.5 * (face[2 * p] + face[2 * p + 1])
        for i in range(N):
            for j in range(N):
                e = i * N + j
                val = -(alpha * pw[2, e] + beta * pw[3, e])
                mb[slot_of(p), D0 + e] = d + val if i == j else val
                mb[slot_of(p), OUT0 + e] = gamma * pw[0, e]
                mb[slot_of(p), IN0 + e] = delta * pw[1, e]
        return c

    lax.fori_loop(0, HALF, build_even, 0)
    last = scal[HALF - 1, 1] * scal[HALF - 1, 2] * scal[HALF - 1, 0]
    for e in range(NN):
        mb[slot_of(HALF), D0 + e] = jnp.zeros((SEG, LANES), F32)
        mb[slot_of(HALF), OUT0 + e] = jnp.zeros((SEG, LANES), F32)
        mb[slot_of(HALF), IN0 + e] = last * pw[1, e]

    sd[...] = jnp.zeros((JOINT_ROWS, LANES), F32)
    sd[pl.ds(LAM_ROW, 1), :] = first_lam[0:1]
    sd[pl.ds(MASK_ROW, 1), :] = first_mask[0:1]
    eliminate(mb, mf, 0, 8)


def eliminate(mb, mf, start, stop):
    def step(it, c):
        s = jnp.where(it < 8, 1, jnp.where(it < 12, 2, jnp.where(it < 14, 4, 8)))
        first = jnp.where(it < 8, 0, jnp.where(it < 12, 8, jnp.where(it < 14, 12, 14)))
        m = s * (2 * (it - first) + 1)
        sm, sp, sq = slot_of(m), slot_of(m - s), slot_of(m + s)
        di = invert(load_mat(mb, sm, D0))
        store_mat(mb, sm, D0, di)
        for i in range(N):
            row = load_row(mb, sp, OUT0, i)
            for j in range(N):
                mf[sm, LO0 + i * N + j] = dot_row(row, di, j)
            row = load_row(mb, sq, IN0, i)
            for j in range(N):
                mf[sm, LI0 + i * N + j] = dot_row(row, di, j)
        in_m = load_mat(mb, sm, IN0)
        for i in range(N):
            row = load_row(mf, sm, LO0, i)
            for j in range(N):
                e = i * N + j
                mb[sp, D0 + e] = mb[sp, D0 + e] - dot_row(row, in_m, j)
            row = load_row(mf, sm, LI0, i)
            for j in range(N):
                mb[sq, IN0 + i * N + j] = dot_row(row, in_m, j)
        out_m = load_mat(mb, sm, OUT0)
        for i in range(N):
            row = load_row(mf, sm, LI0, i)
            for j in range(N):
                e = i * N + j
                mb[sq, D0 + e] = mb[sq, D0 + e] - dot_row(row, out_m, j)
            row = load_row(mf, sm, LO0, i)
            for j in range(N):
                mb[sp, OUT0 + i * N + j] = dot_row(row, out_m, j)
        return c

    lax.fori_loop(start, stop, step, 0)


def factor_rest_kernel(mb_in, mf_in, sd_in, mb, mf, sd):
    eliminate(mb, mf, 8, len(STEPS))
    s0, s16 = slot_of(0), slot_of(HALF)
    for e in range(NN):
        mb[0, D0 + e] = mb[s0, D0 + e] + down(mb[s16, D0 + e], 1)
        mb[0, OUT0 + e] = mb[s0, OUT0 + e]
        mb[0, IN0 + e] = down(mb[s16, IN0 + e], 1)
    for level, s in enumerate((1, 2, 4)):
        d = load_mat(mb, level, D0)
        di = invert(d)
        store_mat(mb, level, D0, di)
        di_up = [[up(di[i][j], s) for j in range(N)] for i in range(N)]
        for i in range(N):
            row = load_row(mb, level, OUT0, i)
            for j in range(N):
                mf[level, LO0 + i * N + j] = dot_row(row, di_up, j)
        di_down = [[down(di[i][j], s) for j in range(N)] for i in range(N)]
        for i in range(N):
            row = load_row(mb, level, IN0, i)
            for j in range(N):
                mf[level, LI0 + i * N + j] = dot_row(row, di_down, j)
        in_up = [[up(mb[level, IN0 + i * N + j], s) for j in range(N)] for i in range(N)]
        acc = []
        for i in range(N):
            row = load_row(mf, level, LO0, i)
            acc.append([d[i][j] - dot_row(row, in_up, j) for j in range(N)])
        out_down = [[down(mb[level, OUT0 + i * N + j], s) for j in range(N)] for i in range(N)]
        for i in range(N):
            row = load_row(mf, level, LI0, i)
            for j in range(N):
                val = acc[i][j] - dot_row(row, out_down, j)
                if level < 2:
                    mb[level + 1, D0 + i * N + j] = val
                else:
                    sd[pl.ds(i * N + j, 1), :] = val[0:1]
        if level < 2:
            out_up = [[up(mb[level, OUT0 + i * N + j], s) for j in range(N)] for i in range(N)]
            for i in range(N):
                row = load_row(mf, level, LO0, i)
                for j in range(N):
                    mb[level + 1, OUT0 + i * N + j] = dot_row(row, out_up, j)
            in_down = [[down(mb[level, IN0 + i * N + j], s) for j in range(N)] for i in range(N)]
            for i in range(N):
                row = load_row(mf, level, LI0, i)
                for j in range(N):
                    mb[level + 1, IN0 + i * N + j] = dot_row(row, in_down, j)


def join(own_ref, other_ref, j_ref):
    lam, mask = own_ref[pl.ds(LAM_ROW, 1), :], own_ref[pl.ds(MASK_ROW, 1), :]
    other_lam, other_mask = other_ref[pl.ds(LAM_ROW, 1), :], other_ref[pl.ds(MASK_ROW, 1), :]
    c = 0.25 * (lam * other_mask + other_lam * mask)

    def total(ref):
        mat = [[ref[pl.ds(i * N + j, 1), :] for j in range(N)] for i in range(N)]
        return [[mat[i][j] + c if i == j else mat[i][j] for j in range(N)] for i in range(N)]

    own, inv_other = total(own_ref), invert(total(other_ref))
    schur = [[own[i][j] - c * (c * inv_other[i][j]) for j in range(N)] for i in range(N)]
    j1 = invert(schur)
    j2 = mat_mul(j1, inv_other)
    for i in range(N):
        for j in range(N):
            j_ref[pl.ds(i * N + j, 1), :] = j1[i][j]
            j_ref[pl.ds(NN + i * N + j, 1), :] = c * j2[i][j]


def stencil_block(u, v, z, planes, zprev, znext, tprev, tnext):
    cur = u[v, z]
    rows = lax.broadcasted_iota(jnp.int32, cur.shape, 0)
    behind = u[v, z - 1] if z > 0 else zprev[v]
    ahead = u[v, z + 1] if z < planes - 1 else znext[v]
    sectors = cur.shape[0]
    before_t = jnp.where(rows == 0, tprev[v, pl.ds(z, 1), :], pltpu.roll(cur, 1, 0))
    after_t = jnp.where(rows == sectors - 1, tnext[v, pl.ds(z, 1), :], pltpu.roll(cur, sectors - 1, 0))
    return behind + ahead + before_t + after_t - 4.0 * cur + 0.5 * (behind - ahead)


def forward_body(rhs_t, mf, scal, cst, e_ref, o_ref):
    a, b = load_mat(cst, 0, 0), load_mat(cst, 1, 0)
    zero = jnp.zeros((SEG, LANES), F32)
    carry = [zero] * N
    first = None
    for m in range(HALF):
        inv, fl, fr = scal[m, 0], scal[m, 1], scal[m, 2]
        odd = [strided(rhs_t.at[v], 2 * m + 1) for v in range(N)]
        scaled = [x * inv for x in odd]
        ta = mat_vec(a, scaled)
        tb = mat_vec(b, scaled)
        for v in range(N):
            o_ref[m, v] = odd[v]
            e_ref[slot_of(m), v] = strided(rhs_t.at[v], 2 * m) + carry[v] + fl * ta[v]
        carry = [fr * tb[v] for v in range(N)]
    for v in range(N):
        e_ref[slot_of(0), v] = e_ref[slot_of(0), v] + down(carry[v], 1)
        e_ref[slot_of(HALF), v] = zero
    for m, s in STEPS:
        vec = [e_ref[slot_of(m), v] for v in range(N)]
        lo = mat_vec(load_mat(mf, slot_of(m), LO0), vec)
        li = mat_vec(load_mat(mf, slot_of(m), LI0), vec)
        for v in range(N):
            e_ref[slot_of(m - s), v] = e_ref[slot_of(m - s), v] + lo[v]
            e_ref[slot_of(m + s), v] = e_ref[slot_of(m + s), v] + li[v]
    cur = [e_ref[slot_of(0), v] + down(e_ref[slot_of(HALF), v], 1) for v in range(N)]
    for level, s in enumerate((1, 2, 4)):
        for v in range(N):
            e_ref[level, v] = cur[v]
        lo = mat_vec(load_mat(mf, level, LO0), [up(x, s) for x in cur])
        li = mat_vec(load_mat(mf, level, LI0), [down(x, s) for x in cur])
        cur = [cur[v] + lo[v] + li[v] for v in range(N)]
    return [cur[v][0:1] for v in range(N)]


def doubling_bits():
    return [bit for bit in (16, 8, 2, 4, 1) if bit < lax.axis_size("az")]


def table_place(index):
    apart = lax.shift_right_logical(index, 2) ^ lax.axis_index("az")
    block = jnp.zeros_like(apart)
    for i, bit in enumerate(doubling_bits()):
        block = block | (jnp.where((apart & bit) != 0, 1, 0) << i)
    return block * 4 + (index & 3)


def forward_first_kernel(
    u, zprev, znext, tprev, tnext, mask_ref, place, low, high, mf, scal, cst, sd,
    e_ref, o_ref, joint, rhs_t,
):
    planes, sectors = place.shape
    radial = mask_ref.shape[1]
    mask = mask_ref[...]
    half = low.shape[0]
    rows = lax.broadcasted_iota(jnp.int32, (2 * half, sectors), 0)
    onehot = [(rows == place[pl.ds(z, 1), :]).astype(F32).T for z in range(planes)]
    hot_low = jnp.concatenate([x[:, :half] for x in onehot], axis=0)
    hot_high = jnp.concatenate([x[:, half:] for x in onehot], axis=0)

    def pick(hot, rows, v):
        return jnp.dot(
            hot,
            rows[:, pl.ds(v * radial, radial)],
            precision=lax.Precision.HIGHEST,
            preferred_element_type=F32,
        )

    for v in range(N):
        force = pick(hot_low, low, v) + pick(hot_high, high, v)
        blocks = [stencil_block(u, v, z, planes, zprev, znext, tprev, tnext) for z in range(planes)]
        rhs = mask * (jnp.concatenate(blocks, axis=0) + force)
        rhs_t[v] = rhs.T
    reduced = forward_body(rhs_t, mf, scal, cst, e_ref, o_ref)
    joint[...] = sd[...]
    for v in range(N):
        joint[pl.ds(VEC_ROW + v, 1), :] = reduced[v]


def forward_second_kernel(
    u, zprev, znext, tprev, tnext, mask_ref, mf, scal, cst, e_ref, o_ref, y_ref, rhs_t
):
    planes = u.shape[1]
    mask = mask_ref[...]
    for v in range(N):
        blocks = [stencil_block(u, v, z, planes, zprev, znext, tprev, tnext) for z in range(planes)]
        rhs_t[v] = (mask * jnp.concatenate(blocks, axis=0)).T
    reduced = forward_body(rhs_t, mf, scal, cst, e_ref, o_ref)
    y_ref[...] = jnp.zeros((SEG, LANES), F32)
    for v in range(N):
        y_ref[pl.ds(v, 1), :] = reduced[v]


def backward_body(own, other, j_ref, mb, scal, cst, e_ref, o_ref, x_ref, x_t):
    a, b = load_mat(cst, 0, 0), load_mat(cst, 1, 0)
    sub = lax.broadcasted_iota(jnp.int32, (SEG, LANES), 0)
    cur = []
    for i in range(N):
        acc = j_ref[pl.ds(i * N, 1), :] * own[0]
        for k in range(N):
            if k > 0:
                acc = acc + j_ref[pl.ds(i * N + k, 1), :] * own[k]
            acc = acc + j_ref[pl.ds(NN + i * N + k, 1), :] * other[k]
        cur.append(jnp.broadcast_to(acc, (SEG, LANES)))

    def recover(slot, high, low):
        o = mat_vec(load_mat(mb, slot, OUT0), high)
        i = mat_vec(load_mat(mb, slot, IN0), low)
        total = [e_ref[slot, v] + o[v] + i[v] for v in range(N)]
        return mat_vec(load_mat(mb, slot, D0), total)

    for level, s in ((2, 4), (1, 2), (0, 1)):
        new = recover(level, [up(x, s) for x in cur], [down(x, s) for x in cur])
        cur = [jnp.where(sub % (2 * s) == s, new[v], cur[v]) for v in range(N)]
    for v in range(N):
        x_ref[0, v] = cur[v]
        x_ref[HALF, v] = up(cur[v], 1)
    for m, s in reversed(STEPS):
        new = recover(
            slot_of(m), [x_ref[m + s, v] for v in range(N)], [x_ref[m - s, v] for v in range(N)]
        )
        for v in range(N):
            x_ref[m, v] = new[v]
    low = [x_ref[0, v] for v in range(N)]
    for m in range(HALF):
        inv, fl, fr = scal[m, 0], scal[m, 1], scal[m, 2]
        high = [x_ref[m + 1, v] for v in range(N)]
        ta = mat_vec(a, high)
        tb = mat_vec(b, low)
        for v in range(N):
            odd = inv * (o_ref[m, v] + fr * ta[v] + fl * tb[v])
            x_t.at[v][pl.ds(2 * m, SEG, stride=2 * HALF), :] = low[v]
            x_t.at[v][pl.ds(2 * m + 1, SEG, stride=2 * HALF), :] = odd
        low = high


def backward_first_kernel(
    joint, other_joint, mb, scal, cst, e_ref, o_ref,
    out, zfirst, zlast, tfirst, tlast, j_ref, x_ref, x_t,
):
    join(joint, other_joint, j_ref)
    own = [joint[pl.ds(VEC_ROW + v, 1), :] for v in range(N)]
    other = [other_joint[pl.ds(VEC_ROW + v, 1), :] for v in range(N)]
    backward_body(own, other, j_ref, mb, scal, cst, e_ref, o_ref, x_ref, x_t)
    _, planes, sectors, radial = out.shape
    for v in range(N):
        field = x_t[v].T.reshape(planes, sectors, radial)
        out[v] = field
        zfirst[v] = field[0]
        zlast[v] = field[planes - 1]
        for z in range(planes):
            tfirst[v, pl.ds(z, 1), :] = field[z, 0:1]
            tlast[v, pl.ds(z, 1), :] = field[z, sectors - 1 : sectors]


def backward_second_kernel(
    y_own, y_other, j_ref, mb, scal, cst, e_ref, o_ref, first, out, x_ref, x_t
):
    own = [y_own[pl.ds(v, 1), :] for v in range(N)]
    other = [y_other[pl.ds(v, 1), :] for v in range(N)]
    backward_body(own, other, j_ref, mb, scal, cst, e_ref, o_ref, x_ref, x_t)
    _, planes, sectors, radial = out.shape
    for v in range(N):
        out[v] = first[v] + 0.5 * x_t[v].T.reshape(planes, sectors, radial)


def call(kernel, inputs, outs, scratch, us, hbm=False, aliases=None):
    vmem = pl.BlockSpec(memory_space=pltpu.VMEM)
    if hbm:
        inputs = [pltpu.with_memory_space_constraint(x, pltpu.HBM) for x in inputs]
    in_spec = pl.BlockSpec(memory_space=pltpu.HBM) if hbm else vmem
    out_shape = [s if isinstance(s, jax.ShapeDtypeStruct) else jax.ShapeDtypeStruct(s, F32) for s in outs]
    return pl.pallas_call(
        kernel,
        out_shape=out_shape,
        in_specs=[in_spec] * len(inputs),
        out_specs=[vmem] * len(outs),
        scratch_shapes=[pltpu.VMEM(s, F32) if isinstance(s, tuple) else s for s in scratch],
        input_output_aliases=aliases or {},
        compiler_params=pltpu.CompilerParams(vmem_limit_bytes=VMEM_LIMIT),
        cost_estimate=pl.CostEstimate(
            flops=int(us * 1e9), bytes_accessed=int(us * 3e6), transcendentals=0
        ),
    )(*inputs)


def shifted(x, axis, step, wrap):
    size = lax.axis_size(axis)
    pairs = [(i, (i + step) % size) for i in range(size) if wrap or 0 <= i + step < size]
    return lax.ppermute(x, axis, pairs)


def halos(zfirst, zlast, tfirst, tlast):
    return (
        shifted(zlast, "ax", 1, False),
        shifted(zfirst, "ax", -1, False),
        shifted(tlast, "az", 1, True),
        shifted(tfirst, "az", -1, True),
    )


def xor_swap(x, bit):
    return lax.ppermute(x, "az", [(i, i ^ bit) for i in range(lax.axis_size("az"))])


def append(low, high):
    (both,) = call(append_kernel, (low, high), [(2 * low.shape[0], low.shape[1])], [], 0.2)
    return both


def after(x, *others):
    return lax.optimization_barrier((x, *others))[0]


def per_device(
    flow_state, radial_coef, blanking, canard_index, canard_table, coupling, upwind_split
):
    comps, planes, sectors, radial = flow_state.shape
    tile = (SEG, LANES)
    half_turn = lax.axis_size("az") // 2
    local_rows = canard_table.shape[1]
    field = (comps, planes, sectors, radial)
    edges = [(comps, sectors, radial)] * 2 + [(comps, planes, radial)] * 2

    ints = jax.ShapeDtypeStruct(canard_index.shape, jnp.int32)
    u, rows, coef, mask, place, cst, *first_edges = call(
        prelude_kernel,
        (flow_state, canard_table.transpose(0, 2, 1, 3), radial_coef, blanking, canard_index, coupling, upwind_split),
        [
            field,
            (local_rows, comps * radial),
            (planes, sectors, radial),
            (LANES, radial),
            ints,
            (2, NN) + tile,
        ]
        + edges,
        [
            (comps, local_rows, radial),
            pltpu.VMEM((planes, sectors, radial), jnp.int32),
            pltpu.VMEM(canard_index.shape, jnp.int32),
            pltpu.SMEM((N, N), F32),
            pltpu.SMEM((N,), F32),
            pltpu.SemaphoreType.DMA((7,)),
        ],
        1.2,
        hbm=True,
    )
    bits = doubling_bits()
    swapped = xor_swap(rows, bits[0])
    first_halos = halos(*first_edges)
    rows = append(rows, swapped)
    mb, mf, scal, sd = call(
        factor_kernel,
        (after(coef, rows), mask, cst),
        [
            (HALF + 3, 3 * NN) + tile,
            (HALF + 2, 2 * NN) + tile,
            (HALF, 3) + tile,
            (JOINT_ROWS, LANES),
        ],
        [(radial, LANES), (radial, LANES), (2 * HALF + 1,) + tile, (4, NN) + tile],
        3.2,
    )
    for i, bit in enumerate(bits[1:-1]):
        swapped = xor_swap(rows, bit)
        if i == 0:
            swapped = after(swapped, sd)
        elif i == 1:
            mb, mf, sd = call(
                factor_rest_kernel,
                (after(mb, rows), mf, sd),
                [mb.shape, mf.shape, sd.shape],
                [],
                3.0,
                aliases={0: 0, 1: 1, 2: 2},
            )
            swapped = after(swapped, sd, *first_halos[:2])
        else:
            swapped = after(swapped, *first_halos[2:])
        rows = append(rows, swapped)
    others = xor_swap(rows, bits[-1])
    fwd_outs = [(HALF + 3, N) + tile, (HALF, N) + tile]
    rhs_scratch = [(N, radial, LANES)]
    back_scratch = [(HALF + 1, N) + tile, (N, radial, LANES)]

    e1, o1, joint = call(
        forward_first_kernel,
        (u, *first_halos, mask, place, rows, others, mf, scal, cst, sd),
        fwd_outs + [(JOINT_ROWS, LANES)],
        rhs_scratch,
        2.4,
    )
    other_joint = shifted(joint, "az", half_turn, True)
    first, *second_edges, axis_inverse = call(
        backward_first_kernel,
        (joint, other_joint, mb, scal, cst, e1, o1),
        [field] + edges + [(2 * NN, LANES)],
        back_scratch,
        2.0,
    )
    second_halos = halos(*second_edges)
    e2, o2, y2 = call(
        forward_second_kernel,
        (first, *second_halos, mask, mf, scal, cst),
        fwd_outs + [tile],
        rhs_scratch,
        2.0,
    )
    other_y2 = shifted(y2, "az", half_turn, True)
    (update,) = call(
        backward_second_kernel,
        (y2, other_y2, axis_inverse, mb, scal, cst, e2, o2, first),
        [field],
        back_scratch,
        2.0,
    )
    return update


def solution(mesh):
    return jax.shard_map(
        per_device,
        mesh=mesh,
        in_specs=(
            P(None, "ax", "az", None),
            P("ax", "az", None),
            P("ax", "az", None),
            P("ax", "az"),
            P("ax", "az", None, None),
            P(),
            P(),
        ),
        out_specs=P(None, "ax", "az", None),
        check_vma=False,
    )
```

```python
import jax
import jax.numpy as jnp
from jax import lax
from jax.experimental import pallas as pl
from jax.experimental.pallas import tpu as pltpu
from jax.sharding import PartitionSpec as P

N = 5
NN = 25
SEG = 8
LANES = 128
HALF = 16
VMEM_LIMIT = 16 * 1024 * 1024
F32 = jnp.float32
STEPS = [(s * (2 * i + 1), s) for s in (1, 2, 4, 8) for i in range(8 // s)]


def up(x, s):
    return pltpu.roll(x, SEG - s, 0)


def down(x, s):
    return pltpu.roll(x, s, 0)


def splat_consts(coupling_ref, upwind_ref):
    shape = (SEG, LANES)
    p = [[jnp.full(shape, coupling_ref[i, j], F32) for j in range(N)] for i in range(N)]
    w = [jnp.full(shape, upwind_ref[i], F32) for i in range(N)]
    a = [[p[i][j] + w[i] if i == j else p[i][j] for j in range(N)] for i in range(N)]
    b = [[(1.0 - w[i]) - p[j][i] if i == j else -p[j][i] for j in range(N)] for i in range(N)]
    return a, b


def dot_row(row, cols, j):
    acc = row[0] * cols[0][j]
    for k in range(1, N):
        acc = acc + row[k] * cols[k][j]
    return acc


def mat_mul(x, y):
    return [[dot_row(x[i], y, j) for j in range(N)] for i in range(N)]


def mat_vec(x, v):
    out = []
    for i in range(N):
        acc = x[i][0] * v[0]
        for k in range(1, N):
            acc = acc + x[i][k] * v[k]
        out.append(acc)
    return out


def invert(matrix):
    m = [list(row) for row in matrix]
    for p in range(N):
        piv = 1.0 / m[p][p]
        m[p] = [piv if j == p else m[p][j] * piv for j in range(N)]
        for i in range(N):
            if i != p:
                f = m[i][p]
                m[i] = [-(f * piv) if j == p else m[i][j] - f * m[p][j] for j in range(N)]
    return m


def load_mat(ref, slot, base):
    return [[ref[slot, base + i * N + j] for j in range(N)] for i in range(N)]


def load_row(ref, slot, base, i):
    return [ref[slot, base + i * N + j] for j in range(N)]


def store_mat(ref, slot, base, mat):
    for i in range(N):
        for j in range(N):
            ref[slot, base + i * N + j] = mat[i][j]


def strided(ref, k):
    return ref[pl.ds(k, SEG, stride=2 * HALF), :]


def slot_of(q):
    return q + 2


LAM_ROW, MASK_ROW, VEC_ROW, JOINT_ROWS = NN, NN + 1, NN + 2, 32
D0, OUT0, IN0 = 0, NN, 2 * NN
LO0, LI0 = 0, NN


def is_even(axis):
    return lax.axis_index(axis) % 2 == 0


def pack_edges(field, v, za, zb, ta, tb):
    _, planes, sectors, _ = field.shape
    z_up, t_up = is_even("ax"), is_even("az")
    za[v] = field[v, jnp.where(z_up, planes - 1, 0)]
    zb[v] = field[v, jnp.where(z_up, 0, planes - 1)]
    for z in range(planes):
        first, last = field[v, z, pl.ds(0, 1), :], field[v, z, pl.ds(sectors - 1, 1), :]
        ta[v, pl.ds(z, 1), :] = jnp.where(t_up, last, first)
        tb[v, pl.ds(z, 1), :] = jnp.where(t_up, first, last)


def prelude_kernel(
    flow, coef, blank, index, coup, upw,
    u, coef_ref, mask_ref, place, cst, za, zb, ta, tb,
    blank_ref, index_ref, coup_ref, upw_ref, sem,
):
    pairs = (
        (flow, u),
        (coup, coup_ref),
        (upw, upw_ref),
        (index, index_ref),
        (blank, blank_ref),
        (coef, coef_ref),
    )
    copies = [pltpu.make_async_copy(src, dst, sem.at[i]) for i, (src, dst) in enumerate(pairs)]
    for copy in copies:
        copy.start()
    _, planes, sectors, radial = u.shape
    copies[1].wait()
    copies[2].wait()
    a, b = splat_consts(coup_ref, upw_ref)
    store_mat(cst, 0, 0, a)
    store_mat(cst, 1, 0, b)
    copies[3].wait()
    place[...] = table_place(index_ref[...])
    copies[4].wait()
    mask_ref[...] = blank_ref[...].astype(F32).reshape(planes * sectors, radial)
    copies[5].wait()
    copies[0].wait()
    for v in range(N):
        pack_edges(u, v, za, zb, ta, tb)


def append_kernel(low, high, out):
    half = low.shape[1]
    out[:, pl.ds(0, half), :] = low[...]
    out[:, pl.ds(half, half), :] = high[...]


def factor_kernel(coef_ref, mask_ref, cst, m1, f1, scal, sd, mask_t, lam_t, face, pw):
    mask = mask_ref[...]
    lam = coef_ref[...].reshape(LANES, 2 * HALF * SEG) * mask
    lam_t[...] = lam.T
    mask_t[...] = mask.T
    a, b = load_mat(cst, 0, 0), load_mat(cst, 1, 0)
    for which, mat in enumerate((mat_mul(a, a), mat_mul(b, b), mat_mul(a, b), mat_mul(b, a))):
        store_mat(pw, which, 0, mat)

    sub = lax.broadcasted_iota(jnp.int32, (SEG, LANES), 0)
    first_lam, first_mask = strided(lam_t, 0), strided(mask_t, 0)
    lam_k, mask_k = first_lam, first_mask
    for k in range(2 * HALF):
        if k < 2 * HALF - 1:
            lam_n, mask_n = strided(lam_t, k + 1), strided(mask_t, k + 1)
            f = 0.5 * (lam_k * mask_n + lam_n * mask_k)
        else:
            lam_n, mask_n = up(first_lam, 1), up(first_mask, 1)
            f = jnp.where(sub == SEG - 1, 0.0, 0.5 * (lam_k * mask_n + lam_n * mask_k))
        face[k + 1] = f
        lam_k, mask_k = lam_n, mask_n
    face[0] = down(face[2 * HALF], 1)

    def build_odd(m, c):
        fl, fr = face[2 * m + 1], face[2 * m + 2]
        scal[m, 0] = 1.0 / (1.0 + 0.5 * (fl + fr))
        scal[m, 1] = fl
        scal[m, 2] = fr
        return c

    lax.fori_loop(0, HALF, build_odd, 0)

    def build_even(p, c):
        prev = jnp.where(p == 0, HALF - 1, p - 1)
        inv, fl, fr = scal[p, 0], scal[p, 1], scal[p, 2]
        inv_p, fl_p, fr_p = scal[prev, 0], scal[prev, 1], scal[prev, 2]
        beta = fr_p * fr_p * inv_p
        delta = fr_p * fl_p * inv_p
        beta = jnp.where(p == 0, down(beta, 1), beta)
        alpha = fl * fl * inv
        gamma = fl * fr * inv
        d = 1.0 + 0.5 * (face[2 * p] + face[2 * p + 1])
        for i in range(N):
            for j in range(N):
                e = i * N + j
                val = -(alpha * pw[2, e] + beta * pw[3, e])
                m1[p, D0 + e] = d + val if i == j else val
                m1[p, OUT0 + e] = gamma * pw[0, e]
                m1[p, IN0 + e] = delta * pw[1, e]
        return c

    lax.fori_loop(0, HALF, build_even, 0)
    last = scal[HALF - 1, 1] * scal[HALF - 1, 2] * scal[HALF - 1, 0]
    for e in range(NN):
        m1[HALF, D0 + e] = jnp.zeros((SEG, LANES), F32)
        m1[HALF, OUT0 + e] = jnp.zeros((SEG, LANES), F32)
        m1[HALF, IN0 + e] = last * pw[1, e]

    sd[...] = jnp.zeros((JOINT_ROWS, LANES), F32)
    sd[pl.ds(LAM_ROW, 1), :] = first_lam[0:1]
    sd[pl.ds(MASK_ROW, 1), :] = first_mask[0:1]

    def step(i, c):
        eliminate(m1, f1, 1, 2 * i + 1, i)
        return c

    lax.fori_loop(0, HALF // 2, step, 0)


def eliminate(mb, mf, s, sm, fm):
    sp, sq = sm - s, sm + s
    di = invert(load_mat(mb, sm, D0))
    store_mat(mb, sm, D0, di)
    for i in range(N):
        row = load_row(mb, sp, OUT0, i)
        for j in range(N):
            mf[fm, LO0 + i * N + j] = dot_row(row, di, j)
        row = load_row(mb, sq, IN0, i)
        for j in range(N):
            mf[fm, LI0 + i * N + j] = dot_row(row, di, j)
    in_m = load_mat(mb, sm, IN0)
    for i in range(N):
        row = load_row(mf, fm, LO0, i)
        for j in range(N):
            e = i * N + j
            mb[sp, D0 + e] = mb[sp, D0 + e] - dot_row(row, in_m, j)
        row = load_row(mf, fm, LI0, i)
        for j in range(N):
            mb[sq, IN0 + i * N + j] = dot_row(row, in_m, j)
    out_m = load_mat(mb, sm, OUT0)
    for i in range(N):
        row = load_row(mf, fm, LI0, i)
        for j in range(N):
            e = i * N + j
            mb[sq, D0 + e] = mb[sq, D0 + e] - dot_row(row, out_m, j)
        row = load_row(mf, fm, LO0, i)
        for j in range(N):
            mb[sp, OUT0 + i * N + j] = dot_row(row, out_m, j)


def factor_rest_kernel(m1, sd_in, mb, mf, sd):
    def fetch(q, c):
        for e in range(3 * NN):
            mb[slot_of(q), e] = m1[2 * q, e]
        return c

    lax.fori_loop(0, HALF // 2 + 1, fetch, 0)

    def step(it, c):
        s = jnp.where(it < 4, 1, jnp.where(it < 6, 2, 4))
        first = jnp.where(it < 4, 0, jnp.where(it < 6, 4, 6))
        q = s * (2 * (it - first) + 1)
        eliminate(mb, mf, s, slot_of(q), slot_of(q))
        return c

    lax.fori_loop(0, HALF // 2 - 1, step, 0)
    sd[...] = sd_in[...]
    s0, s16 = slot_of(0), slot_of(HALF // 2)
    for e in range(NN):
        mb[0, D0 + e] = mb[s0, D0 + e] + down(mb[s16, D0 + e], 1)
        mb[0, OUT0 + e] = mb[s0, OUT0 + e]
        mb[0, IN0 + e] = down(mb[s16, IN0 + e], 1)
    for level, s in enumerate((1, 2, 4)):
        d = load_mat(mb, level, D0)
        di = invert(d)
        store_mat(mb, level, D0, di)
        di_up = [[up(di[i][j], s) for j in range(N)] for i in range(N)]
        for i in range(N):
            row = load_row(mb, level, OUT0, i)
            for j in range(N):
                mf[level, LO0 + i * N + j] = dot_row(row, di_up, j)
        di_down = [[down(di[i][j], s) for j in range(N)] for i in range(N)]
        for i in range(N):
            row = load_row(mb, level, IN0, i)
            for j in range(N):
                mf[level, LI0 + i * N + j] = dot_row(row, di_down, j)
        in_up = [[up(mb[level, IN0 + i * N + j], s) for j in range(N)] for i in range(N)]
        acc = []
        for i in range(N):
            row = load_row(mf, level, LO0, i)
            acc.append([d[i][j] - dot_row(row, in_up, j) for j in range(N)])
        out_down = [[down(mb[level, OUT0 + i * N + j], s) for j in range(N)] for i in range(N)]
        for i in range(N):
            row = load_row(mf, level, LI0, i)
            for j in range(N):
                val = acc[i][j] - dot_row(row, out_down, j)
                if level < 2:
                    mb[level + 1, D0 + i * N + j] = val
                else:
                    sd[pl.ds(i * N + j, 1), :] = val[0:1]
        if level < 2:
            out_up = [[up(mb[level, OUT0 + i * N + j], s) for j in range(N)] for i in range(N)]
            for i in range(N):
                row = load_row(mf, level, LO0, i)
                for j in range(N):
                    mb[level + 1, OUT0 + i * N + j] = dot_row(row, out_up, j)
            in_down = [[down(mb[level, IN0 + i * N + j], s) for j in range(N)] for i in range(N)]
            for i in range(N):
                row = load_row(mf, level, LI0, i)
                for j in range(N):
                    mb[level + 1, IN0 + i * N + j] = dot_row(row, in_down, j)


def join(own_ref, other_ref, j_ref):
    lam, mask = own_ref[pl.ds(LAM_ROW, 1), :], own_ref[pl.ds(MASK_ROW, 1), :]
    other_lam, other_mask = other_ref[pl.ds(LAM_ROW, 1), :], other_ref[pl.ds(MASK_ROW, 1), :]
    c = 0.25 * (lam * other_mask + other_lam * mask)

    def total(ref):
        mat = [[ref[pl.ds(i * N + j, 1), :] for j in range(N)] for i in range(N)]
        return [[mat[i][j] + c if i == j else mat[i][j] for j in range(N)] for i in range(N)]

    own, inv_other = total(own_ref), invert(total(other_ref))
    schur = [[own[i][j] - c * (c * inv_other[i][j]) for j in range(N)] for i in range(N)]
    j1 = invert(schur)
    j2 = mat_mul(j1, inv_other)
    for i in range(N):
        for j in range(N):
            j_ref[pl.ds(i * N + j, 1), :] = j1[i][j]
            j_ref[pl.ds(NN + i * N + j, 1), :] = c * j2[i][j]


def stencil_block(u, v, z, planes, za, zb, ta, tb):
    z_up, t_up = is_even("ax"), is_even("az")
    cur = u[v, z]
    rows = lax.broadcasted_iota(jnp.int32, cur.shape, 0)
    behind = u[v, z - 1] if z > 0 else jnp.where(z_up, zb[v], za[v])
    ahead = u[v, z + 1] if z < planes - 1 else jnp.where(z_up, za[v], zb[v])
    sectors = cur.shape[0]
    t_a, t_b = ta[v, pl.ds(z, 1), :], tb[v, pl.ds(z, 1), :]
    before_t = jnp.where(rows == 0, jnp.where(t_up, t_b, t_a), pltpu.roll(cur, 1, 0))
    after_t = jnp.where(rows == sectors - 1, jnp.where(t_up, t_a, t_b), pltpu.roll(cur, sectors - 1, 0))
    return behind + ahead + before_t + after_t - 4.0 * cur + 0.5 * (behind - ahead)


def forward_body(rhs_t, f1, f2, scal, cst, e_ref, o_ref):
    a, b = load_mat(cst, 0, 0), load_mat(cst, 1, 0)
    zero = jnp.zeros((SEG, LANES), F32)
    carry = [zero] * N
    first = None
    for m in range(HALF):
        inv, fl, fr = scal[m, 0], scal[m, 1], scal[m, 2]
        odd = [strided(rhs_t.at[v], 2 * m + 1) for v in range(N)]
        scaled = [x * inv for x in odd]
        ta = mat_vec(a, scaled)
        tb = mat_vec(b, scaled)
        for v in range(N):
            o_ref[m, v] = odd[v]
            e_ref[m, v] = strided(rhs_t.at[v], 2 * m) + carry[v] + fl * ta[v]
        carry = [fr * tb[v] for v in range(N)]
    for v in range(N):
        e_ref[0, v] = e_ref[0, v] + down(carry[v], 1)
        e_ref[HALF, v] = zero
    for m, s in STEPS:
        vec = [e_ref[m, v] for v in range(N)]
        mf, slot = (f1, m // 2) if s == 1 else (f2, slot_of(m // 2))
        lo = mat_vec(load_mat(mf, slot, LO0), vec)
        li = mat_vec(load_mat(mf, slot, LI0), vec)
        for v in range(N):
            e_ref[m - s, v] = e_ref[m - s, v] + lo[v]
            e_ref[m + s, v] = e_ref[m + s, v] + li[v]
    cur = [e_ref[0, v] + down(e_ref[HALF, v], 1) for v in range(N)]
    for level, s in enumerate((1, 2, 4)):
        for v in range(N):
            e_ref[HALF + 1 + level, v] = cur[v]
        lo = mat_vec(load_mat(f2, level, LO0), [up(x, s) for x in cur])
        li = mat_vec(load_mat(f2, level, LI0), [down(x, s) for x in cur])
        cur = [cur[v] + lo[v] + li[v] for v in range(N)]
    return [cur[v][0:1] for v in range(N)]


def doubling_bits():
    return [bit for bit in (24, 8, 4, 2, 1) if bit < lax.axis_size("az")]


def table_place(index):
    apart = lax.shift_right_logical(index, 2) ^ lax.axis_index("az")
    block = jnp.zeros_like(apart)
    for i, bit in enumerate(doubling_bits()):
        used = (apart & (1 << (bit.bit_length() - 1))) != 0
        apart = jnp.where(used, apart ^ bit, apart)
        block = block | (jnp.where(used, 1, 0) << i)
    return block * 4 + (index & 3)


def one_hot(place, start, count):
    planes, sectors = place.shape
    rows = start + lax.broadcasted_iota(jnp.int32, (count, sectors), 0)
    hot = [jnp.where(rows == place[pl.ds(z, 1), :], 1.0, 0.0) for z in range(planes)]
    return jnp.concatenate(hot, axis=1)


def pick(rows, hot):
    return lax.dot_general(
        rows,
        hot,
        (((0,), (0,)), ((), ())),
        precision=lax.Precision.HIGHEST,
        preferred_element_type=F32,
    )


def rhs_kernel(u, za, zb, ta, tb, mask_ref, mask_t, place, low, rhs_t):
    planes = u.shape[1]
    mask = mask_ref[...]
    hot = one_hot(place, 0, low.shape[1])
    for v in range(N):
        blocks = [stencil_block(u, v, z, planes, za, zb, ta, tb) for z in range(planes)]
        rhs_t[v] = (mask * jnp.concatenate(blocks, axis=0)).T + mask_t[...] * pick(low[v], hot)


def forward_first_kernel(
    rhs_in, mask_t, place, high, f1, f2, scal, cst, sd, e_ref, o_ref, joint, rhs_t
):
    hot = one_hot(place, high.shape[1], high.shape[1])
    for v in range(N):
        rhs_t[v] = rhs_in[v] + mask_t[...] * pick(high[v], hot)
    reduced = forward_body(rhs_t, f1, f2, scal, cst, e_ref, o_ref)
    joint[...] = sd[...]
    for v in range(N):
        joint[pl.ds(VEC_ROW + v, 1), :] = reduced[v]


def forward_second_kernel(
    u, za, zb, ta, tb, mask_ref, f1, f2, scal, cst, e_ref, o_ref, y_ref, rhs_t
):
    planes = u.shape[1]
    mask = mask_ref[...]
    for v in range(N):
        blocks = [stencil_block(u, v, z, planes, za, zb, ta, tb) for z in range(planes)]
        rhs_t[v] = (mask * jnp.concatenate(blocks, axis=0)).T
    reduced = forward_body(rhs_t, f1, f2, scal, cst, e_ref, o_ref)
    y_ref[...] = jnp.zeros((SEG, LANES), F32)
    for v in range(N):
        y_ref[pl.ds(v, 1), :] = reduced[v]


def backward_body(own, other, j_ref, m1, m2, scal, cst, e_ref, o_ref, x_ref, x_t):
    a, b = load_mat(cst, 0, 0), load_mat(cst, 1, 0)
    sub = lax.broadcasted_iota(jnp.int32, (SEG, LANES), 0)
    cur = []
    for i in range(N):
        acc = j_ref[pl.ds(i * N, 1), :] * own[0]
        for k in range(N):
            if k > 0:
                acc = acc + j_ref[pl.ds(i * N + k, 1), :] * own[k]
            acc = acc + j_ref[pl.ds(NN + i * N + k, 1), :] * other[k]
        cur.append(jnp.broadcast_to(acc, (SEG, LANES)))

    def recover(mb, slot, rhs, high, low):
        o = mat_vec(load_mat(mb, slot, OUT0), high)
        i = mat_vec(load_mat(mb, slot, IN0), low)
        total = [e_ref[rhs, v] + o[v] + i[v] for v in range(N)]
        return mat_vec(load_mat(mb, slot, D0), total)

    for level, s in ((2, 4), (1, 2), (0, 1)):
        new = recover(m2, level, HALF + 1 + level, [up(x, s) for x in cur], [down(x, s) for x in cur])
        cur = [jnp.where(sub % (2 * s) == s, new[v], cur[v]) for v in range(N)]
    for v in range(N):
        x_ref[0, v] = cur[v]
        x_ref[HALF, v] = up(cur[v], 1)
    for m, s in reversed(STEPS):
        mb, slot = (m1, m) if s == 1 else (m2, slot_of(m // 2))
        new = recover(
            mb, slot, m, [x_ref[m + s, v] for v in range(N)], [x_ref[m - s, v] for v in range(N)]
        )
        for v in range(N):
            x_ref[m, v] = new[v]
    low = [x_ref[0, v] for v in range(N)]
    for m in range(HALF):
        inv, fl, fr = scal[m, 0], scal[m, 1], scal[m, 2]
        high = [x_ref[m + 1, v] for v in range(N)]
        ta = mat_vec(a, high)
        tb = mat_vec(b, low)
        for v in range(N):
            odd = inv * (o_ref[m, v] + fr * ta[v] + fl * tb[v])
            x_t.at[v][pl.ds(2 * m, SEG, stride=2 * HALF), :] = low[v]
            x_t.at[v][pl.ds(2 * m + 1, SEG, stride=2 * HALF), :] = odd
        low = high


def backward_first_kernel(
    joint, other_joint, m1, m2, scal, cst, e_ref, o_ref,
    out, za, zb, ta, tb, j_ref, x_ref, x_t,
):
    join(joint, other_joint, j_ref)
    own = [joint[pl.ds(VEC_ROW + v, 1), :] for v in range(N)]
    other = [other_joint[pl.ds(VEC_ROW + v, 1), :] for v in range(N)]
    backward_body(own, other, j_ref, m1, m2, scal, cst, e_ref, o_ref, x_ref, x_t)
    _, planes, sectors, radial = out.shape
    for v in range(N):
        out[v] = x_t[v].T.reshape(planes, sectors, radial)
        pack_edges(out, v, za, zb, ta, tb)


def backward_second_kernel(
    y_own, y_other, j_ref, m1, m2, scal, cst, e_ref, o_ref, first, out, x_ref, x_t
):
    own = [y_own[pl.ds(v, 1), :] for v in range(N)]
    other = [y_other[pl.ds(v, 1), :] for v in range(N)]
    backward_body(own, other, j_ref, m1, m2, scal, cst, e_ref, o_ref, x_ref, x_t)
    _, planes, sectors, radial = out.shape
    for v in range(N):
        out[v] = first[v] + 0.5 * x_t[v].T.reshape(planes, sectors, radial)


def call(kernel, inputs, outs, scratch, us, hbm=False, aliases=None):
    vmem = pl.BlockSpec(memory_space=pltpu.VMEM)
    if hbm:
        inputs = [pltpu.with_memory_space_constraint(x, pltpu.HBM) for x in inputs]
    in_spec = pl.BlockSpec(memory_space=pltpu.HBM) if hbm else vmem
    out_shape = [s if isinstance(s, jax.ShapeDtypeStruct) else jax.ShapeDtypeStruct(s, F32) for s in outs]
    return pl.pallas_call(
        kernel,
        out_shape=out_shape,
        in_specs=[in_spec] * len(inputs),
        out_specs=[vmem] * len(outs),
        scratch_shapes=[pltpu.VMEM(s, F32) if isinstance(s, tuple) else s for s in scratch],
        input_output_aliases=aliases or {},
        compiler_params=pltpu.CompilerParams(vmem_limit_bytes=VMEM_LIMIT),
        cost_estimate=pl.CostEstimate(
            flops=int(us * 1e9), bytes_accessed=int(us * 3e6), transcendentals=0
        ),
    )(*inputs)


def swapped_along(x, axis, odd, wrap):
    size = lax.axis_size(axis)
    pairs = []
    for i in range(odd, size, 2):
        if wrap or i + 1 < size:
            j = (i + 1) % size
            pairs += [(i, j), (j, i)]
    return lax.ppermute(x, axis, pairs)


def halos(za, zb, ta, tb):
    return (
        swapped_along(za, "ax", 0, False),
        swapped_along(zb, "ax", 1, False),
        swapped_along(ta, "az", 0, True),
        swapped_along(tb, "az", 1, True),
    )


def xor_swap(x, bit):
    return lax.ppermute(x, "az", [(i, i ^ bit) for i in range(lax.axis_size("az"))])


def append(low, high):
    (both,) = call(append_kernel, (low, high), [(N, 2 * low.shape[1], low.shape[2])], [], 0.2)
    return both


def after(x, *others):
    return lax.optimization_barrier((x, *others))[0]


def per_device(
    flow_state, radial_coef, blanking, canard_index, canard_table, coupling, upwind_split
):
    comps, planes, sectors, radial = flow_state.shape
    tile = (SEG, LANES)
    half_turn = lax.axis_size("az") // 2
    field = (comps, planes, sectors, radial)
    edges = [(comps, sectors, radial)] * 2 + [(comps, planes, radial)] * 2
    columns = (comps, radial, LANES)
    bits = doubling_bits()

    rows = canard_table[0].transpose(1, 0, 2)
    got = xor_swap(rows, bits[0])
    u, coef, mask, place, cst, *first_edges = call(
        prelude_kernel,
        (flow_state, radial_coef, blanking, canard_index, coupling, upwind_split),
        [
            field,
            (planes, sectors, radial),
            (LANES, radial),
            jax.ShapeDtypeStruct(canard_index.shape, jnp.int32),
            (2, NN) + tile,
        ]
        + edges,
        [
            pltpu.VMEM((planes, sectors, radial), jnp.int32),
            pltpu.VMEM(canard_index.shape, jnp.int32),
            pltpu.SMEM((N, N), F32),
            pltpu.SMEM((N,), F32),
            pltpu.SemaphoreType.DMA((6,)),
        ],
        1.2,
        hbm=True,
    )
    first_halos = halos(*first_edges)
    rows = append(rows, after(got, cst))
    done = {}

    def factor(rows, got):
        done["one"] = call(
            factor_kernel,
            (after(coef, rows), mask, cst),
            [
                (HALF + 1, 3 * NN) + tile,
                (HALF // 2, 2 * NN) + tile,
                (HALF, 3) + tile,
                (JOINT_ROWS, LANES),
                (radial, LANES),
            ],
            [(radial, LANES), (2 * HALF + 1,) + tile, (4, NN) + tile],
            3.2,
        )
        return after(got, done["one"][3])

    def factor_rest(rows, got):
        done["rest"] = call(
            factor_rest_kernel,
            (after(done["one"][0], rows), done["one"][3]),
            [
                (HALF // 2 + 3, 3 * NN) + tile,
                (HALF // 2 + 2, 2 * NN) + tile,
                (JOINT_ROWS, LANES),
            ],
            [],
            3.0,
        )
        return after(got, done["rest"][2], *first_halos[:2])

    def sector_halos(rows, got):
        return after(got, *first_halos[2:])

    fillers = [factor, factor_rest, sector_halos]
    for i, bit in enumerate(bits[1:-1]):
        rows = append(rows, fillers[i](rows, xor_swap(rows, bit)))
    for filler in fillers[len(bits) - 2 :]:
        rows = filler(rows, rows)
    others = xor_swap(rows, bits[-1])
    m1, f1, scal, _, mask_t = done["one"]
    m2, f2, sd = done["rest"]
    (rhs,) = call(
        rhs_kernel, (u, *first_halos, mask, mask_t, place, rows), [columns], [], 1.3
    )
    others = after(others, rhs)

    fwd_outs = [(HALF + 4, N) + tile, (HALF, N) + tile]
    back_scratch = [(HALF + 1, N) + tile, columns]
    e1, o1, joint = call(
        forward_first_kernel,
        (rhs, mask_t, place, others, f1, f2, scal, cst, sd),
        fwd_outs + [(JOINT_ROWS, LANES)],
        [columns],
        1.2,
    )
    other_joint = xor_swap(joint, half_turn)
    first, *second_edges, axis_inverse = call(
        backward_first_kernel,
        (joint, other_joint, m1, m2, scal, cst, e1, o1),
        [field] + edges + [(2 * NN, LANES)],
        back_scratch,
        1.3,
    )
    second_halos = halos(*second_edges)
    e2, o2, y2 = call(
        forward_second_kernel,
        (first, *second_halos, mask, f1, f2, scal, cst),
        fwd_outs + [tile],
        [columns],
        1.3,
    )
    other_y2 = xor_swap(y2, half_turn)
    (update,) = call(
        backward_second_kernel,
        (y2, other_y2, axis_inverse, m1, m2, scal, cst, e2, o2, first),
        [field],
        back_scratch,
        2.0,
    )
    return update


def solution(mesh):
    return jax.shard_map(
        per_device,
        mesh=mesh,
        in_specs=(
            P(None, "ax", "az", None),
            P("ax", "az", None),
            P("ax", "az", None),
            P("ax", "az"),
            P("ax", "az", None, None),
            P(),
            P(),
        ),
        out_specs=P(None, "ax", "az", None),
        check_vma=False,
    )
```

```python
import jax
import jax.numpy as jnp
from jax import lax
from jax.experimental import pallas as pl
from jax.experimental.pallas import tpu as pltpu
from jax.sharding import PartitionSpec as P

N = 5
NN = 25
SEG = 8
LANES = 128
HALF = 16
VMEM_LIMIT = 16 * 1024 * 1024
F32 = jnp.float32
STEPS = [(s * (2 * i + 1), s) for s in (1, 2, 4, 8) for i in range(8 // s)]


def up(x, s):
    return pltpu.roll(x, SEG - s, 0)


def down(x, s):
    return pltpu.roll(x, s, 0)


def splat_consts(coupling_ref, upwind_ref):
    shape = (SEG, LANES)
    p = [[jnp.full(shape, coupling_ref[i, j], F32) for j in range(N)] for i in range(N)]
    w = [jnp.full(shape, upwind_ref[i], F32) for i in range(N)]
    a = [[p[i][j] + w[i] if i == j else p[i][j] for j in range(N)] for i in range(N)]
    b = [[(1.0 - w[i]) - p[j][i] if i == j else -p[j][i] for j in range(N)] for i in range(N)]
    return a, b


def dot_row(row, cols, j):
    acc = row[0] * cols[0][j]
    for k in range(1, N):
        acc = acc + row[k] * cols[k][j]
    return acc


def mat_mul(x, y):
    return [[dot_row(x[i], y, j) for j in range(N)] for i in range(N)]


def mat_vec(x, v):
    out = []
    for i in range(N):
        acc = x[i][0] * v[0]
        for k in range(1, N):
            acc = acc + x[i][k] * v[k]
        out.append(acc)
    return out


def invert(matrix):
    m = [list(row) for row in matrix]
    for p in range(N):
        piv = 1.0 / m[p][p]
        m[p] = [piv if j == p else m[p][j] * piv for j in range(N)]
        for i in range(N):
            if i != p:
                f = m[i][p]
                m[i] = [-(f * piv) if j == p else m[i][j] - f * m[p][j] for j in range(N)]
    return m


def load_mat(ref, slot, base):
    return [[ref[slot, base + i * N + j] for j in range(N)] for i in range(N)]


def load_row(ref, slot, base, i):
    return [ref[slot, base + i * N + j] for j in range(N)]


def store_mat(ref, slot, base, mat):
    for i in range(N):
        for j in range(N):
            ref[slot, base + i * N + j] = mat[i][j]


def strided(ref, k):
    return ref[pl.ds(k, SEG, stride=2 * HALF), :]


def slot_of(q):
    return q + 2


LAM_ROW, MASK_ROW, VEC_ROW, JOINT_ROWS = NN, NN + 1, NN + 2, 32
D0, OUT0, IN0 = 0, NN, 2 * NN
LO0, LI0 = 0, NN


def is_even(axis):
    return lax.axis_index(axis) % 2 == 0


def pack_far_sector(field, v, tb):
    _, planes, sectors, _ = field.shape
    up = is_even("az")
    for z in range(planes):
        first, last = field[v, z, pl.ds(0, 1), :], field[v, z, pl.ds(sectors - 1, 1), :]
        tb[v, pl.ds(z, 1), :] = jnp.where(up, first, last)


def pack_edges(field, v, za, zb, ta):
    _, planes, sectors, _ = field.shape
    z_up, t_up = is_even("ax"), is_even("az")
    za[v] = field[v, jnp.where(z_up, planes - 1, 0)]
    zb[v] = field[v, jnp.where(z_up, 0, planes - 1)]
    for z in range(planes):
        first, last = field[v, z, pl.ds(0, 1), :], field[v, z, pl.ds(sectors - 1, 1), :]
        ta[v, pl.ds(z, 1), :] = jnp.where(t_up, last, first)


def prelude_kernel(
    flow, coef, blank, index, coup, upw,
    u, coef_ref, mask_ref, place, cst, za, zb, ta, tb,
    blank_ref, index_ref, coup_ref, upw_ref, sem,
):
    pairs = (
        (flow, u),
        (coup, coup_ref),
        (upw, upw_ref),
        (index, index_ref),
        (blank, blank_ref),
        (coef, coef_ref),
    )
    copies = [pltpu.make_async_copy(src, dst, sem.at[i]) for i, (src, dst) in enumerate(pairs)]
    for copy in copies:
        copy.start()
    _, planes, sectors, radial = u.shape
    copies[1].wait()
    copies[2].wait()
    a, b = splat_consts(coup_ref, upw_ref)
    store_mat(cst, 0, 0, a)
    store_mat(cst, 1, 0, b)
    copies[3].wait()
    place[...] = table_place(index_ref[...])
    copies[4].wait()
    mask_ref[...] = blank_ref[...].astype(F32).reshape(planes * sectors, radial)
    copies[5].wait()
    copies[0].wait()
    for v in range(N):
        pack_edges(u, v, za, zb, ta)
        pack_far_sector(u, v, tb)


def append_kernel(low, high, out):
    half = low.shape[1]
    out[:, pl.ds(0, half), :] = low[...]
    out[:, pl.ds(half, half), :] = high[...]


def factor_kernel(coef_ref, mask_ref, cst, m1, f1, scal, sd, mask_t, lam_t, face, pw):
    mask = mask_ref[...]
    lam = coef_ref[...].reshape(LANES, 2 * HALF * SEG) * mask
    lam_t[...] = lam.T
    mask_t[...] = mask.T
    a, b = load_mat(cst, 0, 0), load_mat(cst, 1, 0)
    for which, mat in enumerate((mat_mul(a, a), mat_mul(b, b), mat_mul(a, b), mat_mul(b, a))):
        store_mat(pw, which, 0, mat)

    sub = lax.broadcasted_iota(jnp.int32, (SEG, LANES), 0)
    first_lam, first_mask = strided(lam_t, 0), strided(mask_t, 0)
    lam_k, mask_k = first_lam, first_mask
    for k in range(2 * HALF):
        if k < 2 * HALF - 1:
            lam_n, mask_n = strided(lam_t, k + 1), strided(mask_t, k + 1)
            f = 0.5 * (lam_k * mask_n + lam_n * mask_k)
        else:
            lam_n, mask_n = up(first_lam, 1), up(first_mask, 1)
            f = jnp.where(sub == SEG - 1, 0.0, 0.5 * (lam_k * mask_n + lam_n * mask_k))
        face[k + 1] = f
        lam_k, mask_k = lam_n, mask_n
    face[0] = down(face[2 * HALF], 1)

    def build_odd(m, c):
        fl, fr = face[2 * m + 1], face[2 * m + 2]
        scal[m, 0] = 1.0 / (1.0 + 0.5 * (fl + fr))
        scal[m, 1] = fl
        scal[m, 2] = fr
        return c

    lax.fori_loop(0, HALF, build_odd, 0)

    def build_even(p, c):
        prev = jnp.where(p == 0, HALF - 1, p - 1)
        inv, fl, fr = scal[p, 0], scal[p, 1], scal[p, 2]
        inv_p, fl_p, fr_p = scal[prev, 0], scal[prev, 1], scal[prev, 2]
        beta = fr_p * fr_p * inv_p
        delta = fr_p * fl_p * inv_p
        beta = jnp.where(p == 0, down(beta, 1), beta)
        alpha = fl * fl * inv
        gamma = fl * fr * inv
        d = 1.0 + 0.5 * (face[2 * p] + face[2 * p + 1])
        for i in range(N):
            for j in range(N):
                e = i * N + j
                val = -(alpha * pw[2, e] + beta * pw[3, e])
                m1[p, D0 + e] = d + val if i == j else val
                m1[p, OUT0 + e] = gamma * pw[0, e]
                m1[p, IN0 + e] = delta * pw[1, e]
        return c

    lax.fori_loop(0, HALF, build_even, 0)
    last = scal[HALF - 1, 1] * scal[HALF - 1, 2] * scal[HALF - 1, 0]
    for e in range(NN):
        m1[HALF, D0 + e] = jnp.zeros((SEG, LANES), F32)
        m1[HALF, OUT0 + e] = jnp.zeros((SEG, LANES), F32)
        m1[HALF, IN0 + e] = last * pw[1, e]

    sd[...] = jnp.zeros((JOINT_ROWS, LANES), F32)
    sd[pl.ds(LAM_ROW, 1), :] = first_lam[0:1]
    sd[pl.ds(MASK_ROW, 1), :] = first_mask[0:1]

    def step(i, c):
        eliminate(m1, f1, 1, 2 * i + 1, i)
        return c

    lax.fori_loop(0, HALF // 2, step, 0)


def eliminate(mb, mf, s, sm, fm):
    sp, sq = sm - s, sm + s
    di = invert(load_mat(mb, sm, D0))
    store_mat(mb, sm, D0, di)
    for i in range(N):
        row = load_row(mb, sp, OUT0, i)
        for j in range(N):
            mf[fm, LO0 + i * N + j] = dot_row(row, di, j)
        row = load_row(mb, sq, IN0, i)
        for j in range(N):
            mf[fm, LI0 + i * N + j] = dot_row(row, di, j)
    in_m = load_mat(mb, sm, IN0)
    for i in range(N):
        row = load_row(mf, fm, LO0, i)
        for j in range(N):
            e = i * N + j
            mb[sp, D0 + e] = mb[sp, D0 + e] - dot_row(row, in_m, j)
        row = load_row(mf, fm, LI0, i)
        for j in range(N):
            mb[sq, IN0 + i * N + j] = dot_row(row, in_m, j)
    out_m = load_mat(mb, sm, OUT0)
    for i in range(N):
        row = load_row(mf, fm, LI0, i)
        for j in range(N):
            e = i * N + j
            mb[sq, D0 + e] = mb[sq, D0 + e] - dot_row(row, out_m, j)
        row = load_row(mf, fm, LO0, i)
        for j in range(N):
            mb[sp, OUT0 + i * N + j] = dot_row(row, out_m, j)


def factor_rest_kernel(m1, sd_in, mb, mf, sd):
    def fetch(q, c):
        for e in range(3 * NN):
            mb[slot_of(q), e] = m1[2 * q, e]
        return c

    lax.fori_loop(0, HALF // 2 + 1, fetch, 0)

    def step(it, c):
        s = jnp.where(it < 4, 1, jnp.where(it < 6, 2, 4))
        first = jnp.where(it < 4, 0, jnp.where(it < 6, 4, 6))
        q = s * (2 * (it - first) + 1)
        eliminate(mb, mf, s, slot_of(q), slot_of(q))
        return c

    lax.fori_loop(0, HALF // 2 - 1, step, 0)
    sd[...] = sd_in[...]
    s0, s16 = slot_of(0), slot_of(HALF // 2)
    for e in range(NN):
        mb[0, D0 + e] = mb[s0, D0 + e] + down(mb[s16, D0 + e], 1)
        mb[0, OUT0 + e] = mb[s0, OUT0 + e]
        mb[0, IN0 + e] = down(mb[s16, IN0 + e], 1)
    for level, s in enumerate((1, 2, 4)):
        d = load_mat(mb, level, D0)
        di = invert(d)
        store_mat(mb, level, D0, di)
        di_up = [[up(di[i][j], s) for j in range(N)] for i in range(N)]
        for i in range(N):
            row = load_row(mb, level, OUT0, i)
            for j in range(N):
                mf[level, LO0 + i * N + j] = dot_row(row, di_up, j)
        di_down = [[down(di[i][j], s) for j in range(N)] for i in range(N)]
        for i in range(N):
            row = load_row(mb, level, IN0, i)
            for j in range(N):
                mf[level, LI0 + i * N + j] = dot_row(row, di_down, j)
        in_up = [[up(mb[level, IN0 + i * N + j], s) for j in range(N)] for i in range(N)]
        acc = []
        for i in range(N):
            row = load_row(mf, level, LO0, i)
            acc.append([d[i][j] - dot_row(row, in_up, j) for j in range(N)])
        out_down = [[down(mb[level, OUT0 + i * N + j], s) for j in range(N)] for i in range(N)]
        for i in range(N):
            row = load_row(mf, level, LI0, i)
            for j in range(N):
                val = acc[i][j] - dot_row(row, out_down, j)
                if level < 2:
                    mb[level + 1, D0 + i * N + j] = val
                else:
                    sd[pl.ds(i * N + j, 1), :] = val[0:1]
        if level < 2:
            out_up = [[up(mb[level, OUT0 + i * N + j], s) for j in range(N)] for i in range(N)]
            for i in range(N):
                row = load_row(mf, level, LO0, i)
                for j in range(N):
                    mb[level + 1, OUT0 + i * N + j] = dot_row(row, out_up, j)
            in_down = [[down(mb[level, IN0 + i * N + j], s) for j in range(N)] for i in range(N)]
            for i in range(N):
                row = load_row(mf, level, LI0, i)
                for j in range(N):
                    mb[level + 1, IN0 + i * N + j] = dot_row(row, in_down, j)


def join(own_ref, other_ref, j_ref):
    lam, mask = own_ref[pl.ds(LAM_ROW, 1), :], own_ref[pl.ds(MASK_ROW, 1), :]
    other_lam, other_mask = other_ref[pl.ds(LAM_ROW, 1), :], other_ref[pl.ds(MASK_ROW, 1), :]
    c = 0.25 * (lam * other_mask + other_lam * mask)

    def total(ref):
        mat = [[ref[pl.ds(i * N + j, 1), :] for j in range(N)] for i in range(N)]
        return [[mat[i][j] + c if i == j else mat[i][j] for j in range(N)] for i in range(N)]

    own, inv_other = total(own_ref), invert(total(other_ref))
    schur = [[own[i][j] - c * (c * inv_other[i][j]) for j in range(N)] for i in range(N)]
    j1 = invert(schur)
    j2 = mat_mul(j1, inv_other)
    for i in range(N):
        for j in range(N):
            j_ref[pl.ds(i * N + j, 1), :] = j1[i][j]
            j_ref[pl.ds(NN + i * N + j, 1), :] = c * j2[i][j]


def stencil_block(u, v, z, planes, za, zb, ta, tb):
    z_up, t_up = is_even("ax"), is_even("az")
    cur = u[v, z]
    rows = lax.broadcasted_iota(jnp.int32, cur.shape, 0)
    behind = u[v, z - 1] if z > 0 else jnp.where(z_up, zb[v], za[v])
    ahead = u[v, z + 1] if z < planes - 1 else jnp.where(z_up, za[v], zb[v])
    sectors = cur.shape[0]
    t_a, t_b = ta[v, pl.ds(z, 1), :], tb[v, pl.ds(z, 1), :]
    before_t = jnp.where(rows == 0, jnp.where(t_up, t_b, t_a), pltpu.roll(cur, 1, 0))
    after_t = jnp.where(rows == sectors - 1, jnp.where(t_up, t_a, t_b), pltpu.roll(cur, sectors - 1, 0))
    return behind + ahead + before_t + after_t - 4.0 * cur + 0.5 * (behind - ahead)


def forward_body(rhs_t, f1, f2, scal, cst, e_ref, o_ref):
    a, b = load_mat(cst, 0, 0), load_mat(cst, 1, 0)
    zero = jnp.zeros((SEG, LANES), F32)
    carry = [zero] * N
    first = None
    for m in range(HALF):
        inv, fl, fr = scal[m, 0], scal[m, 1], scal[m, 2]
        odd = [strided(rhs_t.at[v], 2 * m + 1) for v in range(N)]
        scaled = [x * inv for x in odd]
        ta = mat_vec(a, scaled)
        tb = mat_vec(b, scaled)
        for v in range(N):
            o_ref[m, v] = odd[v]
            e_ref[m, v] = strided(rhs_t.at[v], 2 * m) + carry[v] + fl * ta[v]
        carry = [fr * tb[v] for v in range(N)]
    for v in range(N):
        e_ref[0, v] = e_ref[0, v] + down(carry[v], 1)
        e_ref[HALF, v] = zero
    for m, s in STEPS:
        vec = [e_ref[m, v] for v in range(N)]
        mf, slot = (f1, m // 2) if s == 1 else (f2, slot_of(m // 2))
        lo = mat_vec(load_mat(mf, slot, LO0), vec)
        li = mat_vec(load_mat(mf, slot, LI0), vec)
        for v in range(N):
            e_ref[m - s, v] = e_ref[m - s, v] + lo[v]
            e_ref[m + s, v] = e_ref[m + s, v] + li[v]
    cur = [e_ref[0, v] + down(e_ref[HALF, v], 1) for v in range(N)]
    for level, s in enumerate((1, 2, 4)):
        for v in range(N):
            e_ref[HALF + 1 + level, v] = cur[v]
        lo = mat_vec(load_mat(f2, level, LO0), [up(x, s) for x in cur])
        li = mat_vec(load_mat(f2, level, LI0), [down(x, s) for x in cur])
        cur = [cur[v] + lo[v] + li[v] for v in range(N)]
    return [cur[v][0:1] for v in range(N)]


def doubling_bits():
    return [bit for bit in (24, 8, 4, 2, 1) if bit < lax.axis_size("az")]


def table_place(index):
    apart = lax.shift_right_logical(index, 2) ^ lax.axis_index("az")
    block = jnp.zeros_like(apart)
    for i, bit in enumerate(doubling_bits()):
        used = (apart & (1 << (bit.bit_length() - 1))) != 0
        apart = jnp.where(used, apart ^ bit, apart)
        block = block | (jnp.where(used, 1, 0) << i)
    return block * 4 + (index & 3)


def one_hot(place, start, count):
    planes, sectors = place.shape
    rows = start + lax.broadcasted_iota(jnp.int32, (count, sectors), 0)
    hot = [jnp.where(rows == place[pl.ds(z, 1), :], 1.0, 0.0) for z in range(planes)]
    return jnp.concatenate(hot, axis=1)


def pick(rows, hot):
    return lax.dot_general(
        rows,
        hot,
        (((0,), (0,)), ((), ())),
        precision=lax.Precision.HIGHEST,
        preferred_element_type=F32,
    )


def rhs_kernel(u, za, zb, ta, tb, mask_ref, mask_t, place, low, rhs_t):
    planes = u.shape[1]
    mask = mask_ref[...]
    hot = one_hot(place, 0, low.shape[1])
    for v in range(N):
        blocks = [stencil_block(u, v, z, planes, za, zb, ta, tb) for z in range(planes)]
        rhs_t[v] = (mask * jnp.concatenate(blocks, axis=0)).T + mask_t[...] * pick(low[v], hot)


def forward_first_kernel(
    rhs_in, mask_t, place, high, f1, f2, scal, cst, sd, e_ref, o_ref, joint, rhs_t
):
    hot = one_hot(place, high.shape[1], high.shape[1])
    for v in range(N):
        rhs_t[v] = rhs_in[v] + mask_t[...] * pick(high[v], hot)
    reduced = forward_body(rhs_t, f1, f2, scal, cst, e_ref, o_ref)
    joint[...] = sd[...]
    for v in range(N):
        joint[pl.ds(VEC_ROW + v, 1), :] = reduced[v]


def forward_second_kernel(
    u, za, zb, tb, ta, mask_ref, f1, f2, scal, cst, e_ref, o_ref, y_ref, rhs_t
):
    planes = u.shape[1]
    mask = mask_ref[...]
    for v in range(N):
        blocks = [stencil_block(u, v, z, planes, za, zb, ta, tb) for z in range(planes)]
        rhs_t[v] = (mask * jnp.concatenate(blocks, axis=0)).T
    reduced = forward_body(rhs_t, f1, f2, scal, cst, e_ref, o_ref)
    y_ref[...] = jnp.zeros((SEG, LANES), F32)
    for v in range(N):
        y_ref[pl.ds(v, 1), :] = reduced[v]


def backward_body(own, other, j_ref, m1, m2, scal, cst, e_ref, o_ref, x_ref, x_t):
    a, b = load_mat(cst, 0, 0), load_mat(cst, 1, 0)
    sub = lax.broadcasted_iota(jnp.int32, (SEG, LANES), 0)
    cur = []
    for i in range(N):
        acc = j_ref[pl.ds(i * N, 1), :] * own[0]
        for k in range(N):
            if k > 0:
                acc = acc + j_ref[pl.ds(i * N + k, 1), :] * own[k]
            acc = acc + j_ref[pl.ds(NN + i * N + k, 1), :] * other[k]
        cur.append(jnp.broadcast_to(acc, (SEG, LANES)))

    def recover(mb, slot, rhs, high, low):
        o = mat_vec(load_mat(mb, slot, OUT0), high)
        i = mat_vec(load_mat(mb, slot, IN0), low)
        total = [e_ref[rhs, v] + o[v] + i[v] for v in range(N)]
        return mat_vec(load_mat(mb, slot, D0), total)

    for level, s in ((2, 4), (1, 2), (0, 1)):
        new = recover(m2, level, HALF + 1 + level, [up(x, s) for x in cur], [down(x, s) for x in cur])
        cur = [jnp.where(sub % (2 * s) == s, new[v], cur[v]) for v in range(N)]
    for v in range(N):
        x_ref[0, v] = cur[v]
        x_ref[HALF, v] = up(cur[v], 1)
    for m, s in reversed(STEPS):
        mb, slot = (m1, m) if s == 1 else (m2, slot_of(m // 2))
        new = recover(
            mb, slot, m, [x_ref[m + s, v] for v in range(N)], [x_ref[m - s, v] for v in range(N)]
        )
        for v in range(N):
            x_ref[m, v] = new[v]
    low = [x_ref[0, v] for v in range(N)]
    for m in range(HALF):
        inv, fl, fr = scal[m, 0], scal[m, 1], scal[m, 2]
        high = [x_ref[m + 1, v] for v in range(N)]
        ta = mat_vec(a, high)
        tb = mat_vec(b, low)
        for v in range(N):
            odd = inv * (o_ref[m, v] + fr * ta[v] + fl * tb[v])
            x_t.at[v][pl.ds(2 * m, SEG, stride=2 * HALF), :] = low[v]
            x_t.at[v][pl.ds(2 * m + 1, SEG, stride=2 * HALF), :] = odd
        low = high


def backward_first_kernel(
    joint, other_joint, m1, m2, scal, cst, e_ref, o_ref,
    out, za, zb, ta, tb, j_ref, x_ref, x_t,
):
    join(joint, other_joint, j_ref)
    own = [joint[pl.ds(VEC_ROW + v, 1), :] for v in range(N)]
    other = [other_joint[pl.ds(VEC_ROW + v, 1), :] for v in range(N)]
    backward_body(own, other, j_ref, m1, m2, scal, cst, e_ref, o_ref, x_ref, x_t)
    _, planes, sectors, radial = out.shape
    for v in range(N):
        out[v] = x_t[v].T.reshape(planes, sectors, radial)
        pack_edges(out, v, za, zb, ta)
        pack_far_sector(out, v, tb)


def backward_second_kernel(
    y_own, y_other, j_ref, m1, m2, scal, cst, e_ref, o_ref, first, out, x_ref, x_t, stage, sem
):
    own = [y_own[pl.ds(v, 1), :] for v in range(N)]
    other = [y_other[pl.ds(v, 1), :] for v in range(N)]
    backward_body(own, other, j_ref, m1, m2, scal, cst, e_ref, o_ref, x_ref, x_t)
    _, planes, sectors, radial = out.shape
    copies = [pltpu.make_async_copy(stage.at[v], out.at[v], sem.at[v]) for v in range(N)]
    for v in range(N):
        stage[v] = first[v] + 0.5 * x_t[v].T.reshape(planes, sectors, radial)
        copies[v].start()
    for copy in copies:
        copy.wait()


def call(kernel, inputs, outs, scratch, us, hbm=False, out_hbm=False):
    vmem = pl.BlockSpec(memory_space=pltpu.VMEM)
    if hbm:
        inputs = [pltpu.with_memory_space_constraint(x, pltpu.HBM) for x in inputs]
    in_spec = pl.BlockSpec(memory_space=pltpu.HBM) if hbm else vmem
    out_shape = [s if isinstance(s, jax.ShapeDtypeStruct) else jax.ShapeDtypeStruct(s, F32) for s in outs]
    return pl.pallas_call(
        kernel,
        out_shape=out_shape,
        in_specs=[in_spec] * len(inputs),
        out_specs=[pl.BlockSpec(memory_space=pltpu.HBM) if out_hbm else vmem] * len(outs),
        scratch_shapes=[pltpu.VMEM(s, F32) if isinstance(s, tuple) else s for s in scratch],
        compiler_params=pltpu.CompilerParams(vmem_limit_bytes=VMEM_LIMIT),
        cost_estimate=pl.CostEstimate(
            flops=int(us * 1e9), bytes_accessed=int(us * 3e6), transcendentals=0
        ),
    )(*inputs)


def swapped_along(x, axis, odd, wrap):
    size = lax.axis_size(axis)
    pairs = []
    for i in range(odd, size, 2):
        if wrap or i + 1 < size:
            j = (i + 1) % size
            pairs += [(i, j), (j, i)]
    return lax.ppermute(x, axis, pairs)


def z_near(x):
    return swapped_along(x, "ax", 0, False)


def z_far(x):
    return swapped_along(x, "ax", 1, False)


def t_near(x):
    return swapped_along(x, "az", 0, True)


def t_far(x):
    return swapped_along(x, "az", 1, True)


def xor_swap(x, bit):
    return lax.ppermute(x, "az", [(i, i ^ bit) for i in range(lax.axis_size("az"))])


def append(low, high):
    (both,) = call(append_kernel, (low, high), [(N, 2 * low.shape[1], low.shape[2])], [], 0.2)
    return both


def after(x, *others):
    return lax.optimization_barrier((x, *others))[0]


def per_device(
    flow_state, radial_coef, blanking, canard_index, canard_table, coupling, upwind_split
):
    comps, planes, sectors, radial = flow_state.shape
    tile = (SEG, LANES)
    half_turn = lax.axis_size("az") // 2
    field = (comps, planes, sectors, radial)
    edges = [(comps, sectors, radial)] * 2 + [(comps, planes, radial)] * 2
    columns = (comps, radial, LANES)
    bits = doubling_bits()

    rows = canard_table[0].transpose(1, 0, 2)
    got = xor_swap(rows, bits[0])
    u, coef, mask, place, cst, za, zb, ta, tb = call(
        prelude_kernel,
        (flow_state, radial_coef, blanking, canard_index, coupling, upwind_split),
        [
            field,
            (planes, sectors, radial),
            (LANES, radial),
            jax.ShapeDtypeStruct(canard_index.shape, jnp.int32),
            (2, NN) + tile,
        ]
        + edges,
        [
            pltpu.VMEM((planes, sectors, radial), jnp.int32),
            pltpu.VMEM(canard_index.shape, jnp.int32),
            pltpu.SMEM((N, N), F32),
            pltpu.SMEM((N,), F32),
            pltpu.SemaphoreType.DMA((6,)),
        ],
        1.2,
        hbm=True,
    )
    first = {"zb": z_far(zb)}
    rows = append(rows, after(got, cst))
    done = {}

    def factor(rows, got):
        done["one"] = call(
            factor_kernel,
            (after(coef, rows), mask, cst),
            [
                (HALF + 1, 3 * NN) + tile,
                (HALF // 2, 2 * NN) + tile,
                (HALF, 3) + tile,
                (JOINT_ROWS, LANES),
                (radial, LANES),
            ],
            [(radial, LANES), (2 * HALF + 1,) + tile, (4, NN) + tile],
            3.2,
        )
        return after(got, done["one"][3])

    def far_halos(rows, got):
        first["tb"] = t_far(after(tb, rows))
        first["za"] = z_near(after(za, rows))
        return after(got, first["zb"])

    def factor_rest(rows, got):
        first["ta"] = t_near(after(ta, rows))
        done["rest"] = call(
            factor_rest_kernel,
            (after(done["one"][0], rows), done["one"][3]),
            [
                (HALF // 2 + 3, 3 * NN) + tile,
                (HALF // 2 + 2, 2 * NN) + tile,
                (JOINT_ROWS, LANES),
            ],
            [],
            3.0,
        )
        return after(got, done["rest"][2], first["za"], first["ta"], first["tb"])

    fillers = [factor, far_halos, factor_rest]
    for i, bit in enumerate(bits[1:-1]):
        rows = append(rows, fillers[i](rows, xor_swap(rows, bit)))
    for filler in fillers[len(bits) - 2 :]:
        rows = filler(rows, rows)
    others = xor_swap(rows, bits[-1])
    m1, f1, scal, _, mask_t = done["one"]
    m2, f2, sd = done["rest"]
    (rhs,) = call(
        rhs_kernel,
        (u, first["za"], first["zb"], first["ta"], first["tb"], mask, mask_t, place, rows),
        [columns],
        [],
        1.3,
    )
    others = after(others, rhs)

    fwd_outs = [(HALF + 4, N) + tile, (HALF, N) + tile]
    back_scratch = [(HALF + 1, N) + tile, columns]
    e1, o1, joint = call(
        forward_first_kernel,
        (rhs, mask_t, place, others, f1, f2, scal, cst, sd),
        fwd_outs + [(JOINT_ROWS, LANES)],
        [columns],
        1.2,
    )
    other_joint = xor_swap(joint, half_turn)
    delta, za, zb, ta, tb, axis_inverse = call(
        backward_first_kernel,
        (joint, other_joint, m1, m2, scal, cst, e1, o1),
        [field] + edges + [(2 * NN, LANES)],
        back_scratch,
        1.3,
    )
    tb, zb, za, ta = t_far(tb), z_far(zb), z_near(za), t_near(ta)
    e2, o2, y2 = call(
        forward_second_kernel,
        (delta, za, zb, tb, ta, mask, f1, f2, scal, cst),
        fwd_outs + [tile],
        [columns],
        1.3,
    )
    other_y2 = xor_swap(y2, half_turn)
    (update,) = call(
        backward_second_kernel,
        (y2, other_y2, axis_inverse, m1, m2, scal, cst, e2, o2, delta),
        [field],
        back_scratch + [field, pltpu.SemaphoreType.DMA((N,))],
        2.0,
        out_hbm=True,
    )
    return update


def solution(mesh):
    return jax.shard_map(
        per_device,
        mesh=mesh,
        in_specs=(
            P(None, "ax", "az", None),
            P("ax", "az", None),
            P("ax", "az", None),
            P("ax", "az"),
            P("ax", "az", None, None),
            P(),
            P(),
        ),
        out_specs=P(None, "ax", "az", None),
        check_vma=False,
    )
```

```python
import jax
import jax.numpy as jnp
from jax import lax
from jax.experimental import pallas as pl
from jax.experimental.pallas import tpu as pltpu
from jax.sharding import PartitionSpec as P

N = 5
NN = 25
SEG = 8
LANES = 128
HALF = 16
VMEM_LIMIT = 16 * 1024 * 1024
F32 = jnp.float32
STEPS = [(s * (2 * i + 1), s) for s in (1, 2, 4, 8) for i in range(8 // s)]


def up(x, s):
    return pltpu.roll(x, SEG - s, 0)


def down(x, s):
    return pltpu.roll(x, s, 0)


def splat_consts(coupling_ref, upwind_ref):
    shape = (SEG, LANES)
    p = [[jnp.full(shape, coupling_ref[i, j], F32) for j in range(N)] for i in range(N)]
    w = [jnp.full(shape, upwind_ref[i], F32) for i in range(N)]
    a = [[p[i][j] + w[i] if i == j else p[i][j] for j in range(N)] for i in range(N)]
    b = [[(1.0 - w[i]) - p[j][i] if i == j else -p[j][i] for j in range(N)] for i in range(N)]
    return a, b


def dot_row(row, cols, j):
    acc = row[0] * cols[0][j]
    for k in range(1, N):
        acc = acc + row[k] * cols[k][j]
    return acc


def mat_mul(x, y):
    return [[dot_row(x[i], y, j) for j in range(N)] for i in range(N)]


def mat_vec(x, v):
    out = []
    for i in range(N):
        acc = x[i][0] * v[0]
        for k in range(1, N):
            acc = acc + x[i][k] * v[k]
        out.append(acc)
    return out


def invert(matrix):
    m = [list(row) for row in matrix]
    for p in range(N):
        piv = 1.0 / m[p][p]
        m[p] = [piv if j == p else m[p][j] * piv for j in range(N)]
        for i in range(N):
            if i != p:
                f = m[i][p]
                m[i] = [-(f * piv) if j == p else m[i][j] - f * m[p][j] for j in range(N)]
    return m


def load_mat(ref, slot, base):
    return [[ref[slot, base + i * N + j] for j in range(N)] for i in range(N)]


def load_row(ref, slot, base, i):
    return [ref[slot, base + i * N + j] for j in range(N)]


def store_mat(ref, slot, base, mat):
    for i in range(N):
        for j in range(N):
            ref[slot, base + i * N + j] = mat[i][j]


def strided(ref, k):
    return ref[pl.ds(k, SEG, stride=2 * HALF), :]


def slot_of(q):
    return q + 2


LAM_ROW, MASK_ROW, VEC_ROW, JOINT_ROWS = NN, NN + 1, NN + 2, 32
D0, OUT0, IN0 = 0, NN, 2 * NN
LO0, LI0 = 0, NN


def is_even(axis):
    return lax.axis_index(axis) % 2 == 0


def pack_far_sector(field, v, tb):
    _, planes, sectors, _ = field.shape
    up = is_even("az")
    for z in range(planes):
        first, last = field[v, z, pl.ds(0, 1), :], field[v, z, pl.ds(sectors - 1, 1), :]
        tb[v, pl.ds(z, 1), :] = jnp.where(up, first, last)


def pack_edges(field, v, za, zb, ta):
    _, planes, sectors, _ = field.shape
    z_up, t_up = is_even("ax"), is_even("az")
    za[v] = field[v, jnp.where(z_up, planes - 1, 0)]
    zb[v] = field[v, jnp.where(z_up, 0, planes - 1)]
    for z in range(planes):
        first, last = field[v, z, pl.ds(0, 1), :], field[v, z, pl.ds(sectors - 1, 1), :]
        ta[v, pl.ds(z, 1), :] = jnp.where(t_up, last, first)


def prelude_kernel(
    flow, coef, blank, index, coup, upw,
    u, coef_ref, mask_ref, place, cst, za, zb, ta, tb,
    blank_ref, index_ref, coup_ref, upw_ref, sem,
):
    pairs = (
        (flow, u),
        (coup, coup_ref),
        (upw, upw_ref),
        (index, index_ref),
        (blank, blank_ref),
        (coef, coef_ref),
    )
    copies = [pltpu.make_async_copy(src, dst, sem.at[i]) for i, (src, dst) in enumerate(pairs)]
    for copy in copies:
        copy.start()
    _, planes, sectors, radial = u.shape
    copies[1].wait()
    copies[2].wait()
    a, b = splat_consts(coup_ref, upw_ref)
    store_mat(cst, 0, 0, a)
    store_mat(cst, 1, 0, b)
    copies[3].wait()
    place[...] = table_place(index_ref[...])
    copies[4].wait()
    mask_ref[...] = blank_ref[...].astype(F32).reshape(planes * sectors, radial)
    copies[5].wait()
    copies[0].wait()
    for v in range(N):
        pack_edges(u, v, za, zb, ta)
        pack_far_sector(u, v, tb)


def append_kernel(low, high, out):
    half = low.shape[1]
    out[:, pl.ds(0, half), :] = low[...]
    out[:, pl.ds(half, half), :] = high[...]


def factor_kernel(coef_ref, mask_ref, cst, m1, f1, scal, sd, mask_t, lam_t, face, pw):
    mask = mask_ref[...]
    lam = coef_ref[...].reshape(LANES, 2 * HALF * SEG) * mask
    lam_t[...] = lam.T
    mask_t[...] = mask.T
    a, b = load_mat(cst, 0, 0), load_mat(cst, 1, 0)
    for which, mat in enumerate((mat_mul(a, a), mat_mul(b, b), mat_mul(a, b), mat_mul(b, a))):
        store_mat(pw, which, 0, mat)

    sub = lax.broadcasted_iota(jnp.int32, (SEG, LANES), 0)
    first_lam, first_mask = strided(lam_t, 0), strided(mask_t, 0)
    lam_k, mask_k = first_lam, first_mask
    for k in range(2 * HALF):
        if k < 2 * HALF - 1:
            lam_n, mask_n = strided(lam_t, k + 1), strided(mask_t, k + 1)
            f = 0.5 * (lam_k * mask_n + lam_n * mask_k)
        else:
            lam_n, mask_n = up(first_lam, 1), up(first_mask, 1)
            f = jnp.where(sub == SEG - 1, 0.0, 0.5 * (lam_k * mask_n + lam_n * mask_k))
        face[k + 1] = f
        lam_k, mask_k = lam_n, mask_n
    face[0] = down(face[2 * HALF], 1)

    def build_odd(m, c):
        fl, fr = face[2 * m + 1], face[2 * m + 2]
        scal[m, 0] = 1.0 / (1.0 + 0.5 * (fl + fr))
        scal[m, 1] = fl
        scal[m, 2] = fr
        return c

    lax.fori_loop(0, HALF, build_odd, 0)

    def build_even(p, c):
        prev = jnp.where(p == 0, HALF - 1, p - 1)
        inv, fl, fr = scal[p, 0], scal[p, 1], scal[p, 2]
        inv_p, fl_p, fr_p = scal[prev, 0], scal[prev, 1], scal[prev, 2]
        beta = fr_p * fr_p * inv_p
        delta = fr_p * fl_p * inv_p
        beta = jnp.where(p == 0, down(beta, 1), beta)
        alpha = fl * fl * inv
        gamma = fl * fr * inv
        d = 1.0 + 0.5 * (face[2 * p] + face[2 * p + 1])
        for i in range(N):
            for j in range(N):
                e = i * N + j
                val = -(alpha * pw[2, e] + beta * pw[3, e])
                m1[p, D0 + e] = d + val if i == j else val
                m1[p, OUT0 + e] = gamma * pw[0, e]
                m1[p, IN0 + e] = delta * pw[1, e]
        return c

    lax.fori_loop(0, HALF, build_even, 0)
    last = scal[HALF - 1, 1] * scal[HALF - 1, 2] * scal[HALF - 1, 0]
    for e in range(NN):
        m1[HALF, D0 + e] = jnp.zeros((SEG, LANES), F32)
        m1[HALF, OUT0 + e] = jnp.zeros((SEG, LANES), F32)
        m1[HALF, IN0 + e] = last * pw[1, e]

    sd[...] = jnp.zeros((JOINT_ROWS, LANES), F32)
    sd[pl.ds(LAM_ROW, 1), :] = first_lam[0:1]
    sd[pl.ds(MASK_ROW, 1), :] = first_mask[0:1]

    def step(i, c):
        eliminate(m1, f1, 1, 2 * i + 1, i)
        return c

    lax.fori_loop(0, HALF // 2, step, 0)


def eliminate(mb, mf, s, sm, fm):
    sp, sq = sm - s, sm + s
    di = invert(load_mat(mb, sm, D0))
    store_mat(mb, sm, D0, di)
    for i in range(N):
        row = load_row(mb, sp, OUT0, i)
        for j in range(N):
            mf[fm, LO0 + i * N + j] = dot_row(row, di, j)
        row = load_row(mb, sq, IN0, i)
        for j in range(N):
            mf[fm, LI0 + i * N + j] = dot_row(row, di, j)
    in_m = load_mat(mb, sm, IN0)
    for i in range(N):
        row = load_row(mf, fm, LO0, i)
        for j in range(N):
            e = i * N + j
            mb[sp, D0 + e] = mb[sp, D0 + e] - dot_row(row, in_m, j)
        row = load_row(mf, fm, LI0, i)
        for j in range(N):
            mb[sq, IN0 + i * N + j] = dot_row(row, in_m, j)
    out_m = load_mat(mb, sm, OUT0)
    for i in range(N):
        row = load_row(mf, fm, LI0, i)
        for j in range(N):
            e = i * N + j
            mb[sq, D0 + e] = mb[sq, D0 + e] - dot_row(row, out_m, j)
        row = load_row(mf, fm, LO0, i)
        for j in range(N):
            mb[sp, OUT0 + i * N + j] = dot_row(row, out_m, j)


def factor_rest_kernel(m1, sd_in, mb, mf, sd):
    def fetch(q, c):
        for e in range(3 * NN):
            mb[slot_of(q), e] = m1[2 * q, e]
        return c

    lax.fori_loop(0, HALF // 2 + 1, fetch, 0)

    def step(it, c):
        s = jnp.where(it < 4, 1, jnp.where(it < 6, 2, 4))
        first = jnp.where(it < 4, 0, jnp.where(it < 6, 4, 6))
        q = s * (2 * (it - first) + 1)
        eliminate(mb, mf, s, slot_of(q), slot_of(q))
        return c

    lax.fori_loop(0, HALF // 2 - 1, step, 0)
    sd[...] = sd_in[...]
    s0, s16 = slot_of(0), slot_of(HALF // 2)
    for e in range(NN):
        mb[0, D0 + e] = mb[s0, D0 + e] + down(mb[s16, D0 + e], 1)
        mb[0, OUT0 + e] = mb[s0, OUT0 + e]
        mb[0, IN0 + e] = down(mb[s16, IN0 + e], 1)
    for level, s in enumerate((1, 2, 4)):
        d = load_mat(mb, level, D0)
        di = invert(d)
        store_mat(mb, level, D0, di)
        di_up = [[up(di[i][j], s) for j in range(N)] for i in range(N)]
        for i in range(N):
            row = load_row(mb, level, OUT0, i)
            for j in range(N):
                mf[level, LO0 + i * N + j] = dot_row(row, di_up, j)
        di_down = [[down(di[i][j], s) for j in range(N)] for i in range(N)]
        for i in range(N):
            row = load_row(mb, level, IN0, i)
            for j in range(N):
                mf[level, LI0 + i * N + j] = dot_row(row, di_down, j)
        in_up = [[up(mb[level, IN0 + i * N + j], s) for j in range(N)] for i in range(N)]
        acc = []
        for i in range(N):
            row = load_row(mf, level, LO0, i)
            acc.append([d[i][j] - dot_row(row, in_up, j) for j in range(N)])
        out_down = [[down(mb[level, OUT0 + i * N + j], s) for j in range(N)] for i in range(N)]
        for i in range(N):
            row = load_row(mf, level, LI0, i)
            for j in range(N):
                val = acc[i][j] - dot_row(row, out_down, j)
                if level < 2:
                    mb[level + 1, D0 + i * N + j] = val
                else:
                    sd[pl.ds(i * N + j, 1), :] = val[0:1]
        if level < 2:
            out_up = [[up(mb[level, OUT0 + i * N + j], s) for j in range(N)] for i in range(N)]
            for i in range(N):
                row = load_row(mf, level, LO0, i)
                for j in range(N):
                    mb[level + 1, OUT0 + i * N + j] = dot_row(row, out_up, j)
            in_down = [[down(mb[level, IN0 + i * N + j], s) for j in range(N)] for i in range(N)]
            for i in range(N):
                row = load_row(mf, level, LI0, i)
                for j in range(N):
                    mb[level + 1, IN0 + i * N + j] = dot_row(row, in_down, j)


def join(own_ref, other_ref, j_ref):
    lam, mask = own_ref[pl.ds(LAM_ROW, 1), :], own_ref[pl.ds(MASK_ROW, 1), :]
    other_lam, other_mask = other_ref[pl.ds(LAM_ROW, 1), :], other_ref[pl.ds(MASK_ROW, 1), :]
    c = 0.25 * (lam * other_mask + other_lam * mask)

    def total(ref):
        mat = [[ref[pl.ds(i * N + j, 1), :] for j in range(N)] for i in range(N)]
        return [[mat[i][j] + c if i == j else mat[i][j] for j in range(N)] for i in range(N)]

    own, inv_other = total(own_ref), invert(total(other_ref))
    schur = [[own[i][j] - c * (c * inv_other[i][j]) for j in range(N)] for i in range(N)]
    j1 = invert(schur)
    j2 = mat_mul(j1, inv_other)
    for i in range(N):
        for j in range(N):
            j_ref[pl.ds(i * N + j, 1), :] = j1[i][j]
            j_ref[pl.ds(NN + i * N + j, 1), :] = c * j2[i][j]


def plane_neighbours(za, zb, v):
    z_up = is_even("ax")
    return jnp.where(z_up, zb[v], za[v]), jnp.where(z_up, za[v], zb[v])


def stencil_block(u, v, z, before, after, ta, tb):
    planes, sectors = u.shape[1], u.shape[2]
    t_up = is_even("az")
    cur = u[v, z]
    rows = lax.broadcasted_iota(jnp.int32, cur.shape, 0)
    behind = u[v, z - 1] if z > 0 else before
    ahead = u[v, z + 1] if z < planes - 1 else after
    t_a, t_b = ta[v, pl.ds(z, 1), :], tb[v, pl.ds(z, 1), :]
    before_t = jnp.where(rows == 0, jnp.where(t_up, t_b, t_a), pltpu.roll(cur, 1, 0))
    after_t = jnp.where(rows == sectors - 1, jnp.where(t_up, t_a, t_b), pltpu.roll(cur, sectors - 1, 0))
    total = before_t + after_t - 4.0 * cur
    if behind is not None:
        total = total + 1.5 * behind
    if ahead is not None:
        total = total + 0.5 * ahead
    return total


def forward_body(rhs_t, f1, f2, scal, cst, e_ref, o_ref):
    a, b = load_mat(cst, 0, 0), load_mat(cst, 1, 0)
    zero = jnp.zeros((SEG, LANES), F32)
    carry = [zero] * N
    first = None
    for m in range(HALF):
        inv, fl, fr = scal[m, 0], scal[m, 1], scal[m, 2]
        odd = [strided(rhs_t.at[v], 2 * m + 1) for v in range(N)]
        scaled = [x * inv for x in odd]
        ta = mat_vec(a, scaled)
        tb = mat_vec(b, scaled)
        for v in range(N):
            o_ref[m, v] = odd[v]
            e_ref[m, v] = strided(rhs_t.at[v], 2 * m) + carry[v] + fl * ta[v]
        carry = [fr * tb[v] for v in range(N)]
    for v in range(N):
        e_ref[0, v] = e_ref[0, v] + down(carry[v], 1)
        e_ref[HALF, v] = zero
    for m, s in STEPS:
        vec = [e_ref[m, v] for v in range(N)]
        mf, slot = (f1, m // 2) if s == 1 else (f2, slot_of(m // 2))
        lo = mat_vec(load_mat(mf, slot, LO0), vec)
        li = mat_vec(load_mat(mf, slot, LI0), vec)
        for v in range(N):
            e_ref[m - s, v] = e_ref[m - s, v] + lo[v]
            e_ref[m + s, v] = e_ref[m + s, v] + li[v]
    cur = [e_ref[0, v] + down(e_ref[HALF, v], 1) for v in range(N)]
    for level, s in enumerate((1, 2, 4)):
        for v in range(N):
            e_ref[HALF + 1 + level, v] = cur[v]
        lo = mat_vec(load_mat(f2, level, LO0), [up(x, s) for x in cur])
        li = mat_vec(load_mat(f2, level, LI0), [down(x, s) for x in cur])
        cur = [cur[v] + lo[v] + li[v] for v in range(N)]
    return [cur[v][0:1] for v in range(N)]


def doubling_bits():
    return [bit for bit in (24, 8, 4, 2, 1) if bit < lax.axis_size("az")]


def table_place(index):
    apart = lax.shift_right_logical(index, 2) ^ lax.axis_index("az")
    block = jnp.zeros_like(apart)
    for i, bit in enumerate(doubling_bits()):
        used = (apart & (1 << (bit.bit_length() - 1))) != 0
        apart = jnp.where(used, apart ^ bit, apart)
        block = block | (jnp.where(used, 1, 0) << i)
    return block * 4 + (index & 3)


def one_hot(place, start, count):
    planes, sectors = place.shape
    rows = start + lax.broadcasted_iota(jnp.int32, (count, sectors), 0)
    hot = [jnp.where(rows == place[pl.ds(z, 1), :], 1.0, 0.0) for z in range(planes)]
    return jnp.concatenate(hot, axis=1)


def pick(rows, hot):
    return lax.dot_general(
        rows,
        hot,
        (((0,), (0,)), ((), ())),
        precision=lax.Precision.HIGHEST,
        preferred_element_type=F32,
    )


def rhs_kernel(u, za, zb, ta, tb, mask_ref, mask_t, place, low, rhs_t):
    planes = u.shape[1]
    mask = mask_ref[...]
    hot = one_hot(place, 0, low.shape[1])
    for v in range(N):
        before, after = plane_neighbours(za, zb, v)
        blocks = [stencil_block(u, v, z, before, after, ta, tb) for z in range(planes)]
        rhs_t[v] = (mask * jnp.concatenate(blocks, axis=0)).T + mask_t[...] * pick(low[v], hot)


def forward_first_kernel(
    rhs_in, mask_t, place, high, f1, f2, scal, cst, sd, e_ref, o_ref, joint, rhs_t
):
    hot = one_hot(place, high.shape[1], high.shape[1])
    for v in range(N):
        rhs_t[v] = rhs_in[v] + mask_t[...] * pick(high[v], hot)
    reduced = forward_body(rhs_t, f1, f2, scal, cst, e_ref, o_ref)
    joint[...] = sd[...]
    for v in range(N):
        joint[pl.ds(VEC_ROW + v, 1), :] = reduced[v]


def rhs_second_kernel(u, tb, ta, mask_ref, rhs_t):
    planes = u.shape[1]
    mask = mask_ref[...]
    for v in range(N):
        blocks = [stencil_block(u, v, z, None, None, ta, tb) for z in range(planes)]
        rhs_t[v] = (mask * jnp.concatenate(blocks, axis=0)).T


def forward_second_kernel(
    rhs_in, za, zb, mask_t, f1, f2, scal, cst, e_ref, o_ref, y_ref, rhs_t
):
    sectors, radial = za.shape[1], za.shape[2]
    zero = jnp.zeros((LANES - 2 * sectors, radial), F32)
    for v in range(N):
        before, after = plane_neighbours(za, zb, v)
        outer = jnp.concatenate([1.5 * before, zero, 0.5 * after], axis=0)
        rhs_t[v] = rhs_in[v] + mask_t[...] * outer.T
    reduced = forward_body(rhs_t, f1, f2, scal, cst, e_ref, o_ref)
    y_ref[...] = jnp.zeros((SEG, LANES), F32)
    for v in range(N):
        y_ref[pl.ds(v, 1), :] = reduced[v]


def backward_body(own, other, j_ref, m1, m2, scal, cst, e_ref, o_ref, x_ref, x_t):
    a, b = load_mat(cst, 0, 0), load_mat(cst, 1, 0)
    sub = lax.broadcasted_iota(jnp.int32, (SEG, LANES), 0)
    cur = []
    for i in range(N):
        acc = j_ref[pl.ds(i * N, 1), :] * own[0]
        for k in range(N):
            if k > 0:
                acc = acc + j_ref[pl.ds(i * N + k, 1), :] * own[k]
            acc = acc + j_ref[pl.ds(NN + i * N + k, 1), :] * other[k]
        cur.append(jnp.broadcast_to(acc, (SEG, LANES)))

    def recover(mb, slot, rhs, high, low):
        o = mat_vec(load_mat(mb, slot, OUT0), high)
        i = mat_vec(load_mat(mb, slot, IN0), low)
        total = [e_ref[rhs, v] + o[v] + i[v] for v in range(N)]
        return mat_vec(load_mat(mb, slot, D0), total)

    for level, s in ((2, 4), (1, 2), (0, 1)):
        new = recover(m2, level, HALF + 1 + level, [up(x, s) for x in cur], [down(x, s) for x in cur])
        cur = [jnp.where(sub % (2 * s) == s, new[v], cur[v]) for v in range(N)]
    for v in range(N):
        x_ref[0, v] = cur[v]
        x_ref[HALF, v] = up(cur[v], 1)
    for m, s in reversed(STEPS):
        mb, slot = (m1, m) if s == 1 else (m2, slot_of(m // 2))
        new = recover(
            mb, slot, m, [x_ref[m + s, v] for v in range(N)], [x_ref[m - s, v] for v in range(N)]
        )
        for v in range(N):
            x_ref[m, v] = new[v]
    low = [x_ref[0, v] for v in range(N)]
    for m in range(HALF):
        inv, fl, fr = scal[m, 0], scal[m, 1], scal[m, 2]
        high = [x_ref[m + 1, v] for v in range(N)]
        ta = mat_vec(a, high)
        tb = mat_vec(b, low)
        for v in range(N):
            odd = inv * (o_ref[m, v] + fr * ta[v] + fl * tb[v])
            x_t.at[v][pl.ds(2 * m, SEG, stride=2 * HALF), :] = low[v]
            x_t.at[v][pl.ds(2 * m + 1, SEG, stride=2 * HALF), :] = odd
        low = high


def backward_first_kernel(
    joint, other_joint, m1, m2, scal, cst, e_ref, o_ref,
    out, za, zb, ta, tb, j_ref, x_ref, x_t,
):
    join(joint, other_joint, j_ref)
    own = [joint[pl.ds(VEC_ROW + v, 1), :] for v in range(N)]
    other = [other_joint[pl.ds(VEC_ROW + v, 1), :] for v in range(N)]
    backward_body(own, other, j_ref, m1, m2, scal, cst, e_ref, o_ref, x_ref, x_t)
    _, planes, sectors, radial = out.shape
    for v in range(N):
        out[v] = x_t[v].T.reshape(planes, sectors, radial)
        pack_edges(out, v, za, zb, ta)
        pack_far_sector(out, v, tb)


def backward_second_kernel(
    y_own, y_other, j_ref, m1, m2, scal, cst, e_ref, o_ref, first, out, x_ref, x_t, stage, sem
):
    own = [y_own[pl.ds(v, 1), :] for v in range(N)]
    other = [y_other[pl.ds(v, 1), :] for v in range(N)]
    backward_body(own, other, j_ref, m1, m2, scal, cst, e_ref, o_ref, x_ref, x_t)
    _, planes, sectors, radial = out.shape
    copies = [pltpu.make_async_copy(stage.at[v], out.at[v], sem.at[v]) for v in range(N)]
    for v in range(N):
        stage[v] = first[v] + 0.5 * x_t[v].T.reshape(planes, sectors, radial)
        copies[v].start()
    for copy in copies:
        copy.wait()


def call(kernel, inputs, outs, scratch, us, hbm=False, out_hbm=False):
    vmem = pl.BlockSpec(memory_space=pltpu.VMEM)
    if hbm:
        inputs = [pltpu.with_memory_space_constraint(x, pltpu.HBM) for x in inputs]
    in_spec = pl.BlockSpec(memory_space=pltpu.HBM) if hbm else vmem
    out_shape = [s if isinstance(s, jax.ShapeDtypeStruct) else jax.ShapeDtypeStruct(s, F32) for s in outs]
    return pl.pallas_call(
        kernel,
        out_shape=out_shape,
        in_specs=[in_spec] * len(inputs),
        out_specs=[pl.BlockSpec(memory_space=pltpu.HBM) if out_hbm else vmem] * len(outs),
        scratch_shapes=[pltpu.VMEM(s, F32) if isinstance(s, tuple) else s for s in scratch],
        compiler_params=pltpu.CompilerParams(vmem_limit_bytes=VMEM_LIMIT),
        cost_estimate=pl.CostEstimate(
            flops=int(us * 1e9), bytes_accessed=int(us * 3e6), transcendentals=0
        ),
    )(*inputs)


def swapped_along(x, axis, odd, wrap):
    size = lax.axis_size(axis)
    pairs = []
    for i in range(odd, size, 2):
        if wrap or i + 1 < size:
            j = (i + 1) % size
            pairs += [(i, j), (j, i)]
    return lax.ppermute(x, axis, pairs)


def z_near(x):
    return swapped_along(x, "ax", 0, False)


def z_far(x):
    return swapped_along(x, "ax", 1, False)


def t_near(x):
    return swapped_along(x, "az", 0, True)


def t_far(x):
    return swapped_along(x, "az", 1, True)


def xor_swap(x, bit):
    return lax.ppermute(x, "az", [(i, i ^ bit) for i in range(lax.axis_size("az"))])


def append(low, high):
    (both,) = call(append_kernel, (low, high), [(N, 2 * low.shape[1], low.shape[2])], [], 0.2)
    return both


def after(x, *others):
    return lax.optimization_barrier((x, *others))[0]


def per_device(
    flow_state, radial_coef, blanking, canard_index, canard_table, coupling, upwind_split
):
    comps, planes, sectors, radial = flow_state.shape
    tile = (SEG, LANES)
    half_turn = lax.axis_size("az") // 2
    field = (comps, planes, sectors, radial)
    edges = [(comps, sectors, radial)] * 2 + [(comps, planes, radial)] * 2
    columns = (comps, radial, LANES)
    bits = doubling_bits()

    rows = canard_table[0].transpose(1, 0, 2)
    got = xor_swap(rows, bits[0])
    u, coef, mask, place, cst, za, zb, ta, tb = call(
        prelude_kernel,
        (flow_state, radial_coef, blanking, canard_index, coupling, upwind_split),
        [
            field,
            (planes, sectors, radial),
            (LANES, radial),
            jax.ShapeDtypeStruct(canard_index.shape, jnp.int32),
            (2, NN) + tile,
        ]
        + edges,
        [
            pltpu.VMEM((planes, sectors, radial), jnp.int32),
            pltpu.VMEM(canard_index.shape, jnp.int32),
            pltpu.SMEM((N, N), F32),
            pltpu.SMEM((N,), F32),
            pltpu.SemaphoreType.DMA((6,)),
        ],
        1.2,
        hbm=True,
    )
    rows = append(rows, after(got, cst))
    halo, done = {"za": z_near(za), "zb": z_far(zb)}, []

    def factor(rows, got):
        done.extend(
            call(
                factor_kernel,
                (after(coef, rows), mask, cst),
                [
                    (HALF + 1, 3 * NN) + tile,
                    (HALF // 2, 2 * NN) + tile,
                    (HALF, 3) + tile,
                    (JOINT_ROWS, LANES),
                    (radial, LANES),
                ],
                [(radial, LANES), (2 * HALF + 1,) + tile, (4, NN) + tile],
                3.2,
            )
        )
        return after(got, done[3])

    def sector_halos(rows, got):
        halo["tb"], halo["ta"] = t_far(after(tb, rows)), t_near(after(ta, rows))
        return after(got, halo["za"], halo["zb"])

    def factor_rest(rows, got):
        m1, sd = done[0], done[3]
        done.extend(
            call(
                factor_rest_kernel,
                (after(m1, rows), sd),
                [
                    (HALF // 2 + 3, 3 * NN) + tile,
                    (HALF // 2 + 2, 2 * NN) + tile,
                    (JOINT_ROWS, LANES),
                ],
                [],
                3.0,
            )
        )
        return after(got, done[-1], halo["ta"], halo["tb"])

    fillers = [factor, sector_halos, factor_rest]
    for i, bit in enumerate(bits[1:-1]):
        rows = append(rows, fillers[i](rows, xor_swap(rows, bit)))
    for filler in fillers[len(bits) - 2 :]:
        rows = filler(rows, rows)
    m1, f1, scal, _, mask_t, m2, f2, sd = done
    others = xor_swap(rows, bits[-1])
    (rhs,) = call(
        rhs_kernel,
        (u, halo["za"], halo["zb"], halo["ta"], halo["tb"], mask, mask_t, place, rows),
        [columns],
        [],
        1.3,
    )
    others = after(others, rhs)

    fwd_outs = [(HALF + 4, N) + tile, (HALF, N) + tile]
    back_scratch = [(HALF + 1, N) + tile, columns]
    e1, o1, joint = call(
        forward_first_kernel,
        (rhs, mask_t, place, others, f1, f2, scal, cst, sd),
        fwd_outs + [(JOINT_ROWS, LANES)],
        [columns],
        1.2,
    )
    other_joint = xor_swap(joint, half_turn)
    delta, za, zb, ta, tb, axis_inverse = call(
        backward_first_kernel,
        (joint, other_joint, m1, m2, scal, cst, e1, o1),
        [field] + edges + [(2 * NN, LANES)],
        back_scratch,
        1.3,
    )
    tb, zb, za, ta = t_far(tb), z_far(zb), z_near(za), t_near(ta)
    (rhs,) = call(rhs_second_kernel, (delta, tb, ta, mask), [columns], [], 4.0)
    e2, o2, y2 = call(
        forward_second_kernel,
        (rhs, za, zb, mask_t, f1, f2, scal, cst),
        fwd_outs + [tile],
        [columns],
        1.3,
    )
    other_y2 = xor_swap(y2, half_turn)
    (update,) = call(
        backward_second_kernel,
        (y2, other_y2, axis_inverse, m1, m2, scal, cst, e2, o2, delta),
        [field],
        back_scratch + [field, pltpu.SemaphoreType.DMA((N,))],
        2.0,
        out_hbm=True,
    )
    return update


def solution(mesh):
    return jax.shard_map(
        per_device,
        mesh=mesh,
        in_specs=(
            P(None, "ax", "az", None),
            P("ax", "az", None),
            P("ax", "az", None),
            P("ax", "az"),
            P("ax", "az", None, None),
            P(),
            P(),
        ),
        out_specs=P(None, "ax", "az", None),
        check_vma=False,
    )
```

```python
import jax
import jax.numpy as jnp
from jax import lax
from jax.experimental import pallas as pl
from jax.experimental.pallas import tpu as pltpu
from jax.sharding import PartitionSpec as P

N = 5
NN = 25
SEG = 8
LANES = 128
HALF = 16
VMEM_LIMIT = 16 * 1024 * 1024
F32 = jnp.float32
STEPS = [(s * (2 * i + 1), s) for s in (1, 2, 4, 8) for i in range(8 // s)]


def up(x, s):
    return pltpu.roll(x, SEG - s, 0)


def down(x, s):
    return pltpu.roll(x, s, 0)


def splat_consts(coupling_ref, upwind_ref):
    shape = (SEG, LANES)
    p = [[jnp.full(shape, coupling_ref[i, j], F32) for j in range(N)] for i in range(N)]
    w = [jnp.full(shape, upwind_ref[i], F32) for i in range(N)]
    a = [[p[i][j] + w[i] if i == j else p[i][j] for j in range(N)] for i in range(N)]
    b = [[(1.0 - w[i]) - p[j][i] if i == j else -p[j][i] for j in range(N)] for i in range(N)]
    return a, b


def dot_row(row, cols, j):
    acc = row[0] * cols[0][j]
    for k in range(1, N):
        acc = acc + row[k] * cols[k][j]
    return acc


def mat_mul(x, y):
    return [[dot_row(x[i], y, j) for j in range(N)] for i in range(N)]


def mat_vec(x, v):
    out = []
    for row in x:
        t = [row[k] * v[k] for k in range(N)]
        out.append((t[0] + t[1]) + (t[2] + t[3]) + t[4])
    return out


def invert(matrix):
    m = [list(row) for row in matrix]
    for p in range(N):
        piv = 1.0 / m[p][p]
        m[p] = [piv if j == p else m[p][j] * piv for j in range(N)]
        for i in range(N):
            if i != p:
                f = m[i][p]
                m[i] = [-(f * piv) if j == p else m[i][j] - f * m[p][j] for j in range(N)]
    return m


def load_mat(ref, slot, base):
    return [[ref[slot, base + i * N + j] for j in range(N)] for i in range(N)]


def load_row(ref, slot, base, i):
    return [ref[slot, base + i * N + j] for j in range(N)]


def store_mat(ref, slot, base, mat):
    for i in range(N):
        for j in range(N):
            ref[slot, base + i * N + j] = mat[i][j]


def strided(ref, k):
    return ref[pl.ds(k, SEG, stride=2 * HALF), :]


def slot_of(q):
    return q + 2


LAM_ROW, MASK_ROW, VEC_ROW, JOINT_ROWS = NN, NN + 1, NN + 2, 32
D0, OUT0, IN0 = 0, NN, 2 * NN
LO0, LI0 = 0, NN


def is_even(axis):
    return lax.axis_index(axis) % 2 == 0


def pack_far_sector(field, v, tb):
    _, planes, sectors, _ = field.shape
    up = is_even("az")
    for z in range(planes):
        first, last = field[v, z, pl.ds(0, 1), :], field[v, z, pl.ds(sectors - 1, 1), :]
        tb[v, pl.ds(z, 1), :] = jnp.where(up, first, last)


def pack_edges(field, v, za, zb, ta):
    _, planes, sectors, _ = field.shape
    z_up, t_up = is_even("ax"), is_even("az")
    za[v] = field[v, jnp.where(z_up, planes - 1, 0)]
    zb[v] = field[v, jnp.where(z_up, 0, planes - 1)]
    for z in range(planes):
        first, last = field[v, z, pl.ds(0, 1), :], field[v, z, pl.ds(sectors - 1, 1), :]
        ta[v, pl.ds(z, 1), :] = jnp.where(t_up, last, first)


def prelude_kernel(
    flow, coef, blank, index, coup, upw,
    u, coef_ref, mask_ref, place, cst, za, zb, ta, tb,
    blank_ref, index_ref, coup_ref, upw_ref, sem,
):
    pairs = (
        (flow, u),
        (coup, coup_ref),
        (upw, upw_ref),
        (index, index_ref),
        (blank, blank_ref),
        (coef, coef_ref),
    )
    copies = [pltpu.make_async_copy(src, dst, sem.at[i]) for i, (src, dst) in enumerate(pairs)]
    for copy in copies:
        copy.start()
    _, planes, sectors, radial = u.shape
    copies[1].wait()
    copies[2].wait()
    a, b = splat_consts(coup_ref, upw_ref)
    store_mat(cst, 0, 0, a)
    store_mat(cst, 1, 0, b)
    copies[3].wait()
    place[...] = table_place(index_ref[...])
    copies[4].wait()
    mask_ref[...] = blank_ref[...].astype(F32).reshape(planes * sectors, radial)
    copies[5].wait()
    copies[0].wait()
    for v in range(N):
        pack_edges(u, v, za, zb, ta)
        pack_far_sector(u, v, tb)


def append_kernel(low, high, out):
    half = low.shape[1]
    out[:, pl.ds(0, half), :] = low[...]
    out[:, pl.ds(half, half), :] = high[...]


def factor_kernel(coef_ref, mask_ref, cst, m1, f1, scal, sd, mask_t, lam_t, face, pw):
    mask = mask_ref[...]
    lam = coef_ref[...].reshape(LANES, 2 * HALF * SEG) * mask
    lam_t[...] = lam.T
    mask_t[...] = mask.T
    a, b = load_mat(cst, 0, 0), load_mat(cst, 1, 0)
    for which, mat in enumerate((mat_mul(a, a), mat_mul(b, b), mat_mul(a, b), mat_mul(b, a))):
        store_mat(pw, which, 0, mat)

    sub = lax.broadcasted_iota(jnp.int32, (SEG, LANES), 0)
    first_lam, first_mask = strided(lam_t, 0), strided(mask_t, 0)
    lam_k, mask_k = first_lam, first_mask
    for k in range(2 * HALF):
        if k < 2 * HALF - 1:
            lam_n, mask_n = strided(lam_t, k + 1), strided(mask_t, k + 1)
            f = 0.5 * (lam_k * mask_n + lam_n * mask_k)
        else:
            lam_n, mask_n = up(first_lam, 1), up(first_mask, 1)
            f = jnp.where(sub == SEG - 1, 0.0, 0.5 * (lam_k * mask_n + lam_n * mask_k))
        face[k + 1] = f
        lam_k, mask_k = lam_n, mask_n
    face[0] = down(face[2 * HALF], 1)

    def build_odd(m, c):
        fl, fr = face[2 * m + 1], face[2 * m + 2]
        scal[m, 0] = 1.0 / (1.0 + 0.5 * (fl + fr))
        scal[m, 1] = fl
        scal[m, 2] = fr
        return c

    lax.fori_loop(0, HALF, build_odd, 0)

    def build_even(p, c):
        prev = jnp.where(p == 0, HALF - 1, p - 1)
        inv, fl, fr = scal[p, 0], scal[p, 1], scal[p, 2]
        inv_p, fl_p, fr_p = scal[prev, 0], scal[prev, 1], scal[prev, 2]
        beta = fr_p * fr_p * inv_p
        delta = fr_p * fl_p * inv_p
        beta = jnp.where(p == 0, down(beta, 1), beta)
        alpha = fl * fl * inv
        gamma = fl * fr * inv
        d = 1.0 + 0.5 * (face[2 * p] + face[2 * p + 1])
        for i in range(N):
            for j in range(N):
                e = i * N + j
                val = -(alpha * pw[2, e] + beta * pw[3, e])
                m1[p, D0 + e] = d + val if i == j else val
                m1[p, OUT0 + e] = gamma * pw[0, e]
                m1[p, IN0 + e] = delta * pw[1, e]
        return c

    lax.fori_loop(0, HALF, build_even, 0)
    last = scal[HALF - 1, 1] * scal[HALF - 1, 2] * scal[HALF - 1, 0]
    for e in range(NN):
        m1[HALF, D0 + e] = jnp.zeros((SEG, LANES), F32)
        m1[HALF, OUT0 + e] = jnp.zeros((SEG, LANES), F32)
        m1[HALF, IN0 + e] = last * pw[1, e]

    sd[...] = jnp.zeros((JOINT_ROWS, LANES), F32)
    sd[pl.ds(LAM_ROW, 1), :] = first_lam[0:1]
    sd[pl.ds(MASK_ROW, 1), :] = first_mask[0:1]

    def step(i, c):
        eliminate(m1, f1, 1, 2 * i + 1, i)
        return c

    lax.fori_loop(0, HALF // 2, step, 0)


def eliminate(mb, mf, s, sm, fm):
    sp, sq = sm - s, sm + s
    di = invert(load_mat(mb, sm, D0))
    store_mat(mb, sm, D0, di)
    for i in range(N):
        row = load_row(mb, sp, OUT0, i)
        for j in range(N):
            mf[fm, LO0 + i * N + j] = dot_row(row, di, j)
        row = load_row(mb, sq, IN0, i)
        for j in range(N):
            mf[fm, LI0 + i * N + j] = dot_row(row, di, j)
    in_m = load_mat(mb, sm, IN0)
    for i in range(N):
        row = load_row(mf, fm, LO0, i)
        for j in range(N):
            e = i * N + j
            mb[sp, D0 + e] = mb[sp, D0 + e] - dot_row(row, in_m, j)
        row = load_row(mf, fm, LI0, i)
        for j in range(N):
            mb[sq, IN0 + i * N + j] = dot_row(row, in_m, j)
    out_m = load_mat(mb, sm, OUT0)
    for i in range(N):
        row = load_row(mf, fm, LI0, i)
        for j in range(N):
            e = i * N + j
            mb[sq, D0 + e] = mb[sq, D0 + e] - dot_row(row, out_m, j)
        row = load_row(mf, fm, LO0, i)
        for j in range(N):
            mb[sp, OUT0 + i * N + j] = dot_row(row, out_m, j)


def factor_rest_kernel(m1, sd_in, mb, mf, sd):
    def fetch(q, c):
        for e in range(3 * NN):
            mb[slot_of(q), e] = m1[2 * q, e]
        return c

    lax.fori_loop(0, HALF // 2 + 1, fetch, 0)

    def step(it, c):
        s = jnp.where(it < 4, 1, jnp.where(it < 6, 2, 4))
        first = jnp.where(it < 4, 0, jnp.where(it < 6, 4, 6))
        q = s * (2 * (it - first) + 1)
        eliminate(mb, mf, s, slot_of(q), slot_of(q))
        return c

    lax.fori_loop(0, HALF // 2 - 1, step, 0)
    sd[...] = sd_in[...]
    s0, s16 = slot_of(0), slot_of(HALF // 2)
    for e in range(NN):
        mb[0, D0 + e] = mb[s0, D0 + e] + down(mb[s16, D0 + e], 1)
        mb[0, OUT0 + e] = mb[s0, OUT0 + e]
        mb[0, IN0 + e] = down(mb[s16, IN0 + e], 1)
    for level, s in enumerate((1, 2, 4)):
        d = load_mat(mb, level, D0)
        di = invert(d)
        store_mat(mb, level, D0, di)
        di_up = [[up(di[i][j], s) for j in range(N)] for i in range(N)]
        for i in range(N):
            row = load_row(mb, level, OUT0, i)
            for j in range(N):
                mf[level, LO0 + i * N + j] = dot_row(row, di_up, j)
        di_down = [[down(di[i][j], s) for j in range(N)] for i in range(N)]
        for i in range(N):
            row = load_row(mb, level, IN0, i)
            for j in range(N):
                mf[level, LI0 + i * N + j] = dot_row(row, di_down, j)
        in_up = [[up(mb[level, IN0 + i * N + j], s) for j in range(N)] for i in range(N)]
        acc = []
        for i in range(N):
            row = load_row(mf, level, LO0, i)
            acc.append([d[i][j] - dot_row(row, in_up, j) for j in range(N)])
        out_down = [[down(mb[level, OUT0 + i * N + j], s) for j in range(N)] for i in range(N)]
        for i in range(N):
            row = load_row(mf, level, LI0, i)
            for j in range(N):
                val = acc[i][j] - dot_row(row, out_down, j)
                if level < 2:
                    mb[level + 1, D0 + i * N + j] = val
                else:
                    sd[pl.ds(i * N + j, 1), :] = val[0:1]
        if level < 2:
            out_up = [[up(mb[level, OUT0 + i * N + j], s) for j in range(N)] for i in range(N)]
            for i in range(N):
                row = load_row(mf, level, LO0, i)
                for j in range(N):
                    mb[level + 1, OUT0 + i * N + j] = dot_row(row, out_up, j)
            in_down = [[down(mb[level, IN0 + i * N + j], s) for j in range(N)] for i in range(N)]
            for i in range(N):
                row = load_row(mf, level, LI0, i)
                for j in range(N):
                    mb[level + 1, IN0 + i * N + j] = dot_row(row, in_down, j)


def join(own_ref, other_ref, j_ref):
    lam, mask = own_ref[pl.ds(LAM_ROW, 1), :], own_ref[pl.ds(MASK_ROW, 1), :]
    other_lam, other_mask = other_ref[pl.ds(LAM_ROW, 1), :], other_ref[pl.ds(MASK_ROW, 1), :]
    c = 0.25 * (lam * other_mask + other_lam * mask)

    def total(ref):
        mat = [[ref[pl.ds(i * N + j, 1), :] for j in range(N)] for i in range(N)]
        return [[mat[i][j] + c if i == j else mat[i][j] for j in range(N)] for i in range(N)]

    own, inv_other = total(own_ref), invert(total(other_ref))
    schur = [[own[i][j] - c * (c * inv_other[i][j]) for j in range(N)] for i in range(N)]
    j1 = invert(schur)
    j2 = mat_mul(j1, inv_other)
    for i in range(N):
        for j in range(N):
            j_ref[pl.ds(i * N + j, 1), :] = j1[i][j]
            j_ref[pl.ds(NN + i * N + j, 1), :] = c * j2[i][j]


def plane_neighbours(za, zb, v):
    z_up = is_even("ax")
    return jnp.where(z_up, zb[v], za[v]), jnp.where(z_up, za[v], zb[v])


def stencil_block(u, v, z, before, after, ta, tb):
    planes, sectors = u.shape[1], u.shape[2]
    t_up = is_even("az")
    cur = u[v, z]
    rows = lax.broadcasted_iota(jnp.int32, cur.shape, 0)
    behind = u[v, z - 1] if z > 0 else before
    ahead = u[v, z + 1] if z < planes - 1 else after
    t_a, t_b = ta[v, pl.ds(z, 1), :], tb[v, pl.ds(z, 1), :]
    before_t = jnp.where(rows == 0, jnp.where(t_up, t_b, t_a), pltpu.roll(cur, 1, 0))
    after_t = jnp.where(rows == sectors - 1, jnp.where(t_up, t_a, t_b), pltpu.roll(cur, sectors - 1, 0))
    return (before_t + after_t) + (1.5 * behind + 0.5 * ahead) - 4.0 * cur


def forward_body(rhs_t, f1, f2, scal, cst, e_ref, o_ref):
    a, b = load_mat(cst, 0, 0), load_mat(cst, 1, 0)
    zero = jnp.zeros((SEG, LANES), F32)
    carry = [zero] * N
    first = None
    for m in range(HALF):
        inv, fl, fr = scal[m, 0], scal[m, 1], scal[m, 2]
        odd = [strided(rhs_t.at[v], 2 * m + 1) for v in range(N)]
        scaled = [x * inv for x in odd]
        ta = mat_vec(a, scaled)
        tb = mat_vec(b, scaled)
        for v in range(N):
            o_ref[m, v] = odd[v]
            e_ref[m, v] = strided(rhs_t.at[v], 2 * m) + carry[v] + fl * ta[v]
        carry = [fr * tb[v] for v in range(N)]
    for v in range(N):
        e_ref[0, v] = e_ref[0, v] + down(carry[v], 1)
        e_ref[HALF, v] = zero
    for m, s in STEPS:
        vec = [e_ref[m, v] for v in range(N)]
        mf, slot = (f1, m // 2) if s == 1 else (f2, slot_of(m // 2))
        lo = mat_vec(load_mat(mf, slot, LO0), vec)
        li = mat_vec(load_mat(mf, slot, LI0), vec)
        for v in range(N):
            e_ref[m - s, v] = e_ref[m - s, v] + lo[v]
            e_ref[m + s, v] = e_ref[m + s, v] + li[v]
    cur = [e_ref[0, v] + down(e_ref[HALF, v], 1) for v in range(N)]
    for level, s in enumerate((1, 2, 4)):
        for v in range(N):
            e_ref[HALF + 1 + level, v] = cur[v]
        lo = mat_vec(load_mat(f2, level, LO0), [up(x, s) for x in cur])
        li = mat_vec(load_mat(f2, level, LI0), [down(x, s) for x in cur])
        cur = [cur[v] + lo[v] + li[v] for v in range(N)]
    return [cur[v][0:1] for v in range(N)]


def doubling_bits():
    return [bit for bit in (24, 8, 4, 2, 1) if bit < lax.axis_size("az")]


def table_place(index):
    apart = lax.shift_right_logical(index, 2) ^ lax.axis_index("az")
    block = jnp.zeros_like(apart)
    for i, bit in enumerate(doubling_bits()):
        used = (apart & (1 << (bit.bit_length() - 1))) != 0
        apart = jnp.where(used, apart ^ bit, apart)
        block = block | (jnp.where(used, 1, 0) << i)
    return block * 4 + (index & 3)


def one_hot(place, start, count):
    planes, sectors = place.shape
    rows = start + lax.broadcasted_iota(jnp.int32, (count, sectors), 0)
    hot = [jnp.where(rows == place[pl.ds(z, 1), :], 1.0, 0.0) for z in range(planes)]
    hot = jnp.concatenate(hot, axis=1)
    return jnp.concatenate([hot, hot, hot], axis=0).astype(jnp.bfloat16)


def pick(rows, hot):
    high = rows.astype(jnp.bfloat16)
    rest = rows - high.astype(F32)
    middle = rest.astype(jnp.bfloat16)
    low = (rest - middle.astype(F32)).astype(jnp.bfloat16)
    return lax.dot_general(
        jnp.concatenate([high, middle, low], axis=0),
        hot,
        (((0,), (0,)), ((), ())),
        preferred_element_type=F32,
    )


def rhs_kernel(u, za, zb, ta, tb, mask_ref, mask_t, place, low, rhs_t):
    planes = u.shape[1]
    mask = mask_ref[...]
    hot = one_hot(place, 0, low.shape[1])
    for v in range(N):
        before, after = plane_neighbours(za, zb, v)
        blocks = [stencil_block(u, v, z, before, after, ta, tb) for z in range(planes)]
        rhs_t[v] = (mask * jnp.concatenate(blocks, axis=0)).T + mask_t[...] * pick(low[v], hot)


def forward_first_kernel(
    rhs_in, mask_t, place, high, f1, f2, scal, cst, sd, e_ref, o_ref, joint, rhs_t
):
    hot = one_hot(place, high.shape[1], high.shape[1])
    for v in range(N):
        rhs_t[v] = rhs_in[v] + mask_t[...] * pick(high[v], hot)
    reduced = forward_body(rhs_t, f1, f2, scal, cst, e_ref, o_ref)
    joint[...] = sd[...]
    for v in range(N):
        joint[pl.ds(VEC_ROW + v, 1), :] = reduced[v]


def forward_second_kernel(
    u, za, zb, tb, ta, mask_ref, f1, f2, scal, cst, e_ref, o_ref, y_ref, rhs_t
):
    planes = u.shape[1]
    mask = mask_ref[...]
    for v in range(N):
        before, after = plane_neighbours(za, zb, v)
        blocks = [stencil_block(u, v, z, before, after, ta, tb) for z in range(planes)]
        rhs_t[v] = (mask * jnp.concatenate(blocks, axis=0)).T
    reduced = forward_body(rhs_t, f1, f2, scal, cst, e_ref, o_ref)
    y_ref[...] = jnp.zeros((SEG, LANES), F32)
    for v in range(N):
        y_ref[pl.ds(v, 1), :] = reduced[v]


def backward_body(own, other, j_ref, m1, m2, scal, cst, e_ref, o_ref, x_ref, x_t):
    a, b = load_mat(cst, 0, 0), load_mat(cst, 1, 0)
    sub = lax.broadcasted_iota(jnp.int32, (SEG, LANES), 0)
    cur = []
    for i in range(N):
        acc = j_ref[pl.ds(i * N, 1), :] * own[0]
        for k in range(N):
            if k > 0:
                acc = acc + j_ref[pl.ds(i * N + k, 1), :] * own[k]
            acc = acc + j_ref[pl.ds(NN + i * N + k, 1), :] * other[k]
        cur.append(jnp.broadcast_to(acc, (SEG, LANES)))

    def recover(mb, slot, rhs, high, low):
        o = mat_vec(load_mat(mb, slot, OUT0), high)
        i = mat_vec(load_mat(mb, slot, IN0), low)
        total = [e_ref[rhs, v] + o[v] + i[v] for v in range(N)]
        return mat_vec(load_mat(mb, slot, D0), total)

    for level, s in ((2, 4), (1, 2), (0, 1)):
        new = recover(m2, level, HALF + 1 + level, [up(x, s) for x in cur], [down(x, s) for x in cur])
        cur = [jnp.where(sub % (2 * s) == s, new[v], cur[v]) for v in range(N)]
    for v in range(N):
        x_ref[0, v] = cur[v]
        x_ref[HALF, v] = up(cur[v], 1)
    for m, s in reversed(STEPS):
        mb, slot = (m1, m) if s == 1 else (m2, slot_of(m // 2))
        new = recover(
            mb, slot, m, [x_ref[m + s, v] for v in range(N)], [x_ref[m - s, v] for v in range(N)]
        )
        for v in range(N):
            x_ref[m, v] = new[v]
    low = [x_ref[0, v] for v in range(N)]
    for m in range(HALF):
        inv, fl, fr = scal[m, 0], scal[m, 1], scal[m, 2]
        high = [x_ref[m + 1, v] for v in range(N)]
        ta = mat_vec(a, high)
        tb = mat_vec(b, low)
        for v in range(N):
            odd = inv * (o_ref[m, v] + fr * ta[v] + fl * tb[v])
            x_t.at[v][pl.ds(2 * m, SEG, stride=2 * HALF), :] = low[v]
            x_t.at[v][pl.ds(2 * m + 1, SEG, stride=2 * HALF), :] = odd
        low = high


def backward_first_kernel(
    joint, other_joint, m1, m2, scal, cst, e_ref, o_ref,
    out, za, zb, ta, tb, j_ref, x_ref, x_t,
):
    join(joint, other_joint, j_ref)
    own = [joint[pl.ds(VEC_ROW + v, 1), :] for v in range(N)]
    other = [other_joint[pl.ds(VEC_ROW + v, 1), :] for v in range(N)]
    backward_body(own, other, j_ref, m1, m2, scal, cst, e_ref, o_ref, x_ref, x_t)
    _, planes, sectors, radial = out.shape
    for v in range(N):
        out[v] = x_t[v].T.reshape(planes, sectors, radial)
        pack_edges(out, v, za, zb, ta)
        pack_far_sector(out, v, tb)


def backward_second_kernel(
    y_own, y_other, j_ref, m1, m2, scal, cst, e_ref, o_ref, first, out, x_ref, x_t, stage, sem
):
    own = [y_own[pl.ds(v, 1), :] for v in range(N)]
    other = [y_other[pl.ds(v, 1), :] for v in range(N)]
    backward_body(own, other, j_ref, m1, m2, scal, cst, e_ref, o_ref, x_ref, x_t)
    _, planes, sectors, radial = out.shape
    copies = [pltpu.make_async_copy(stage.at[v], out.at[v], sem.at[v]) for v in range(N)]
    for v in range(N):
        stage[v] = first[v] + 0.5 * x_t[v].T.reshape(planes, sectors, radial)
        copies[v].start()
    for copy in copies:
        copy.wait()


def call(kernel, inputs, outs, scratch, us, hbm=False, out_hbm=False):
    vmem = pl.BlockSpec(memory_space=pltpu.VMEM)
    if hbm:
        inputs = [pltpu.with_memory_space_constraint(x, pltpu.HBM) for x in inputs]
    in_spec = pl.BlockSpec(memory_space=pltpu.HBM) if hbm else vmem
    out_shape = [s if isinstance(s, jax.ShapeDtypeStruct) else jax.ShapeDtypeStruct(s, F32) for s in outs]
    return pl.pallas_call(
        kernel,
        out_shape=out_shape,
        in_specs=[in_spec] * len(inputs),
        out_specs=[pl.BlockSpec(memory_space=pltpu.HBM) if out_hbm else vmem] * len(outs),
        scratch_shapes=[pltpu.VMEM(s, F32) if isinstance(s, tuple) else s for s in scratch],
        compiler_params=pltpu.CompilerParams(vmem_limit_bytes=VMEM_LIMIT),
        cost_estimate=pl.CostEstimate(
            flops=int(us * 1e9), bytes_accessed=int(us * 3e6), transcendentals=0
        ),
    )(*inputs)


def swapped_along(x, axis, odd, wrap):
    size = lax.axis_size(axis)
    pairs = []
    for i in range(odd, size, 2):
        if wrap or i + 1 < size:
            j = (i + 1) % size
            pairs += [(i, j), (j, i)]
    return lax.ppermute(x, axis, pairs)


def z_near(x):
    return swapped_along(x, "ax", 0, False)


def z_far(x):
    return swapped_along(x, "ax", 1, False)


def t_near(x):
    return swapped_along(x, "az", 0, True)


def t_far(x):
    return swapped_along(x, "az", 1, True)


def xor_swap(x, bit):
    return lax.ppermute(x, "az", [(i, i ^ bit) for i in range(lax.axis_size("az"))])


def append(low, high):
    (both,) = call(append_kernel, (low, high), [(N, 2 * low.shape[1], low.shape[2])], [], 0.2)
    return both


def after(x, *others):
    return lax.optimization_barrier((x, *others))[0]


def per_device(
    flow_state, radial_coef, blanking, canard_index, canard_table, coupling, upwind_split
):
    comps, planes, sectors, radial = flow_state.shape
    tile = (SEG, LANES)
    half_turn = lax.axis_size("az") // 2
    field = (comps, planes, sectors, radial)
    edges = [(comps, sectors, radial)] * 2 + [(comps, planes, radial)] * 2
    columns = (comps, radial, LANES)
    bits = doubling_bits()

    rows = canard_table[0].transpose(1, 0, 2)
    got = xor_swap(rows, bits[0])
    u, coef, mask, place, cst, za, zb, ta, tb = call(
        prelude_kernel,
        (flow_state, radial_coef, blanking, canard_index, coupling, upwind_split),
        [
            field,
            (planes, sectors, radial),
            (LANES, radial),
            jax.ShapeDtypeStruct(canard_index.shape, jnp.int32),
            (2, NN) + tile,
        ]
        + edges,
        [
            pltpu.VMEM((planes, sectors, radial), jnp.int32),
            pltpu.VMEM(canard_index.shape, jnp.int32),
            pltpu.SMEM((N, N), F32),
            pltpu.SMEM((N,), F32),
            pltpu.SemaphoreType.DMA((6,)),
        ],
        1.2,
        hbm=True,
    )
    rows = append(rows, after(got, cst))
    halo, done = {"za": z_near(za), "zb": z_far(zb)}, []

    def factor(rows, got):
        done.extend(
            call(
                factor_kernel,
                (after(coef, rows), mask, cst),
                [
                    (HALF + 1, 3 * NN) + tile,
                    (HALF // 2, 2 * NN) + tile,
                    (HALF, 3) + tile,
                    (JOINT_ROWS, LANES),
                    (radial, LANES),
                ],
                [(radial, LANES), (2 * HALF + 1,) + tile, (4, NN) + tile],
                3.2,
            )
        )
        return after(got, done[3])

    def sector_halos(rows, got):
        halo["tb"], halo["ta"] = t_far(after(tb, rows)), t_near(after(ta, rows))
        return after(got, halo["za"], halo["zb"])

    def factor_rest(rows, got):
        m1, sd = done[0], done[3]
        done.extend(
            call(
                factor_rest_kernel,
                (after(m1, rows), sd),
                [
                    (HALF // 2 + 3, 3 * NN) + tile,
                    (HALF // 2 + 2, 2 * NN) + tile,
                    (JOINT_ROWS, LANES),
                ],
                [],
                3.0,
            )
        )
        return after(got, done[-1], halo["ta"], halo["tb"])

    fillers = [factor, sector_halos, factor_rest]
    for i, bit in enumerate(bits[1:-1]):
        rows = append(rows, fillers[i](rows, xor_swap(rows, bit)))
    for filler in fillers[len(bits) - 2 :]:
        rows = filler(rows, rows)
    m1, f1, scal, _, mask_t, m2, f2, sd = done
    others = xor_swap(rows, bits[-1])
    (rhs,) = call(
        rhs_kernel,
        (u, halo["za"], halo["zb"], halo["ta"], halo["tb"], mask, mask_t, place, rows),
        [columns],
        [],
        1.3,
    )
    others = after(others, rhs)

    fwd_outs = [(HALF + 4, N) + tile, (HALF, N) + tile]
    back_scratch = [(HALF + 1, N) + tile, columns]
    e1, o1, joint = call(
        forward_first_kernel,
        (rhs, mask_t, place, others, f1, f2, scal, cst, sd),
        fwd_outs + [(JOINT_ROWS, LANES)],
        [columns],
        1.2,
    )
    other_joint = xor_swap(joint, half_turn)
    delta, za, zb, ta, tb, axis_inverse = call(
        backward_first_kernel,
        (joint, other_joint, m1, m2, scal, cst, e1, o1),
        [field] + edges + [(2 * NN, LANES)],
        back_scratch,
        1.3,
    )
    tb, zb, za, ta = t_far(tb), z_far(zb), z_near(za), t_near(ta)
    e2, o2, y2 = call(
        forward_second_kernel,
        (delta, za, zb, tb, ta, mask, f1, f2, scal, cst),
        fwd_outs + [tile],
        [columns],
        1.3,
    )
    other_y2 = xor_swap(y2, half_turn)
    (update,) = call(
        backward_second_kernel,
        (y2, other_y2, axis_inverse, m1, m2, scal, cst, e2, o2, delta),
        [field],
        back_scratch + [field, pltpu.SemaphoreType.DMA((N,))],
        2.0,
        out_hbm=True,
    )
    return update


def solution(mesh):
    return jax.shard_map(
        per_device,
        mesh=mesh,
        in_specs=(
            P(None, "ax", "az", None),
            P("ax", "az", None),
            P("ax", "az", None),
            P("ax", "az"),
            P("ax", "az", None, None),
            P(),
            P(),
        ),
        out_specs=P(None, "ax", "az", None),
        check_vma=False,
    )
```

```python
import jax
import jax.numpy as jnp
from jax import lax
from jax.experimental import pallas as pl
from jax.experimental.pallas import tpu as pltpu
from jax.sharding import PartitionSpec as P

N = 5
NN = 25
SEG = 8
LANES = 128
HALF = 16
VMEM_LIMIT = 16 * 1024 * 1024
F32 = jnp.float32
STEPS = [(s * (2 * i + 1), s) for s in (1, 2, 4, 8) for i in range(8 // s)]


def up(x, s):
    return pltpu.roll(x, SEG - s, 0)


def down(x, s):
    return pltpu.roll(x, s, 0)


def splat_consts(coupling_ref, upwind_ref):
    shape = (SEG, LANES)
    p = [[jnp.full(shape, coupling_ref[i, j], F32) for j in range(N)] for i in range(N)]
    w = [jnp.full(shape, upwind_ref[i], F32) for i in range(N)]
    a = [[p[i][j] + w[i] if i == j else p[i][j] for j in range(N)] for i in range(N)]
    b = [[(1.0 - w[i]) - p[j][i] if i == j else -p[j][i] for j in range(N)] for i in range(N)]
    return a, b


def dot_row(row, cols, j):
    acc = row[0] * cols[0][j]
    for k in range(1, N):
        acc = acc + row[k] * cols[k][j]
    return acc


def mat_mul(x, y):
    return [[dot_row(x[i], y, j) for j in range(N)] for i in range(N)]


def mat_vec(x, v):
    out = []
    for row in x:
        t = [row[k] * v[k] for k in range(N)]
        out.append((t[0] + t[1]) + (t[2] + t[3]) + t[4])
    return out


def invert(matrix):
    m = [list(row) for row in matrix]
    for p in range(N):
        piv = 1.0 / m[p][p]
        m[p] = [piv if j == p else m[p][j] * piv for j in range(N)]
        for i in range(N):
            if i != p:
                f = m[i][p]
                m[i] = [-(f * piv) if j == p else m[i][j] - f * m[p][j] for j in range(N)]
    return m


def load_mat(ref, slot, base):
    return [[ref[slot, base + i * N + j] for j in range(N)] for i in range(N)]


def load_row(ref, slot, base, i):
    return [ref[slot, base + i * N + j] for j in range(N)]


def store_mat(ref, slot, base, mat):
    for i in range(N):
        for j in range(N):
            ref[slot, base + i * N + j] = mat[i][j]


def strided(ref, k):
    return ref[pl.ds(k, SEG, stride=2 * HALF), :]


def slot_of(q):
    return q + 2


LAM_ROW, MASK_ROW, VEC_ROW, JOINT_ROWS = NN, NN + 1, NN + 2, 32
D0, OUT0, IN0 = 0, NN, 2 * NN
LO0, LI0 = 0, NN


def is_even(axis):
    return lax.axis_index(axis) % 2 == 0


def pack_far_sector(field, v, tb):
    _, planes, sectors, _ = field.shape
    up = is_even("az")
    for z in range(planes):
        first, last = field[v, z, pl.ds(0, 1), :], field[v, z, pl.ds(sectors - 1, 1), :]
        tb[v, pl.ds(z, 1), :] = jnp.where(up, first, last)


def pack_edges(field, v, za, zb, ta):
    _, planes, sectors, _ = field.shape
    z_up, t_up = is_even("ax"), is_even("az")
    za[v] = field[v, jnp.where(z_up, planes - 1, 0)]
    zb[v] = field[v, jnp.where(z_up, 0, planes - 1)]
    for z in range(planes):
        first, last = field[v, z, pl.ds(0, 1), :], field[v, z, pl.ds(sectors - 1, 1), :]
        ta[v, pl.ds(z, 1), :] = jnp.where(t_up, last, first)


def prelude_kernel(
    flow, coef, blank, index, coup, upw,
    u, coef_ref, mask_ref, place, cst, za, zb, ta, tb,
    blank_ref, index_ref, coup_ref, upw_ref, sem,
):
    pairs = (
        (flow, u),
        (coup, coup_ref),
        (upw, upw_ref),
        (index, index_ref),
        (blank, blank_ref),
        (coef, coef_ref),
    )
    copies = [pltpu.make_async_copy(src, dst, sem.at[i]) for i, (src, dst) in enumerate(pairs)]
    for copy in copies:
        copy.start()
    _, planes, sectors, radial = u.shape
    copies[1].wait()
    copies[2].wait()
    a, b = splat_consts(coup_ref, upw_ref)
    store_mat(cst, 0, 0, a)
    store_mat(cst, 1, 0, b)
    copies[3].wait()
    place[...] = table_place(index_ref[...])
    copies[4].wait()
    mask_ref[...] = blank_ref[...].astype(F32).reshape(planes * sectors, radial)
    copies[5].wait()
    copies[0].wait()
    for v in range(N):
        pack_edges(u, v, za, zb, ta)
        pack_far_sector(u, v, tb)


def append_kernel(low, high, out):
    half = low.shape[1]
    out[:, pl.ds(0, half), :] = low[...]
    out[:, pl.ds(half, half), :] = high[...]


def factor_kernel(coef_ref, mask_ref, cst, m1, f1, scal, sd, mask_t, lam_t, face, pw):
    mask = mask_ref[...]
    lam = coef_ref[...].reshape(LANES, 2 * HALF * SEG) * mask
    lam_t[...] = lam.T
    mask_t[...] = mask.T
    a, b = load_mat(cst, 0, 0), load_mat(cst, 1, 0)
    for which, mat in enumerate((mat_mul(a, a), mat_mul(b, b), mat_mul(a, b), mat_mul(b, a))):
        store_mat(pw, which, 0, mat)

    sub = lax.broadcasted_iota(jnp.int32, (SEG, LANES), 0)
    first_lam, first_mask = strided(lam_t, 0), strided(mask_t, 0)
    lam_k, mask_k = first_lam, first_mask
    for k in range(2 * HALF):
        if k < 2 * HALF - 1:
            lam_n, mask_n = strided(lam_t, k + 1), strided(mask_t, k + 1)
            f = 0.5 * (lam_k * mask_n + lam_n * mask_k)
        else:
            lam_n, mask_n = up(first_lam, 1), up(first_mask, 1)
            f = jnp.where(sub == SEG - 1, 0.0, 0.5 * (lam_k * mask_n + lam_n * mask_k))
        face[k + 1] = f
        lam_k, mask_k = lam_n, mask_n
    face[0] = down(face[2 * HALF], 1)

    def build_odd(m, c):
        fl, fr = face[2 * m + 1], face[2 * m + 2]
        scal[m, 0] = 1.0 / (1.0 + 0.5 * (fl + fr))
        scal[m, 1] = fl
        scal[m, 2] = fr
        return c

    lax.fori_loop(0, HALF, build_odd, 0)

    def build_even(p, c):
        prev = jnp.where(p == 0, HALF - 1, p - 1)
        inv, fl, fr = scal[p, 0], scal[p, 1], scal[p, 2]
        inv_p, fl_p, fr_p = scal[prev, 0], scal[prev, 1], scal[prev, 2]
        beta = fr_p * fr_p * inv_p
        delta = fr_p * fl_p * inv_p
        beta = jnp.where(p == 0, down(beta, 1), beta)
        alpha = fl * fl * inv
        gamma = fl * fr * inv
        d = 1.0 + 0.5 * (face[2 * p] + face[2 * p + 1])
        for i in range(N):
            for j in range(N):
                e = i * N + j
                val = -(alpha * pw[2, e] + beta * pw[3, e])
                m1[p, D0 + e] = d + val if i == j else val
                m1[p, OUT0 + e] = gamma * pw[0, e]
                m1[p, IN0 + e] = delta * pw[1, e]
        return c

    lax.fori_loop(0, HALF, build_even, 0)
    last = scal[HALF - 1, 1] * scal[HALF - 1, 2] * scal[HALF - 1, 0]
    for e in range(NN):
        m1[HALF, D0 + e] = jnp.zeros((SEG, LANES), F32)
        m1[HALF, OUT0 + e] = jnp.zeros((SEG, LANES), F32)
        m1[HALF, IN0 + e] = last * pw[1, e]

    sd[...] = jnp.zeros((JOINT_ROWS, LANES), F32)
    sd[pl.ds(LAM_ROW, 1), :] = first_lam[0:1]
    sd[pl.ds(MASK_ROW, 1), :] = first_mask[0:1]

    def step(i, c):
        eliminate(m1, f1, 1, 2 * i + 1, i)
        return c

    lax.fori_loop(0, HALF // 2, step, 0)


def eliminate(mb, mf, s, sm, fm):
    sp, sq = sm - s, sm + s
    di = invert(load_mat(mb, sm, D0))
    store_mat(mb, sm, D0, di)
    for i in range(N):
        row = load_row(mb, sp, OUT0, i)
        for j in range(N):
            mf[fm, LO0 + i * N + j] = dot_row(row, di, j)
        row = load_row(mb, sq, IN0, i)
        for j in range(N):
            mf[fm, LI0 + i * N + j] = dot_row(row, di, j)
    in_m = load_mat(mb, sm, IN0)
    for i in range(N):
        row = load_row(mf, fm, LO0, i)
        for j in range(N):
            e = i * N + j
            mb[sp, D0 + e] = mb[sp, D0 + e] - dot_row(row, in_m, j)
        row = load_row(mf, fm, LI0, i)
        for j in range(N):
            mb[sq, IN0 + i * N + j] = dot_row(row, in_m, j)
    out_m = load_mat(mb, sm, OUT0)
    for i in range(N):
        row = load_row(mf, fm, LI0, i)
        for j in range(N):
            e = i * N + j
            mb[sq, D0 + e] = mb[sq, D0 + e] - dot_row(row, out_m, j)
        row = load_row(mf, fm, LO0, i)
        for j in range(N):
            mb[sp, OUT0 + i * N + j] = dot_row(row, out_m, j)


def factor_rest_kernel(m1, sd_in, mb, mf, sd):
    def fetch(q, c):
        for e in range(3 * NN):
            mb[slot_of(q), e] = m1[2 * q, e]
        return c

    lax.fori_loop(0, HALF // 2 + 1, fetch, 0)

    def step(it, c):
        s = jnp.where(it < 4, 1, jnp.where(it < 6, 2, 4))
        first = jnp.where(it < 4, 0, jnp.where(it < 6, 4, 6))
        q = s * (2 * (it - first) + 1)
        eliminate(mb, mf, s, slot_of(q), slot_of(q))
        return c

    lax.fori_loop(0, HALF // 2 - 1, step, 0)
    sd[...] = sd_in[...]
    s0, s16 = slot_of(0), slot_of(HALF // 2)
    for e in range(NN):
        mb[0, D0 + e] = mb[s0, D0 + e] + down(mb[s16, D0 + e], 1)
        mb[0, OUT0 + e] = mb[s0, OUT0 + e]
        mb[0, IN0 + e] = down(mb[s16, IN0 + e], 1)
    for level, s in enumerate((1, 2, 4)):
        d = load_mat(mb, level, D0)
        di = invert(d)
        store_mat(mb, level, D0, di)
        di_up = [[up(di[i][j], s) for j in range(N)] for i in range(N)]
        for i in range(N):
            row = load_row(mb, level, OUT0, i)
            for j in range(N):
                mf[level, LO0 + i * N + j] = dot_row(row, di_up, j)
        di_down = [[down(di[i][j], s) for j in range(N)] for i in range(N)]
        for i in range(N):
            row = load_row(mb, level, IN0, i)
            for j in range(N):
                mf[level, LI0 + i * N + j] = dot_row(row, di_down, j)
        in_up = [[up(mb[level, IN0 + i * N + j], s) for j in range(N)] for i in range(N)]
        acc = []
        for i in range(N):
            row = load_row(mf, level, LO0, i)
            acc.append([d[i][j] - dot_row(row, in_up, j) for j in range(N)])
        out_down = [[down(mb[level, OUT0 + i * N + j], s) for j in range(N)] for i in range(N)]
        for i in range(N):
            row = load_row(mf, level, LI0, i)
            for j in range(N):
                val = acc[i][j] - dot_row(row, out_down, j)
                if level < 2:
                    mb[level + 1, D0 + i * N + j] = val
                else:
                    sd[pl.ds(i * N + j, 1), :] = val[0:1]
        if level < 2:
            out_up = [[up(mb[level, OUT0 + i * N + j], s) for j in range(N)] for i in range(N)]
            for i in range(N):
                row = load_row(mf, level, LO0, i)
                for j in range(N):
                    mb[level + 1, OUT0 + i * N + j] = dot_row(row, out_up, j)
            in_down = [[down(mb[level, IN0 + i * N + j], s) for j in range(N)] for i in range(N)]
            for i in range(N):
                row = load_row(mf, level, LI0, i)
                for j in range(N):
                    mb[level + 1, IN0 + i * N + j] = dot_row(row, in_down, j)


def join(own_ref, other_ref, j_ref):
    lam, mask = own_ref[pl.ds(LAM_ROW, 1), :], own_ref[pl.ds(MASK_ROW, 1), :]
    other_lam, other_mask = other_ref[pl.ds(LAM_ROW, 1), :], other_ref[pl.ds(MASK_ROW, 1), :]
    c = 0.25 * (lam * other_mask + other_lam * mask)

    def total(ref):
        mat = [[ref[pl.ds(i * N + j, 1), :] for j in range(N)] for i in range(N)]
        return [[mat[i][j] + c if i == j else mat[i][j] for j in range(N)] for i in range(N)]

    own, inv_other = total(own_ref), invert(total(other_ref))
    schur = [[own[i][j] - c * (c * inv_other[i][j]) for j in range(N)] for i in range(N)]
    j1 = invert(schur)
    j2 = mat_mul(j1, inv_other)
    for i in range(N):
        for j in range(N):
            j_ref[pl.ds(i * N + j, 1), :] = j1[i][j]
            j_ref[pl.ds(NN + i * N + j, 1), :] = c * j2[i][j]


def plane_neighbours(za, zb, v):
    z_up = is_even("ax")
    return jnp.where(z_up, zb[v], za[v]), jnp.where(z_up, za[v], zb[v])


def stencil_block(u, v, z, before, after, ta, tb):
    planes, sectors = u.shape[1], u.shape[2]
    t_up = is_even("az")
    cur = u[v, z]
    rows = lax.broadcasted_iota(jnp.int32, cur.shape, 0)
    behind = u[v, z - 1] if z > 0 else before
    ahead = u[v, z + 1] if z < planes - 1 else after
    t_a, t_b = ta[v, pl.ds(z, 1), :], tb[v, pl.ds(z, 1), :]
    before_t = jnp.where(rows == 0, jnp.where(t_up, t_b, t_a), pltpu.roll(cur, 1, 0))
    after_t = jnp.where(rows == sectors - 1, jnp.where(t_up, t_a, t_b), pltpu.roll(cur, sectors - 1, 0))
    return (before_t + after_t) + (1.5 * behind + 0.5 * ahead) - 4.0 * cur


def forward_body(rhs_t, f1, f2, scal, cst, e_ref, o_ref):
    a, b = load_mat(cst, 0, 0), load_mat(cst, 1, 0)
    zero = jnp.zeros((SEG, LANES), F32)
    carry = [zero] * N
    first = None
    for m in range(HALF):
        inv, fl, fr = scal[m, 0], scal[m, 1], scal[m, 2]
        odd = [strided(rhs_t.at[v], 2 * m + 1) for v in range(N)]
        scaled = [x * inv for x in odd]
        ta = mat_vec(a, scaled)
        tb = mat_vec(b, scaled)
        for v in range(N):
            o_ref[m, v] = odd[v]
            e_ref[m, v] = strided(rhs_t.at[v], 2 * m) + carry[v] + fl * ta[v]
        carry = [fr * tb[v] for v in range(N)]
    for v in range(N):
        e_ref[0, v] = e_ref[0, v] + down(carry[v], 1)
        e_ref[HALF, v] = zero
    for m, s in STEPS:
        vec = [e_ref[m, v] for v in range(N)]
        mf, slot = (f1, m // 2) if s == 1 else (f2, slot_of(m // 2))
        lo = mat_vec(load_mat(mf, slot, LO0), vec)
        li = mat_vec(load_mat(mf, slot, LI0), vec)
        for v in range(N):
            e_ref[m - s, v] = e_ref[m - s, v] + lo[v]
            e_ref[m + s, v] = e_ref[m + s, v] + li[v]
    cur = [e_ref[0, v] + down(e_ref[HALF, v], 1) for v in range(N)]
    for level, s in enumerate((1, 2, 4)):
        for v in range(N):
            e_ref[HALF + 1 + level, v] = cur[v]
        lo = mat_vec(load_mat(f2, level, LO0), [up(x, s) for x in cur])
        li = mat_vec(load_mat(f2, level, LI0), [down(x, s) for x in cur])
        cur = [cur[v] + lo[v] + li[v] for v in range(N)]
    return [cur[v][0:1] for v in range(N)]


def doubling_bits():
    return [bit for bit in (24, 8, 2, 4, 1) if bit < lax.axis_size("az")]


def table_place(index):
    apart = lax.shift_right_logical(index, 2) ^ lax.axis_index("az")
    block = jnp.zeros_like(apart)
    for i, bit in enumerate(doubling_bits()):
        used = (apart & (1 << (bit.bit_length() - 1))) != 0
        apart = jnp.where(used, apart ^ bit, apart)
        block = block | (jnp.where(used, 1, 0) << i)
    return block * 4 + (index & 3)


def one_hot(place, start, count):
    planes, sectors = place.shape
    rows = start + lax.broadcasted_iota(jnp.int32, (count, sectors), 0)
    hot = [jnp.where(rows == place[pl.ds(z, 1), :], 1.0, 0.0) for z in range(planes)]
    hot = jnp.concatenate(hot, axis=1)
    return jnp.concatenate([hot, hot, hot], axis=0).astype(jnp.bfloat16)


def pick(rows, hot):
    high = rows.astype(jnp.bfloat16)
    rest = rows - high.astype(F32)
    middle = rest.astype(jnp.bfloat16)
    low = (rest - middle.astype(F32)).astype(jnp.bfloat16)
    return lax.dot_general(
        jnp.concatenate([high, middle, low], axis=0),
        hot,
        (((0,), (0,)), ((), ())),
        preferred_element_type=F32,
    )


def rhs_kernel(u, za, zb, ta, tb, mask_ref, mask_t, place, low, rhs_t):
    planes = u.shape[1]
    mask = mask_ref[...]
    hot = one_hot(place, 0, low.shape[1])
    for v in range(N):
        before, after = plane_neighbours(za, zb, v)
        blocks = [stencil_block(u, v, z, before, after, ta, tb) for z in range(planes)]
        rhs_t[v] = (mask * jnp.concatenate(blocks, axis=0)).T + mask_t[...] * pick(low[v], hot)


def forward_first_kernel(
    rhs_in, mask_t, place, high, f1, f2, scal, cst, sd, e_ref, o_ref, joint, rhs_t
):
    hot = one_hot(place, high.shape[1], high.shape[1])
    for v in range(N):
        rhs_t[v] = rhs_in[v] + mask_t[...] * pick(high[v], hot)
    reduced = forward_body(rhs_t, f1, f2, scal, cst, e_ref, o_ref)
    joint[...] = sd[...]
    for v in range(N):
        joint[pl.ds(VEC_ROW + v, 1), :] = reduced[v]


def forward_second_kernel(
    u, za, zb, tb, ta, mask_ref, f1, f2, scal, cst, e_ref, o_ref, y_ref, rhs_t
):
    planes = u.shape[1]
    mask = mask_ref[...]
    for v in range(N):
        before, after = plane_neighbours(za, zb, v)
        blocks = [stencil_block(u, v, z, before, after, ta, tb) for z in range(planes)]
        rhs_t[v] = (mask * jnp.concatenate(blocks, axis=0)).T
    reduced = forward_body(rhs_t, f1, f2, scal, cst, e_ref, o_ref)
    y_ref[...] = jnp.zeros((SEG, LANES), F32)
    for v in range(N):
        y_ref[pl.ds(v, 1), :] = reduced[v]


def particular(m1, m2, e_ref, x_ref):
    sub = lax.broadcasted_iota(jnp.int32, (SEG, LANES), 0)
    cur = [jnp.zeros((SEG, LANES), F32)] * N

    def recover(mb, slot, rhs, high, low):
        o = mat_vec(load_mat(mb, slot, OUT0), high)
        i = mat_vec(load_mat(mb, slot, IN0), low)
        total = [e_ref[rhs, v] + (o[v] + i[v]) for v in range(N)]
        return mat_vec(load_mat(mb, slot, D0), total)

    for level, s in ((2, 4), (1, 2), (0, 1)):
        new = recover(m2, level, HALF + 1 + level, [up(x, s) for x in cur], [down(x, s) for x in cur])
        cur = [jnp.where(sub % (2 * s) == s, new[v], cur[v]) for v in range(N)]
    for v in range(N):
        x_ref[0, v] = cur[v]
        x_ref[HALF, v] = up(cur[v], 1)
    for m, s in reversed(STEPS):
        mb, slot = (m1, m) if s == 1 else (m2, slot_of(m // 2))
        new = recover(
            mb, slot, m, [x_ref[m + s, v] for v in range(N)], [x_ref[m - s, v] for v in range(N)]
        )
        for v in range(N):
            x_ref[m, v] = new[v]


def response(m1, m2, q):
    sub = lax.broadcasted_iota(jnp.int32, (SEG, LANES), 0)
    one, zero = jnp.ones((SEG, LANES), F32), jnp.zeros((SEG, LANES), F32)
    cur = [[one if i == j else zero for j in range(N)] for i in range(N)]

    def recover(mb, slot, high, low):
        o = mat_mul(load_mat(mb, slot, OUT0), high)
        i = mat_mul(load_mat(mb, slot, IN0), low)
        total = [[o[r][c] + i[r][c] for c in range(N)] for r in range(N)]
        return mat_mul(load_mat(mb, slot, D0), total)

    for level, s in ((2, 4), (1, 2), (0, 1)):
        high = [[up(x, s) for x in row] for row in cur]
        low = [[down(x, s) for x in row] for row in cur]
        new = recover(m2, level, high, low)
        cur = [
            [jnp.where(sub % (2 * s) == s, new[r][c], cur[r][c]) for c in range(N)] for r in range(N)
        ]
    store_mat(q, 0, 0, cur)
    store_mat(q, HALF, 0, [[up(x, 1) for x in row] for row in cur])

    def later(it, c):
        s = jnp.where(it < 1, 4, jnp.where(it < 3, 2, 1))
        n = s * (2 * (it - jnp.where(it < 1, 0, jnp.where(it < 3, 1, 3))) + 1)
        high, low = load_mat(q, 2 * (n + s), 0), load_mat(q, 2 * (n - s), 0)
        store_mat(q, 2 * n, 0, recover(m2, slot_of(n), high, low))
        return c

    lax.fori_loop(0, HALF // 2 - 1, later, 0)

    def first(it, c):
        m = 2 * it + 1
        store_mat(q, m, 0, recover(m1, m, load_mat(q, m + 1, 0), load_mat(q, m - 1, 0)))
        return c

    lax.fori_loop(0, HALF // 2, first, 0)


def response_kernel(m1, m2, e_ref, q, x_ref):
    particular(m1, m2, e_ref, x_ref)
    response(m1, m2, q)


def particular_kernel(m1, m2, e_ref, x_ref):
    particular(m1, m2, e_ref, x_ref)


def axis_value(own, other, j_ref):
    cur = []
    for i in range(N):
        acc = j_ref[pl.ds(i * N, 1), :] * own[0]
        for k in range(N):
            if k > 0:
                acc = acc + j_ref[pl.ds(i * N + k, 1), :] * own[k]
            acc = acc + j_ref[pl.ds(NN + i * N + k, 1), :] * other[k]
        cur.append(jnp.broadcast_to(acc, (SEG, LANES)))
    return cur


def backward_body(own, other, j_ref, q, part, scal, cst, o_ref, x_t):
    a, b = load_mat(cst, 0, 0), load_mat(cst, 1, 0)
    axis = axis_value(own, other, j_ref)

    def even(p):
        add = mat_vec(load_mat(q, p, 0), axis)
        return [part[p, v] + add[v] for v in range(N)]

    low = even(0)
    for m in range(HALF):
        inv, fl, fr = scal[m, 0], scal[m, 1], scal[m, 2]
        high = even(m + 1)
        ta = mat_vec(a, high)
        tb = mat_vec(b, low)
        for v in range(N):
            odd = inv * (o_ref[m, v] + fr * ta[v] + fl * tb[v])
            x_t.at[v][pl.ds(2 * m, SEG, stride=2 * HALF), :] = low[v]
            x_t.at[v][pl.ds(2 * m + 1, SEG, stride=2 * HALF), :] = odd
        low = high


def backward_first_kernel(
    joint, other_joint, q, part, scal, cst, o_ref,
    out, za, zb, ta, tb, j_ref, x_t,
):
    join(joint, other_joint, j_ref)
    own = [joint[pl.ds(VEC_ROW + v, 1), :] for v in range(N)]
    other = [other_joint[pl.ds(VEC_ROW + v, 1), :] for v in range(N)]
    backward_body(own, other, j_ref, q, part, scal, cst, o_ref, x_t)
    _, planes, sectors, radial = out.shape
    for v in range(N):
        out[v] = x_t[v].T.reshape(planes, sectors, radial)
        pack_edges(out, v, za, zb, ta)
        pack_far_sector(out, v, tb)


def backward_second_kernel(
    y_own, y_other, j_ref, q, part, scal, cst, o_ref, first, out, x_t, stage, sem
):
    own = [y_own[pl.ds(v, 1), :] for v in range(N)]
    other = [y_other[pl.ds(v, 1), :] for v in range(N)]
    backward_body(own, other, j_ref, q, part, scal, cst, o_ref, x_t)
    _, planes, sectors, radial = out.shape
    copies = [pltpu.make_async_copy(stage.at[v], out.at[v], sem.at[v]) for v in range(N)]
    for v in range(N):
        stage[v] = first[v] + 0.5 * x_t[v].T.reshape(planes, sectors, radial)
        copies[v].start()
    for copy in copies:
        copy.wait()


def call(kernel, inputs, outs, scratch, us, hbm=False, out_hbm=False):
    vmem = pl.BlockSpec(memory_space=pltpu.VMEM)
    if hbm:
        inputs = [pltpu.with_memory_space_constraint(x, pltpu.HBM) for x in inputs]
    in_spec = pl.BlockSpec(memory_space=pltpu.HBM) if hbm else vmem
    out_shape = [s if isinstance(s, jax.ShapeDtypeStruct) else jax.ShapeDtypeStruct(s, F32) for s in outs]
    return pl.pallas_call(
        kernel,
        out_shape=out_shape,
        in_specs=[in_spec] * len(inputs),
        out_specs=[pl.BlockSpec(memory_space=pltpu.HBM) if out_hbm else vmem] * len(outs),
        scratch_shapes=[pltpu.VMEM(s, F32) if isinstance(s, tuple) else s for s in scratch],
        compiler_params=pltpu.CompilerParams(vmem_limit_bytes=VMEM_LIMIT),
        cost_estimate=pl.CostEstimate(
            flops=int(us * 1e9), bytes_accessed=int(us * 3e6), transcendentals=0
        ),
    )(*inputs)


def swapped_along(x, axis, odd, wrap):
    size = lax.axis_size(axis)
    pairs = []
    for i in range(odd, size, 2):
        if wrap or i + 1 < size:
            j = (i + 1) % size
            pairs += [(i, j), (j, i)]
    return lax.ppermute(x, axis, pairs)


def z_near(x):
    return swapped_along(x, "ax", 0, False)


def z_far(x):
    return swapped_along(x, "ax", 1, False)


def t_near(x):
    return swapped_along(x, "az", 0, True)


def t_far(x):
    return swapped_along(x, "az", 1, True)


def xor_swap(x, bit):
    return lax.ppermute(x, "az", [(i, i ^ bit) for i in range(lax.axis_size("az"))])


def append(low, high):
    (both,) = call(append_kernel, (low, high), [(N, 2 * low.shape[1], low.shape[2])], [], 0.2)
    return both


def after(x, *others):
    return lax.optimization_barrier((x, *others))[0]


def per_device(
    flow_state, radial_coef, blanking, canard_index, canard_table, coupling, upwind_split
):
    comps, planes, sectors, radial = flow_state.shape
    tile = (SEG, LANES)
    half_turn = lax.axis_size("az") // 2
    field = (comps, planes, sectors, radial)
    edges = [(comps, sectors, radial)] * 2 + [(comps, planes, radial)] * 2
    columns = (comps, radial, LANES)
    bits = doubling_bits()

    rows = canard_table[0].transpose(1, 0, 2)
    got = xor_swap(rows, bits[0])
    u, coef, mask, place, cst, za, zb, ta, tb = call(
        prelude_kernel,
        (flow_state, radial_coef, blanking, canard_index, coupling, upwind_split),
        [
            field,
            (planes, sectors, radial),
            (LANES, radial),
            jax.ShapeDtypeStruct(canard_index.shape, jnp.int32),
            (2, NN) + tile,
        ]
        + edges,
        [
            pltpu.VMEM((planes, sectors, radial), jnp.int32),
            pltpu.VMEM(canard_index.shape, jnp.int32),
            pltpu.SMEM((N, N), F32),
            pltpu.SMEM((N,), F32),
            pltpu.SemaphoreType.DMA((6,)),
        ],
        1.2,
        hbm=True,
    )
    rows = append(rows, after(got, cst))
    halo, done = {"zb": z_far(zb)}, []

    def factor(rows, got):
        done.extend(
            call(
                factor_kernel,
                (after(coef, rows), mask, cst),
                [
                    (HALF + 1, 3 * NN) + tile,
                    (HALF // 2, 2 * NN) + tile,
                    (HALF, 3) + tile,
                    (JOINT_ROWS, LANES),
                    (radial, LANES),
                ],
                [(radial, LANES), (2 * HALF + 1,) + tile, (4, NN) + tile],
                3.2,
            )
        )
        return after(got, done[3])

    def sector_halos(rows, got):
        halo["tb"], halo["ta"] = t_far(after(tb, rows)), t_near(after(ta, rows))
        return after(got, halo["zb"])

    def factor_rest(rows, got):
        halo["za"] = z_near(after(za, rows))
        m1, sd = done[0], done[3]
        done.extend(
            call(
                factor_rest_kernel,
                (after(m1, rows), sd),
                [
                    (HALF // 2 + 3, 3 * NN) + tile,
                    (HALF // 2 + 2, 2 * NN) + tile,
                    (JOINT_ROWS, LANES),
                ],
                [],
                3.0,
            )
        )
        return after(got, done[-1], halo["ta"], halo["tb"], halo["za"])

    fillers = [factor, sector_halos, factor_rest]
    for i, bit in enumerate(bits[1:-1]):
        rows = append(rows, fillers[i](rows, xor_swap(rows, bit)))
    for filler in fillers[len(bits) - 2 :]:
        rows = filler(rows, rows)
    m1, f1, scal, _, mask_t, m2, f2, sd = done
    others = xor_swap(rows, bits[-1])
    (rhs,) = call(
        rhs_kernel,
        (u, halo["za"], halo["zb"], halo["ta"], halo["tb"], mask, mask_t, place, rows),
        [columns],
        [],
        1.3,
    )
    others = after(others, rhs)

    fwd_outs = [(HALF + 4, N) + tile, (HALF, N) + tile]
    back_scratch = [columns]
    evens = (HALF + 1, N) + tile
    e1, o1, joint = call(
        forward_first_kernel,
        (rhs, mask_t, place, others, f1, f2, scal, cst, sd),
        fwd_outs + [(JOINT_ROWS, LANES)],
        [columns],
        1.2,
    )
    q, part = call(response_kernel, (m1, m2, e1), [(HALF + 1, NN) + tile, evens], [], 3.0)
    other_joint = after(xor_swap(joint, half_turn), q)
    delta, za, zb, ta, tb, axis_inverse = call(
        backward_first_kernel,
        (joint, other_joint, q, part, scal, cst, o1),
        [field] + edges + [(2 * NN, LANES)],
        back_scratch,
        1.3,
    )
    tb, zb, za, ta = t_far(tb), z_far(zb), z_near(za), t_near(ta)
    e2, o2, y2 = call(
        forward_second_kernel,
        (delta, za, zb, tb, ta, mask, f1, f2, scal, cst),
        fwd_outs + [tile],
        [columns],
        1.3,
    )
    (part,) = call(particular_kernel, (m1, m2, e2), [evens], [], 1.0)
    other_y2 = after(xor_swap(y2, half_turn), part)
    (update,) = call(
        backward_second_kernel,
        (y2, other_y2, axis_inverse, q, part, scal, cst, o2, delta),
        [field],
        back_scratch + [field, pltpu.SemaphoreType.DMA((N,))],
        2.0,
        out_hbm=True,
    )
    return update


def solution(mesh):
    return jax.shard_map(
        per_device,
        mesh=mesh,
        in_specs=(
            P(None, "ax", "az", None),
            P("ax", "az", None),
            P("ax", "az", None),
            P("ax", "az"),
            P("ax", "az", None, None),
            P(),
            P(),
        ),
        out_specs=P(None, "ax", "az", None),
        check_vma=False,
    )
```

```python
import jax
import jax.numpy as jnp
from jax import lax
from jax.experimental import pallas as pl
from jax.experimental.pallas import tpu as pltpu
from jax.sharding import PartitionSpec as P

N = 5
NN = 25
SEG = 8
LANES = 128
HALF = 16
VMEM_LIMIT = 16 * 1024 * 1024
F32 = jnp.float32
STEPS = [(s * (2 * i + 1), s) for s in (1, 2, 4, 8) for i in range(8 // s)]


def up(x, s):
    return pltpu.roll(x, SEG - s, 0)


def down(x, s):
    return pltpu.roll(x, s, 0)


def splat_consts(coupling_ref, upwind_ref):
    shape = (SEG, LANES)
    p = [[jnp.full(shape, coupling_ref[i, j], F32) for j in range(N)] for i in range(N)]
    w = [jnp.full(shape, upwind_ref[i], F32) for i in range(N)]
    a = [[p[i][j] + w[i] if i == j else p[i][j] for j in range(N)] for i in range(N)]
    b = [[(1.0 - w[i]) - p[j][i] if i == j else -p[j][i] for j in range(N)] for i in range(N)]
    return a, b


def dot_row(row, cols, j):
    acc = row[0] * cols[0][j]
    for k in range(1, N):
        acc = acc + row[k] * cols[k][j]
    return acc


def mat_mul(x, y):
    return [[dot_row(x[i], y, j) for j in range(N)] for i in range(N)]


def mat_vec(x, v):
    out = []
    for row in x:
        t = [row[k] * v[k] for k in range(N)]
        out.append((t[0] + t[1]) + (t[2] + t[3]) + t[4])
    return out


def invert(matrix):
    m = [list(row) for row in matrix]
    for p in range(N):
        piv = 1.0 / m[p][p]
        m[p] = [piv if j == p else m[p][j] * piv for j in range(N)]
        for i in range(N):
            if i != p:
                f = m[i][p]
                m[i] = [-(f * piv) if j == p else m[i][j] - f * m[p][j] for j in range(N)]
    return m


def load_mat(ref, slot, base):
    return [[ref[slot, base + i * N + j] for j in range(N)] for i in range(N)]


def load_row(ref, slot, base, i):
    return [ref[slot, base + i * N + j] for j in range(N)]


def store_mat(ref, slot, base, mat):
    for i in range(N):
        for j in range(N):
            ref[slot, base + i * N + j] = mat[i][j]


def strided(ref, k):
    return ref[pl.ds(k, SEG, stride=2 * HALF), :]


def slot_of(q):
    return q + 2


LAM_ROW, MASK_ROW, VEC_ROW, JOINT_ROWS = NN, NN + 1, NN + 2, 32
D0, OUT0, IN0 = 0, NN, 2 * NN
LO0, LI0 = 0, NN


def is_even(axis):
    return lax.axis_index(axis) % 2 == 0


def pack_far_sector(field, v, tb):
    _, planes, sectors, _ = field.shape
    up = is_even("az")
    for z in range(planes):
        first, last = field[v, z, pl.ds(0, 1), :], field[v, z, pl.ds(sectors - 1, 1), :]
        tb[v, pl.ds(z, 1), :] = jnp.where(up, first, last)


def pack_edges(field, v, za, zb, ta):
    _, planes, sectors, _ = field.shape
    z_up, t_up = is_even("ax"), is_even("az")
    za[v] = field[v, jnp.where(z_up, planes - 1, 0)]
    zb[v] = field[v, jnp.where(z_up, 0, planes - 1)]
    for z in range(planes):
        first, last = field[v, z, pl.ds(0, 1), :], field[v, z, pl.ds(sectors - 1, 1), :]
        ta[v, pl.ds(z, 1), :] = jnp.where(t_up, last, first)


def prelude_kernel(
    flow, coef, blank, index, coup, upw,
    u, coef_ref, mask_ref, place, cst, za, zb, ta, tb,
    blank_ref, index_ref, coup_ref, upw_ref, sem,
):
    pairs = (
        (flow, u),
        (coup, coup_ref),
        (upw, upw_ref),
        (index, index_ref),
        (blank, blank_ref),
        (coef, coef_ref),
    )
    copies = [pltpu.make_async_copy(src, dst, sem.at[i]) for i, (src, dst) in enumerate(pairs)]
    for copy in copies:
        copy.start()
    _, planes, sectors, radial = u.shape
    copies[1].wait()
    copies[2].wait()
    a, b = splat_consts(coup_ref, upw_ref)
    store_mat(cst, 0, 0, a)
    store_mat(cst, 1, 0, b)
    copies[3].wait()
    place[...] = table_place(index_ref[...])
    copies[4].wait()
    mask_ref[...] = blank_ref[...].astype(F32).reshape(planes * sectors, radial)
    copies[5].wait()
    copies[0].wait()
    for v in range(N):
        pack_edges(u, v, za, zb, ta)
        pack_far_sector(u, v, tb)


def append_kernel(low, high, out):
    half = low.shape[1]
    out[:, pl.ds(0, half), :] = low[...]
    out[:, pl.ds(half, half), :] = high[...]


def factor_kernel(coef_ref, mask_ref, cst, m1, f1, scal, sd, mask_t, lam_t, face, pw):
    mask = mask_ref[...]
    lam = coef_ref[...].reshape(LANES, 2 * HALF * SEG) * mask
    lam_t[...] = lam.T
    mask_t[...] = mask.T
    a, b = load_mat(cst, 0, 0), load_mat(cst, 1, 0)
    for which, mat in enumerate((mat_mul(a, a), mat_mul(b, b), mat_mul(a, b), mat_mul(b, a))):
        store_mat(pw, which, 0, mat)

    sub = lax.broadcasted_iota(jnp.int32, (SEG, LANES), 0)
    first_lam, first_mask = strided(lam_t, 0), strided(mask_t, 0)
    lam_k, mask_k = first_lam, first_mask
    for k in range(2 * HALF):
        if k < 2 * HALF - 1:
            lam_n, mask_n = strided(lam_t, k + 1), strided(mask_t, k + 1)
            f = 0.5 * (lam_k * mask_n + lam_n * mask_k)
        else:
            lam_n, mask_n = up(first_lam, 1), up(first_mask, 1)
            f = jnp.where(sub == SEG - 1, 0.0, 0.5 * (lam_k * mask_n + lam_n * mask_k))
        face[k + 1] = f
        lam_k, mask_k = lam_n, mask_n
    face[0] = down(face[2 * HALF], 1)

    def build_odd(m, c):
        fl, fr = face[2 * m + 1], face[2 * m + 2]
        scal[m, 0] = 1.0 / (1.0 + 0.5 * (fl + fr))
        scal[m, 1] = fl
        scal[m, 2] = fr
        return c

    lax.fori_loop(0, HALF, build_odd, 0)

    def build_even(p, c):
        prev = jnp.where(p == 0, HALF - 1, p - 1)
        inv, fl, fr = scal[p, 0], scal[p, 1], scal[p, 2]
        inv_p, fl_p, fr_p = scal[prev, 0], scal[prev, 1], scal[prev, 2]
        beta = fr_p * fr_p * inv_p
        delta = fr_p * fl_p * inv_p
        beta = jnp.where(p == 0, down(beta, 1), beta)
        alpha = fl * fl * inv
        gamma = fl * fr * inv
        d = 1.0 + 0.5 * (face[2 * p] + face[2 * p + 1])
        for i in range(N):
            for j in range(N):
                e = i * N + j
                val = -(alpha * pw[2, e] + beta * pw[3, e])
                m1[p, D0 + e] = d + val if i == j else val
                m1[p, OUT0 + e] = gamma * pw[0, e]
                m1[p, IN0 + e] = delta * pw[1, e]
        return c

    lax.fori_loop(0, HALF, build_even, 0)
    last = scal[HALF - 1, 1] * scal[HALF - 1, 2] * scal[HALF - 1, 0]
    for e in range(NN):
        m1[HALF, D0 + e] = jnp.zeros((SEG, LANES), F32)
        m1[HALF, OUT0 + e] = jnp.zeros((SEG, LANES), F32)
        m1[HALF, IN0 + e] = last * pw[1, e]

    sd[...] = jnp.zeros((JOINT_ROWS, LANES), F32)
    sd[pl.ds(LAM_ROW, 1), :] = first_lam[0:1]
    sd[pl.ds(MASK_ROW, 1), :] = first_mask[0:1]

    def step(i, c):
        eliminate(m1, f1, 1, 2 * i + 1, i)
        return c

    lax.fori_loop(0, HALF // 2, step, 0)


def eliminate(mb, mf, s, sm, fm):
    sp, sq = sm - s, sm + s
    di = invert(load_mat(mb, sm, D0))
    store_mat(mb, sm, D0, di)
    for i in range(N):
        row = load_row(mb, sp, OUT0, i)
        for j in range(N):
            mf[fm, LO0 + i * N + j] = dot_row(row, di, j)
        row = load_row(mb, sq, IN0, i)
        for j in range(N):
            mf[fm, LI0 + i * N + j] = dot_row(row, di, j)
    in_m = load_mat(mb, sm, IN0)
    for i in range(N):
        row = load_row(mf, fm, LO0, i)
        for j in range(N):
            e = i * N + j
            mb[sp, D0 + e] = mb[sp, D0 + e] - dot_row(row, in_m, j)
        row = load_row(mf, fm, LI0, i)
        for j in range(N):
            mb[sq, IN0 + i * N + j] = dot_row(row, in_m, j)
    out_m = load_mat(mb, sm, OUT0)
    for i in range(N):
        row = load_row(mf, fm, LI0, i)
        for j in range(N):
            e = i * N + j
            mb[sq, D0 + e] = mb[sq, D0 + e] - dot_row(row, out_m, j)
        row = load_row(mf, fm, LO0, i)
        for j in range(N):
            mb[sp, OUT0 + i * N + j] = dot_row(row, out_m, j)


def factor_rest_kernel(m1, sd_in, mb, mf, sd):
    def fetch(q, c):
        for e in range(3 * NN):
            mb[slot_of(q), e] = m1[2 * q, e]
        return c

    lax.fori_loop(0, HALF // 2 + 1, fetch, 0)

    def step(it, c):
        s = jnp.where(it < 4, 1, jnp.where(it < 6, 2, 4))
        first = jnp.where(it < 4, 0, jnp.where(it < 6, 4, 6))
        q = s * (2 * (it - first) + 1)
        eliminate(mb, mf, s, slot_of(q), slot_of(q))
        return c

    lax.fori_loop(0, HALF // 2 - 1, step, 0)
    sd[...] = sd_in[...]
    s0, s16 = slot_of(0), slot_of(HALF // 2)
    for e in range(NN):
        mb[0, D0 + e] = mb[s0, D0 + e] + down(mb[s16, D0 + e], 1)
        mb[0, OUT0 + e] = mb[s0, OUT0 + e]
        mb[0, IN0 + e] = down(mb[s16, IN0 + e], 1)
    for level, s in enumerate((1, 2, 4)):
        d = load_mat(mb, level, D0)
        di = invert(d)
        store_mat(mb, level, D0, di)
        di_up = [[up(di[i][j], s) for j in range(N)] for i in range(N)]
        for i in range(N):
            row = load_row(mb, level, OUT0, i)
            for j in range(N):
                mf[level, LO0 + i * N + j] = dot_row(row, di_up, j)
        di_down = [[down(di[i][j], s) for j in range(N)] for i in range(N)]
        for i in range(N):
            row = load_row(mb, level, IN0, i)
            for j in range(N):
                mf[level, LI0 + i * N + j] = dot_row(row, di_down, j)
        in_up = [[up(mb[level, IN0 + i * N + j], s) for j in range(N)] for i in range(N)]
        acc = []
        for i in range(N):
            row = load_row(mf, level, LO0, i)
            acc.append([d[i][j] - dot_row(row, in_up, j) for j in range(N)])
        out_down = [[down(mb[level, OUT0 + i * N + j], s) for j in range(N)] for i in range(N)]
        for i in range(N):
            row = load_row(mf, level, LI0, i)
            for j in range(N):
                val = acc[i][j] - dot_row(row, out_down, j)
                if level < 2:
                    mb[level + 1, D0 + i * N + j] = val
                else:
                    sd[pl.ds(i * N + j, 1), :] = val[0:1]
        if level < 2:
            out_up = [[up(mb[level, OUT0 + i * N + j], s) for j in range(N)] for i in range(N)]
            for i in range(N):
                row = load_row(mf, level, LO0, i)
                for j in range(N):
                    mb[level + 1, OUT0 + i * N + j] = dot_row(row, out_up, j)
            in_down = [[down(mb[level, IN0 + i * N + j], s) for j in range(N)] for i in range(N)]
            for i in range(N):
                row = load_row(mf, level, LI0, i)
                for j in range(N):
                    mb[level + 1, IN0 + i * N + j] = dot_row(row, in_down, j)


def join(own_ref, other_ref, j_ref):
    lam, mask = own_ref[pl.ds(LAM_ROW, 1), :], own_ref[pl.ds(MASK_ROW, 1), :]
    other_lam, other_mask = other_ref[pl.ds(LAM_ROW, 1), :], other_ref[pl.ds(MASK_ROW, 1), :]
    c = 0.25 * (lam * other_mask + other_lam * mask)

    def total(ref):
        mat = [[ref[pl.ds(i * N + j, 1), :] for j in range(N)] for i in range(N)]
        return [[mat[i][j] + c if i == j else mat[i][j] for j in range(N)] for i in range(N)]

    own, inv_other = total(own_ref), invert(total(other_ref))
    schur = [[own[i][j] - c * (c * inv_other[i][j]) for j in range(N)] for i in range(N)]
    j1 = invert(schur)
    j2 = mat_mul(j1, inv_other)
    for i in range(N):
        for j in range(N):
            j_ref[pl.ds(i * N + j, 1), :] = j1[i][j]
            j_ref[pl.ds(NN + i * N + j, 1), :] = c * j2[i][j]


def plane_neighbours(za, zb, v):
    z_up = is_even("ax")
    return jnp.where(z_up, zb[v], za[v]), jnp.where(z_up, za[v], zb[v])


def stencil_block(u, v, z, before, after, ta, tb):
    planes, sectors = u.shape[1], u.shape[2]
    t_up = is_even("az")
    cur = u[v, z]
    rows = lax.broadcasted_iota(jnp.int32, cur.shape, 0)
    behind = u[v, z - 1] if z > 0 else before
    ahead = u[v, z + 1] if z < planes - 1 else after
    t_a, t_b = ta[v, pl.ds(z, 1), :], tb[v, pl.ds(z, 1), :]
    before_t = jnp.where(rows == 0, jnp.where(t_up, t_b, t_a), pltpu.roll(cur, 1, 0))
    after_t = jnp.where(rows == sectors - 1, jnp.where(t_up, t_a, t_b), pltpu.roll(cur, sectors - 1, 0))
    return (before_t + after_t) + (1.5 * behind + 0.5 * ahead) - 4.0 * cur


def forward_body(rhs_t, f1, f2, scal, cst, e_ref, o_ref):
    a, b = load_mat(cst, 0, 0), load_mat(cst, 1, 0)
    zero = jnp.zeros((SEG, LANES), F32)
    carry = [zero] * N
    first = None
    for m in range(HALF):
        inv, fl, fr = scal[m, 0], scal[m, 1], scal[m, 2]
        odd = [strided(rhs_t.at[v], 2 * m + 1) for v in range(N)]
        scaled = [x * inv for x in odd]
        ta = mat_vec(a, scaled)
        tb = mat_vec(b, scaled)
        for v in range(N):
            o_ref[m, v] = odd[v]
            e_ref[m, v] = strided(rhs_t.at[v], 2 * m) + carry[v] + fl * ta[v]
        carry = [fr * tb[v] for v in range(N)]
    for v in range(N):
        e_ref[0, v] = e_ref[0, v] + down(carry[v], 1)
        e_ref[HALF, v] = zero
    for m, s in STEPS:
        vec = [e_ref[m, v] for v in range(N)]
        mf, slot = (f1, m // 2) if s == 1 else (f2, slot_of(m // 2))
        lo = mat_vec(load_mat(mf, slot, LO0), vec)
        li = mat_vec(load_mat(mf, slot, LI0), vec)
        for v in range(N):
            e_ref[m - s, v] = e_ref[m - s, v] + lo[v]
            e_ref[m + s, v] = e_ref[m + s, v] + li[v]
    cur = [e_ref[0, v] + down(e_ref[HALF, v], 1) for v in range(N)]
    for level, s in enumerate((1, 2, 4)):
        for v in range(N):
            e_ref[HALF + 1 + level, v] = cur[v]
        lo = mat_vec(load_mat(f2, level, LO0), [up(x, s) for x in cur])
        li = mat_vec(load_mat(f2, level, LI0), [down(x, s) for x in cur])
        cur = [cur[v] + lo[v] + li[v] for v in range(N)]
    return [cur[v][0:1] for v in range(N)]


def doubling_bits():
    return [bit for bit in (24, 8, 2, 4, 1) if bit < lax.axis_size("az")]


def table_place(index):
    apart = lax.shift_right_logical(index, 2) ^ lax.axis_index("az")
    block = jnp.zeros_like(apart)
    for i, bit in enumerate(doubling_bits()):
        used = (apart & (1 << (bit.bit_length() - 1))) != 0
        apart = jnp.where(used, apart ^ bit, apart)
        block = block | (jnp.where(used, 1, 0) << i)
    return block * 4 + (index & 3)


def one_hot(place, start, count):
    planes, sectors = place.shape
    rows = start + lax.broadcasted_iota(jnp.int32, (count, sectors), 0)
    hot = [jnp.where(rows == place[pl.ds(z, 1), :], 1.0, 0.0) for z in range(planes)]
    hot = jnp.concatenate(hot, axis=1)
    return jnp.concatenate([hot, hot, hot], axis=0).astype(jnp.bfloat16)


def pick(rows, hot):
    high = rows.astype(jnp.bfloat16)
    rest = rows - high.astype(F32)
    middle = rest.astype(jnp.bfloat16)
    low = (rest - middle.astype(F32)).astype(jnp.bfloat16)
    return lax.dot_general(
        jnp.concatenate([high, middle, low], axis=0),
        hot,
        (((0,), (0,)), ((), ())),
        preferred_element_type=F32,
    )


def rhs_kernel(u, za, zb, ta, tb, mask_ref, mask_t, place, low, rhs_t):
    planes = u.shape[1]
    mask = mask_ref[...]
    hot = one_hot(place, 0, low.shape[1])
    for v in range(N):
        before, after = plane_neighbours(za, zb, v)
        blocks = [stencil_block(u, v, z, before, after, ta, tb) for z in range(planes)]
        rhs_t[v] = (mask * jnp.concatenate(blocks, axis=0)).T + mask_t[...] * pick(low[v], hot)


def forward_first_kernel(
    rhs_in, mask_t, place, high, f1, f2, scal, cst, sd, e_ref, o_ref, joint, rhs_t
):
    hot = one_hot(place, high.shape[1], high.shape[1])
    for v in range(N):
        rhs_t[v] = rhs_in[v] + mask_t[...] * pick(high[v], hot)
    reduced = forward_body(rhs_t, f1, f2, scal, cst, e_ref, o_ref)
    joint[...] = sd[...]
    for v in range(N):
        joint[pl.ds(VEC_ROW + v, 1), :] = reduced[v]


def forward_second_kernel(
    u, za, zb, tb, ta, mask_ref, f1, f2, scal, cst, e_ref, o_ref, y_ref, rhs_t
):
    planes = u.shape[1]
    mask = mask_ref[...]
    for v in range(N):
        before, after = plane_neighbours(za, zb, v)
        blocks = [stencil_block(u, v, z, before, after, ta, tb) for z in range(planes)]
        rhs_t[v] = (mask * jnp.concatenate(blocks, axis=0)).T
    reduced = forward_body(rhs_t, f1, f2, scal, cst, e_ref, o_ref)
    y_ref[...] = jnp.zeros((SEG, LANES), F32)
    for v in range(N):
        y_ref[pl.ds(v, 1), :] = reduced[v]


def particular(m1, m2, e_ref, x_ref):
    sub = lax.broadcasted_iota(jnp.int32, (SEG, LANES), 0)
    cur = [jnp.zeros((SEG, LANES), F32)] * N

    def recover(mb, slot, rhs, high, low):
        o = mat_vec(load_mat(mb, slot, OUT0), high)
        i = mat_vec(load_mat(mb, slot, IN0), low)
        total = [e_ref[rhs, v] + (o[v] + i[v]) for v in range(N)]
        return mat_vec(load_mat(mb, slot, D0), total)

    for level, s in ((2, 4), (1, 2), (0, 1)):
        new = recover(m2, level, HALF + 1 + level, [up(x, s) for x in cur], [down(x, s) for x in cur])
        cur = [jnp.where(sub % (2 * s) == s, new[v], cur[v]) for v in range(N)]
    for v in range(N):
        x_ref[0, v] = cur[v]
        x_ref[HALF, v] = up(cur[v], 1)
    for m, s in reversed(STEPS):
        mb, slot = (m1, m) if s == 1 else (m2, slot_of(m // 2))
        new = recover(
            mb, slot, m, [x_ref[m + s, v] for v in range(N)], [x_ref[m - s, v] for v in range(N)]
        )
        for v in range(N):
            x_ref[m, v] = new[v]


def response(m1, m2, q):
    sub = lax.broadcasted_iota(jnp.int32, (SEG, LANES), 0)
    one, zero = jnp.ones((SEG, LANES), F32), jnp.zeros((SEG, LANES), F32)
    cur = [[one if i == j else zero for j in range(N)] for i in range(N)]

    def recover(mb, slot, high, low):
        o = mat_mul(load_mat(mb, slot, OUT0), high)
        i = mat_mul(load_mat(mb, slot, IN0), low)
        total = [[o[r][c] + i[r][c] for c in range(N)] for r in range(N)]
        return mat_mul(load_mat(mb, slot, D0), total)

    for level, s in ((2, 4), (1, 2), (0, 1)):
        high = [[up(x, s) for x in row] for row in cur]
        low = [[down(x, s) for x in row] for row in cur]
        new = recover(m2, level, high, low)
        cur = [
            [jnp.where(sub % (2 * s) == s, new[r][c], cur[r][c]) for c in range(N)] for r in range(N)
        ]
    store_mat(q, 0, 0, cur)
    store_mat(q, HALF, 0, [[up(x, 1) for x in row] for row in cur])

    def later(it, c):
        s = jnp.where(it < 1, 4, jnp.where(it < 3, 2, 1))
        n = s * (2 * (it - jnp.where(it < 1, 0, jnp.where(it < 3, 1, 3))) + 1)
        high, low = load_mat(q, 2 * (n + s), 0), load_mat(q, 2 * (n - s), 0)
        store_mat(q, 2 * n, 0, recover(m2, slot_of(n), high, low))
        return c

    lax.fori_loop(0, HALF // 2 - 1, later, 0)

    def first(it, c):
        m = 2 * it + 1
        store_mat(q, m, 0, recover(m1, m, load_mat(q, m + 1, 0), load_mat(q, m - 1, 0)))
        return c

    lax.fori_loop(0, HALF // 2, first, 0)


def response_kernel(m1, m2, e_ref, q, x_ref):
    particular(m1, m2, e_ref, x_ref)
    response(m1, m2, q)


def particular_kernel(m1, m2, e_ref, x_ref):
    particular(m1, m2, e_ref, x_ref)


def axis_value(own, other, j_ref):
    cur = []
    for i in range(N):
        acc = j_ref[pl.ds(i * N, 1), :] * own[0]
        for k in range(N):
            if k > 0:
                acc = acc + j_ref[pl.ds(i * N + k, 1), :] * own[k]
            acc = acc + j_ref[pl.ds(NN + i * N + k, 1), :] * other[k]
        cur.append(jnp.broadcast_to(acc, (SEG, LANES)))
    return cur


def backward_body(own, other, j_ref, q, part, scal, cst, o_ref, x_t):
    a, b = load_mat(cst, 0, 0), load_mat(cst, 1, 0)
    axis = axis_value(own, other, j_ref)

    def even(p):
        add = mat_vec(load_mat(q, p, 0), axis)
        return [part[p, v] + add[v] for v in range(N)]

    low = even(0)
    for m in range(HALF):
        inv, fl, fr = scal[m, 0], scal[m, 1], scal[m, 2]
        high = even(m + 1)
        ta = mat_vec(a, high)
        tb = mat_vec(b, low)
        for v in range(N):
            odd = inv * (o_ref[m, v] + fr * ta[v] + fl * tb[v])
            x_t.at[v][pl.ds(2 * m, SEG, stride=2 * HALF), :] = low[v]
            x_t.at[v][pl.ds(2 * m + 1, SEG, stride=2 * HALF), :] = odd
        low = high


def backward_first_kernel(
    joint, other_joint, q, part, scal, cst, o_ref,
    out, za, zb, ta, tb, j_ref, x_t,
):
    join(joint, other_joint, j_ref)
    own = [joint[pl.ds(VEC_ROW + v, 1), :] for v in range(N)]
    other = [other_joint[pl.ds(VEC_ROW + v, 1), :] for v in range(N)]
    backward_body(own, other, j_ref, q, part, scal, cst, o_ref, x_t)
    _, planes, sectors, radial = out.shape
    for v in range(N):
        out[v] = x_t[v].T.reshape(planes, sectors, radial)
        pack_edges(out, v, za, zb, ta)
        pack_far_sector(out, v, tb)


def backward_second_kernel(
    y_own, y_other, j_ref, q, part, scal, cst, o_ref, first, out, x_t, stage, sem
):
    own = [y_own[pl.ds(v, 1), :] for v in range(N)]
    other = [y_other[pl.ds(v, 1), :] for v in range(N)]
    backward_body(own, other, j_ref, q, part, scal, cst, o_ref, x_t)
    _, planes, sectors, radial = out.shape
    copies = [pltpu.make_async_copy(stage.at[v], out.at[v], sem.at[v]) for v in range(N)]
    for v in range(N):
        stage[v] = first[v] + 0.5 * x_t[v].T.reshape(planes, sectors, radial)
        copies[v].start()
    for copy in copies:
        copy.wait()


def call(kernel, inputs, outs, scratch, us, hbm=False, out_hbm=False):
    vmem = pl.BlockSpec(memory_space=pltpu.VMEM)
    if hbm:
        inputs = [pltpu.with_memory_space_constraint(x, pltpu.HBM) for x in inputs]
    in_spec = pl.BlockSpec(memory_space=pltpu.HBM) if hbm else vmem
    out_shape = [s if isinstance(s, jax.ShapeDtypeStruct) else jax.ShapeDtypeStruct(s, F32) for s in outs]
    return pl.pallas_call(
        kernel,
        out_shape=out_shape,
        in_specs=[in_spec] * len(inputs),
        out_specs=[pl.BlockSpec(memory_space=pltpu.HBM) if out_hbm else vmem] * len(outs),
        scratch_shapes=[pltpu.VMEM(s, F32) if isinstance(s, tuple) else s for s in scratch],
        compiler_params=pltpu.CompilerParams(vmem_limit_bytes=VMEM_LIMIT),
        cost_estimate=pl.CostEstimate(
            flops=int(us * 1e9), bytes_accessed=int(us * 3e6), transcendentals=0
        ),
    )(*inputs)


def swapped_along(x, axis, odd, wrap):
    size = lax.axis_size(axis)
    pairs = []
    for i in range(odd, size, 2):
        if wrap or i + 1 < size:
            j = (i + 1) % size
            pairs += [(i, j), (j, i)]
    return lax.ppermute(x, axis, pairs)


def z_near(x):
    return swapped_along(x, "ax", 0, False)


def z_far(x):
    return swapped_along(x, "ax", 1, False)


def t_near(x):
    return swapped_along(x, "az", 0, True)


def t_far(x):
    return swapped_along(x, "az", 1, True)


def xor_swap(x, bit):
    return lax.ppermute(x, "az", [(i, i ^ bit) for i in range(lax.axis_size("az"))])


def append(low, high):
    (both,) = call(append_kernel, (low, high), [(N, 2 * low.shape[1], low.shape[2])], [], 0.2)
    return both


def after(x, *others):
    return lax.optimization_barrier((x, *others))[0]


def per_device(
    flow_state, radial_coef, blanking, canard_index, canard_table, coupling, upwind_split
):
    comps, planes, sectors, radial = flow_state.shape
    tile = (SEG, LANES)
    half_turn = lax.axis_size("az") // 2
    field = (comps, planes, sectors, radial)
    edges = [(comps, sectors, radial)] * 2 + [(comps, planes, radial)] * 2
    columns = (comps, radial, LANES)
    bits = doubling_bits()

    rows = canard_table[0].transpose(1, 0, 2)
    got = xor_swap(rows, bits[0])
    u, coef, mask, place, cst, za, zb, ta, tb = call(
        prelude_kernel,
        (flow_state, radial_coef, blanking, canard_index, coupling, upwind_split),
        [
            field,
            (planes, sectors, radial),
            (LANES, radial),
            jax.ShapeDtypeStruct(canard_index.shape, jnp.int32),
            (2, NN) + tile,
        ]
        + edges,
        [
            pltpu.VMEM((planes, sectors, radial), jnp.int32),
            pltpu.VMEM(canard_index.shape, jnp.int32),
            pltpu.SMEM((N, N), F32),
            pltpu.SMEM((N,), F32),
            pltpu.SemaphoreType.DMA((6,)),
        ],
        1.2,
        hbm=True,
    )
    rows = append(rows, after(got, cst))
    halo, done = {"zb": z_far(zb)}, []

    def factor(rows, got):
        done.extend(
            call(
                factor_kernel,
                (after(coef, rows), mask, cst),
                [
                    (HALF + 1, 3 * NN) + tile,
                    (HALF // 2, 2 * NN) + tile,
                    (HALF, 3) + tile,
                    (JOINT_ROWS, LANES),
                    (radial, LANES),
                ],
                [(radial, LANES), (2 * HALF + 1,) + tile, (4, NN) + tile],
                3.2,
            )
        )
        return after(got, done[3])

    def sector_halos(rows, got):
        halo["za"], halo["tb"] = z_near(after(za, rows)), t_far(after(tb, rows))
        return after(got, halo["zb"])

    def factor_rest(rows, got):
        halo["ta"] = t_near(after(ta, rows))
        m1, sd = done[0], done[3]
        done.extend(
            call(
                factor_rest_kernel,
                (after(m1, rows), sd),
                [
                    (HALF // 2 + 3, 3 * NN) + tile,
                    (HALF // 2 + 2, 2 * NN) + tile,
                    (JOINT_ROWS, LANES),
                ],
                [],
                3.0,
            )
        )
        return after(got, done[-1], halo["ta"], halo["tb"], halo["za"])

    fillers = [factor, sector_halos, factor_rest]
    for i, bit in enumerate(bits[1:-1]):
        rows = append(rows, fillers[i](rows, xor_swap(rows, bit)))
    for filler in fillers[len(bits) - 2 :]:
        rows = filler(rows, rows)
    m1, f1, scal, _, mask_t, m2, f2, sd = done
    others = xor_swap(rows, bits[-1])
    (rhs,) = call(
        rhs_kernel,
        (u, halo["za"], halo["zb"], halo["ta"], halo["tb"], mask, mask_t, place, rows),
        [columns],
        [],
        1.3,
    )
    others = after(others, rhs)

    fwd_outs = [(HALF + 4, N) + tile, (HALF, N) + tile]
    back_scratch = [columns]
    evens = (HALF + 1, N) + tile
    e1, o1, joint = call(
        forward_first_kernel,
        (rhs, mask_t, place, others, f1, f2, scal, cst, sd),
        fwd_outs + [(JOINT_ROWS, LANES)],
        [columns],
        1.2,
    )
    q, part = call(response_kernel, (m1, m2, e1), [(HALF + 1, NN) + tile, evens], [], 3.0)
    other_joint = after(xor_swap(joint, half_turn), q)
    delta, za, zb, ta, tb, axis_inverse = call(
        backward_first_kernel,
        (joint, other_joint, q, part, scal, cst, o1),
        [field] + edges + [(2 * NN, LANES)],
        back_scratch,
        1.3,
    )
    tb, zb, za, ta = t_far(tb), z_far(zb), z_near(za), t_near(ta)
    e2, o2, y2 = call(
        forward_second_kernel,
        (delta, za, zb, tb, ta, mask, f1, f2, scal, cst),
        fwd_outs + [tile],
        [columns],
        1.3,
    )
    (part,) = call(particular_kernel, (m1, m2, e2), [evens], [], 1.0)
    other_y2 = after(xor_swap(y2, half_turn), part)
    (update,) = call(
        backward_second_kernel,
        (y2, other_y2, axis_inverse, q, part, scal, cst, o2, delta),
        [field],
        back_scratch + [field, pltpu.SemaphoreType.DMA((N,))],
        2.0,
        out_hbm=True,
    )
    return update


def solution(mesh):
    return jax.shard_map(
        per_device,
        mesh=mesh,
        in_specs=(
            P(None, "ax", "az", None),
            P("ax", "az", None),
            P("ax", "az", None),
            P("ax", "az"),
            P("ax", "az", None, None),
            P(),
            P(),
        ),
        out_specs=P(None, "ax", "az", None),
        check_vma=False,
    )
```
